32 devices in a mesh: groups: 2 (over x), gx: 16 (over z, y, core).
Axes of the slice: x: 2, y: 2, z: 4, core: 2. Of those that a mesh axis runs over, the one named last changes fastest.
Arguments:
- log_perm: float32 [512, 32, 128], P(('groups', 'gx')), parts along dimension 0, may hold values from -3 to 3
- saturation: float32 [512, 32, 128], P(('groups', 'gx')), parts along dimension 0, may hold values from 0.05 to 0.95
- porosity: float32 [512, 32, 128], P(('groups', 'gx')), parts along dimension 0, may hold values from 0.1 to 0.3
- source: float32 [512, 32, 128], P(('groups', 'gx')), parts along dimension 0, may hold values from -6 to 6
- support_bits: int32 [512, 32, 128], P(('groups', 'gx')), parts along dimension 0, may hold values from 1 to 255, as said below
Outputs:
- pressure: float32 [512, 32, 128], P(('groups', 'gx')), parts along dimension 0
- new_saturation: float32 [512, 32, 128], P(('groups', 'gx')), parts along dimension 0
The draws below stay inside these ranges and needn't reach their ends.
There are 2 independent parts, one for each index of `groups`. The reference program is written for one: setup_inputs(seed, part) draws one part's arguments, and reference() takes and returns one part's arrays. A program takes and returns all parts, laid end to end along the dimension named above; each array names one. Nothing has to cross between parts.
Inputs may be any that keep to these rules, and one draw needn't show every extreme that they name: `support_bits`: bit k of a cell's value, k = a + 2 b + 4 c, marks the cell as inside the basis support of its colour-k coarse node; the bit of the colour of the cell's own block is always set.
All inputs are finite; a program needn't handle non-finite values.
Results may differ from the reference program's by a relative error of at most 0.0003.
Values sent between devices are 32-bit elements; how exact they have to be, the bound alone decides.
A program may use at most 64 MiB of HBM per device.

```python
import jax
import jax.numpy as jnp
from jax import lax

NY = 32
NZ = 128
BX = 16
BY = 16
BZ = 8
JACOBI = 2
CHEBY = 4
NX = 256
NCX = 16
NCY = 2
NCZ = 16


def draw_support_bits(key, part):
    first = jax.random.randint(jax.random.fold_in(key, 11), (NX, NY, NZ), 0, 256)
    second = jax.random.randint(jax.random.fold_in(key, 12), (NX, NY, NZ), 0, 256)
    home_x = jnp.arange(NX) // BX % 2
    home_y = jnp.arange(NY) // BY % 2
    home_z = jnp.arange(NZ) // BZ % 2
    home = home_x[:, None, None] + 2 * home_y[None, :, None] + 4 * home_z[None, None, :]
    merged = jnp.bitwise_or(jnp.bitwise_or(first, second), jnp.left_shift(jnp.ones_like(home), home))
    return merged.astype(jnp.int32)


def levels(rng, shape, cuts, smallest, top_value):
    factor_of = 1.0
    for position, shards_of in cuts:
        steps = jax.random.uniform(jax.random.fold_in(jax.random.fold_in(rng, 6), position), (shards_of,), jnp.float32, smallest / len(cuts), top_value / len(cuts))
        factor_of = factor_of * jnp.repeat(jnp.exp(steps), shape[position] // shards_of).reshape((-1,) + (1,) * (len(shape) - 1 - position))
    return factor_of


def normal_values(stream_key, shape, deviation, most, cuts=(), kind=jnp.bfloat16):
    result = deviation * jax.random.normal(stream_key, shape, jnp.float32)
    if cuts:
        result = result * levels(stream_key, shape, cuts, -0.22, 0.18)
    return jnp.clip(result, -most, most).astype(kind)


def setup_inputs(seed: int = 0, part: int = 0) -> dict:
    streams_of = jax.random.split(jax.random.key(seed), 6)
    part_keys = jax.random.split(jax.random.fold_in(streams_of[5], part), 6)
    log_perm = normal_values(part_keys[0], (NX, NY, NZ), 1.0, 3.0, ((0, 16),), jnp.float32)
    saturation = jnp.clip(0.05 + 0.9 * jax.random.uniform(part_keys[1], (NX, NY, NZ), jnp.float32) ** levels(part_keys[1], (NX, NY, NZ), ((0, 16),), -0.2, 0.2), 0.05, 0.95)
    porosity = jnp.clip(0.1 + 0.20000001043081284 * jax.random.uniform(part_keys[2], (NX, NY, NZ), jnp.float32) ** levels(part_keys[2], (NX, NY, NZ), ((0, 16),), -0.2, 0.2), 0.1, 0.3)
    source = normal_values(part_keys[3], (NX, NY, NZ), 1.0, 6.0, ((0, 16),), jnp.float32)
    support_bits = draw_support_bits(jax.random.fold_in(jax.random.fold_in(streams_of[5], part), 71), part)
    return dict(log_perm=log_perm, saturation=saturation, porosity=porosity, source=source, support_bits=support_bits)


water_viscosity = 1.0
oil_viscosity = 4.0
compress = 0.02
relax_weight = 2.0 / 3.0
courant = 0.5
upper_margin = 1.25
lower_share = 0.1
tiny_eps = 1e-06

def pad_axis(array, axis, before, after):
    widths = [(0, 0)] * array.ndim
    widths[axis] = (before, after)
    return jnp.pad(array, widths)

def spread(pair, axis):
    stacked = jnp.stack([pair[colour >> axis & 1] for colour in range(8)])
    if axis == 0:
        return stacked[:, :, None, None]
    if axis == 1:
        return stacked[:, None, :, None]
    return stacked[:, None, None, :]

def node_pair(coords, block):
    blocks = coords // block
    upper = coords % block >= block // 2
    beside = jnp.where(upper, blocks + 1, blocks - 1)
    return jnp.stack([jnp.where(blocks % 2 == parity, blocks, beside) for parity in range(2)])

def valid_pair(nodes, count):
    return ((nodes >= 0) & (nodes < count)).astype(jnp.float32)

def mobility(satur):
    return satur * satur / water_viscosity + (1.0 - satur) * (1.0 - satur) / oil_viscosity

def harmonic(left, right):
    return 2.0 * left * right / (left + right)

def coefficients(perm_ext, mob_ext, porous, face_ok):
    face_x = harmonic(perm_ext[:-1], perm_ext[1:]) * (0.5 * (mob_ext[:-1] + mob_ext[1:])) * face_ok
    perm_in = perm_ext[1:-1]
    mob_in = mob_ext[1:-1]
    face_y = harmonic(perm_in[:, :-1], perm_in[:, 1:]) * (0.5 * (mob_in[:, :-1] + mob_in[:, 1:]))
    face_z = harmonic(perm_in[:, :, :-1], perm_in[:, :, 1:]) * (0.5 * (mob_in[:, :, :-1] + mob_in[:, :, 1:]))
    links = (face_x[:-1], face_x[1:], pad_axis(face_y, 1, 1, 0), pad_axis(face_y, 1, 0, 1), pad_axis(face_z, 2, 1, 0), pad_axis(face_z, 2, 0, 1))
    diagonal = compress * porous + links[0] + links[1] + links[2] + links[3] + links[4] + links[5]
    return (face_x, face_y, face_z, links, diagonal)

def same_flags(nodes_x, nodes_y, nodes_z):
    faces_x = (nodes_x[:, :-1] == nodes_x[:, 1:]).astype(jnp.float32)
    faces_y = (nodes_y[:, :-1] == nodes_y[:, 1:]).astype(jnp.float32)
    faces_z = (nodes_z[:, :-1] == nodes_z[:, 1:]).astype(jnp.float32)
    return (spread(faces_x[:, :-1], 0), spread(faces_x[:, 1:], 0), spread(pad_axis(faces_y, 1, 1, 0), 1), spread(pad_axis(faces_y, 1, 0, 1), 1), spread(pad_axis(faces_z, 1, 1, 0), 2), spread(pad_axis(faces_z, 1, 0, 1), 2))

def home_basis(coords_x, coords_y, coords_z, inside):
    home = (coords_x // BX % 2)[:, None, None] + 2 * (coords_y // BY % 2)[None, :, None] + 4 * (coords_z // BZ % 2)[None, None, :]
    colours = jnp.arange(8, dtype=jnp.int32)[:, None, None, None]
    return (colours == home[None]).astype(jnp.float32) * inside[None, :, None, None]

def support_mask(bits, valid_x, valid_y, valid_z, inside):
    colours = jnp.arange(8, dtype=jnp.int32)[:, None, None, None]
    marked = jnp.bitwise_and(jnp.right_shift(bits[None], colours), 1).astype(jnp.float32)
    return marked * spread(valid_x, 0) * spread(valid_y, 1) * spread(valid_z, 2) * inside[None, :, None, None]

def jacobi_sweep(basis_ext, mask, diagonal, links, same, outside):
    centre = basis_ext[:, 1:-1]
    pull = links[0] * same[0] * basis_ext[:, :-2] + links[1] * same[1] * basis_ext[:, 2:]
    pull = pull + links[2] * same[2] * pad_axis(centre[:, :, :-1], 2, 1, 0) + links[3] * same[3] * pad_axis(centre[:, :, 1:], 2, 0, 1)
    pull = pull + links[4] * same[4] * pad_axis(centre[:, :, :, :-1], 3, 1, 0) + links[5] * same[5] * pad_axis(centre[:, :, :, 1:], 3, 0, 1)
    updated = mask * (centre - relax_weight * (diagonal * centre - pull) / diagonal)
    return updated / (lax.optimization_barrier(jnp.sum(updated, axis=0)) + outside)[None]

def apply_plain(field_ext, diagonal, links):
    centre = field_ext[1:-1]
    pull = links[0] * field_ext[:-2] + links[1] * field_ext[2:]
    pull = pull + links[2] * pad_axis(centre[:, :-1], 1, 1, 0) + links[3] * pad_axis(centre[:, 1:], 1, 0, 1)
    pull = pull + links[4] * pad_axis(centre[:, :, :-1], 2, 1, 0) + links[5] * pad_axis(centre[:, :, 1:], 2, 0, 1)
    return diagonal * centre - pull

def block_sums(field):
    length, columns, depth = field.shape
    return lax.optimization_barrier(jnp.sum(field.reshape(length // BX, BX, columns // BY, BY, depth // BZ, BZ), axis=(1, 3, 5)))

def probe_blocks(basis_ext, nodes_x, nodes_y, nodes_z, diagonal, links):
    rest_x = nodes_x % 3
    rest_y = nodes_y % 3
    rest_z = nodes_z % 3

    def one_probe(probe):
        pick = spread((rest_x == probe // 9).astype(jnp.float32), 0)
        pick = pick * spread((rest_y == probe // 3 % 3).astype(jnp.float32), 1)
        pick = pick * spread((rest_z == probe % 3).astype(jnp.float32), 2)
        field = lax.optimization_barrier(jnp.sum(basis_ext * pick, axis=0))
        return block_sums(apply_plain(field, diagonal, links))
    return lax.map(one_probe, jnp.arange(27, dtype=jnp.int32))

def coarse_matrix(probes, first_block):
    shape = probes.shape
    offsets = jnp.arange(27, dtype=jnp.int32)[:, None, None, None]
    index_x = (first_block + jnp.arange(shape[1], dtype=jnp.int32))[None, :, None, None]
    index_y = jnp.arange(shape[2], dtype=jnp.int32)[None, None, :, None]
    index_z = jnp.arange(shape[3], dtype=jnp.int32)[None, None, None, :]
    pick = (index_x + offsets // 9 - 1) % 3 * 9 + (index_y + offsets // 3 % 3 - 1) % 3 * 3 + (index_z + offsets % 3 - 1) % 3
    pick = jnp.broadcast_to(pick, shape).astype(jnp.int32)
    return jnp.take_along_axis(probes, pick, axis=0)

def coarse_apply(matrix, vector_ext):
    count_x, count_y, count_z = (matrix.shape[1], matrix.shape[2], matrix.shape[3])
    padded = pad_axis(pad_axis(vector_ext, 1, 1, 1), 2, 1, 1)
    total = jnp.zeros((count_x, count_y, count_z), jnp.float32)
    for offset in range(27):
        step_x = offset // 9
        step_y = offset // 3 % 3
        step_z = offset % 3
        total = total + matrix[offset] * padded[step_x:step_x + count_x, step_y:step_y + count_y, step_z:step_z + count_z]
    return total

def zero_rims(vector):
    return pad_axis(vector, 0, 1, 1)

def keep_pair(pair):
    return pair

def coarse_solve(matrix, rhs, extend, total_sums, count):
    weight = lax.optimization_barrier(jnp.sum(jnp.abs(matrix), axis=0))

    def apply_op(vector):
        return coarse_apply(matrix, extend(vector))
    first = apply_op(rhs) / weight
    second = apply_op(first) / weight
    sum_first, sum_second = total_sums((jnp.sum(first * first), jnp.sum(second * second)))
    spectral = jnp.sqrt(sum_second / count / (sum_first / count + tiny_eps))
    upper = upper_margin * spectral
    lower = lower_share * upper
    centre = 0.5 * (upper + lower)
    half_width = 0.5 * (upper - lower)
    ratio = centre / half_width
    damping = 1.0 / ratio
    residual = rhs
    update = residual / (weight * centre)
    solution = jnp.zeros_like(rhs)
    for sweep in range(CHEBY):
        solution = solution + update
        if sweep + 1 < CHEBY:
            residual = residual - apply_op(update)
            damping_next = 1.0 / (2.0 * ratio - damping)
            update = damping_next * damping * update + 2.0 * damping_next / half_width * residual / weight
            damping = damping_next
    return solution

def prolong(basis, solution_ext, index_x, nodes_y, nodes_z):
    padded = pad_axis(pad_axis(solution_ext, 1, 1, 1), 2, 1, 1)
    total = jnp.zeros(basis.shape[1:], jnp.float32)
    for colour in range(8):
        picked = jnp.take(padded, index_x[colour & 1], axis=0, mode='clip')
        picked = jnp.take(picked, nodes_y[colour >> 1 & 1] + 1, axis=1, mode='clip')
        picked = jnp.take(picked, nodes_z[colour >> 2 & 1] + 1, axis=2, mode='clip')
        total = total + basis[colour] * picked
    return total

def transport(pressure_ext, satur_ext, mob_ext, face_x, face_y, face_z, porosity, source):
    frac_ext = satur_ext * satur_ext / water_viscosity / mob_ext
    flow_x = face_x * (pressure_ext[:-1] - pressure_ext[1:])
    water_x = jnp.where(flow_x > 0, frac_ext[:-1], frac_ext[1:]) * flow_x
    pressure = pressure_ext[1:-1]
    fraction = frac_ext[1:-1]
    flow_y = face_y * (pressure[:, :-1] - pressure[:, 1:])
    water_y = jnp.where(flow_y > 0, fraction[:, :-1], fraction[:, 1:]) * flow_y
    flow_z = face_z * (pressure[:, :, :-1] - pressure[:, :, 1:])
    water_z = jnp.where(flow_z > 0, fraction[:, :, :-1], fraction[:, :, 1:]) * flow_z
    net_out = water_x[1:] - water_x[:-1] + pad_axis(water_y, 1, 0, 1) - pad_axis(water_y, 1, 1, 0)
    net_out = net_out + pad_axis(water_z, 2, 0, 1) - pad_axis(water_z, 2, 1, 0)
    leaving = jnp.maximum(flow_x[1:], 0.0) + jnp.maximum(-flow_x[:-1], 0.0)
    leaving = leaving + pad_axis(jnp.maximum(flow_y, 0.0), 1, 0, 1) + pad_axis(jnp.maximum(-flow_y, 0.0), 1, 1, 0)
    leaving = leaving + pad_axis(jnp.maximum(flow_z, 0.0), 2, 0, 1) + pad_axis(jnp.maximum(-flow_z, 0.0), 2, 1, 0)
    leaving = leaving + jnp.maximum(-source, 0.0)
    speed = leaving / porosity
    gain = jnp.maximum(source, 0.0) + jnp.minimum(source, 0.0) * fraction - net_out
    return (gain, speed)

def reference(log_perm, saturation, porosity, source, support_bits):
    coords_ext = jnp.arange(-1, NX + 1, dtype=jnp.int32)
    coords_y = jnp.arange(NY, dtype=jnp.int32)
    coords_z = jnp.arange(NZ, dtype=jnp.int32)
    inside_ext = ((coords_ext >= 0) & (coords_ext < NX)).astype(jnp.float32)
    face_ok = (inside_ext[:-1] * inside_ext[1:])[:, None, None]
    perm_ext = jnp.exp(pad_axis(log_perm, 0, 1, 1))
    satur_ext = pad_axis(saturation, 0, 1, 1)
    mob_ext = mobility(satur_ext)
    face_x, face_y, face_z, links, diagonal = coefficients(perm_ext, mob_ext, porosity, face_ok)
    nodes_ext = node_pair(coords_ext, BX)
    nodes_x = nodes_ext[:, 1:-1]
    nodes_y = node_pair(coords_y, BY)
    nodes_z = node_pair(coords_z, BZ)
    mask = support_mask(support_bits, valid_pair(nodes_x, NCX), valid_pair(nodes_y, NCY), valid_pair(nodes_z, NCZ), inside_ext[1:-1])
    same = same_flags(nodes_ext, nodes_y, nodes_z)
    outside = jnp.zeros((NX, 1, 1), jnp.float32)
    basis_ext = home_basis(coords_ext, coords_y, coords_z, inside_ext)
    basis = basis_ext[:, 1:-1]
    for sweep in range(JACOBI):
        basis = jacobi_sweep(basis_ext, mask, diagonal, links, same, outside)
        basis_ext = pad_axis(basis, 1, 1, 1)
    probes = probe_blocks(basis_ext, nodes_ext, nodes_y, nodes_z, diagonal, links)
    matrix = coarse_matrix(probes, 0)
    rhs = block_sums(source)
    solution = coarse_solve(matrix, rhs, zero_rims, keep_pair, NCX * NCY * NCZ)
    pressure = prolong(basis, zero_rims(solution), nodes_x + 1, nodes_y, nodes_z)
    pressure_ext = pad_axis(pressure, 0, 1, 1)
    gain, speed = transport(pressure_ext, satur_ext, mob_ext, face_x, face_y, face_z, porosity, source)
    top = jnp.max(speed)
    new_saturation = saturation + courant / top / porosity * gain
    return (pressure, new_saturation)
```

```python
import jax
import jax.numpy as jnp
from jax import lax
from jax.experimental import pallas as pl
from jax.experimental.pallas import tpu as pltpu
from jax.sharding import PartitionSpec as P

BX = 16
BY = 16
BZ = 8
CHEBY = 4
THIRD = 1.0 / 3.0
RELAX = 2.0 / 3.0
HI = lax.Precision.HIGHEST


def kernel(
    n, lp_h, sat_h, por_h, src_h, bits_h, pres, new_sat,
    lp_e, sat_e, por_e, bits_e, src, q_e, m_e, f_e, tx, ty, tz, wd,
    h1, y1, z1, x1, h2, y2, z2, yz2, x2, edge, halo, xbuf, gsend, gbuf, sbuf, p_e,
    msend, mbuf, lsem, hs_send, hs_recv, es_send, es_recv, g_send, g_recv, m_send, m_recv,
):
    f32 = jnp.float32
    me = lax.axis_index("gx")
    w = lp_h.shape[0]
    ny, nz = lp_h.shape[1], lp_h.shape[2]
    has_lo = me > 0
    has_hi = me < n - 1

    barrier = pltpu.get_barrier_semaphore()
    for d in range(1, n):
        pl.semaphore_signal(barrier, inc=1, device_id={"gx": lax.rem(me + d, n)})

    own = [
        pltpu.make_async_copy(lp_h, lp_e.at[pl.ds(2, w)], lsem.at[0]),
        pltpu.make_async_copy(sat_h, sat_e.at[pl.ds(2, w)], lsem.at[1]),
        pltpu.make_async_copy(por_h, por_e.at[pl.ds(1, w)], lsem.at[2]),
        pltpu.make_async_copy(bits_h, bits_e.at[pl.ds(1, w)], lsem.at[3]),
        pltpu.make_async_copy(src_h, src, lsem.at[4]),
    ]
    for c in own:
        c.start()

    def halo_copies(up):
        base = 0 if up else 4
        to = lax.rem(me + (1 if up else n - 1), n)
        out = []
        for k, (a, b, width) in enumerate(
            ((lp_h, lp_e, 2), (sat_h, sat_e, 2), (por_h, por_e, 1), (bits_h, bits_e, 1))
        ):
            s0 = w - width if up else 0
            d0 = 0 if up else w + width
            out.append(
                pltpu.make_async_remote_copy(
                    src_ref=a.at[pl.ds(s0, width)],
                    dst_ref=b.at[pl.ds(d0, width)],
                    send_sem=hs_send.at[base + k],
                    recv_sem=hs_recv.at[base + k],
                    device_id={"gx": to},
                )
            )
        return out

    up_copies = halo_copies(True)
    dn_copies = halo_copies(False)

    pl.semaphore_wait(barrier, n - 1)

    @pl.when(has_hi)
    def _():
        for c in up_copies:
            c.start()

    @pl.when(has_lo)
    def _():
        for c in dn_copies:
            c.start()

    def fill(lo):
        e2 = pl.ds(0 if lo else w + 2, 2)
        e1 = pl.ds(0 if lo else w + 1, 1)
        lp_e[e2] = jnp.zeros((2, ny, nz), f32)
        sat_e[e2] = jnp.full((2, ny, nz), 0.5, f32)
        por_e[e1] = jnp.full((1, ny, nz), 0.2, f32)
        bits_e[e1] = jnp.full((1, ny, nz), 255, jnp.int32)
        halo[0 if lo else 1] = jnp.zeros((7, ny, nz), f32)

    @pl.when(jnp.logical_not(has_lo))
    def _():
        fill(True)

    @pl.when(jnp.logical_not(has_hi))
    def _():
        fill(False)

    row = lax.broadcasted_iota(jnp.int32, (ny, nz), 0)
    lane = lax.broadcasted_iota(jnp.int32, (ny, nz), 1)
    y_top = (row & (BY - 1)) == BY - 1
    y_bot = (row & (BY - 1)) == 0
    z_top = (lane & (BZ - 1)) == BZ - 1
    z_bot = (lane & (BZ - 1)) == 0
    py = (row >> 4) & 1
    pz = (lane >> 3) & 1

    def yz_bit(jy, jz):
        return jnp.left_shift(jnp.int32(1), 2 * (py ^ jy) + 4 * (pz ^ jz))

    zero = jnp.zeros((ny, nz), f32)

    def keep(bits, bit_yz, kx, value):
        return jnp.where((bits & (bit_yz * (1 + kx))) != 0, value, zero)

    def yn(v):
        return pltpu.roll(v, ny - 1, 0)

    def yp(v):
        return pltpu.roll(v, 1, 0)

    def zn(v):
        return pltpu.roll(v, nz - 1, 1)

    def zp(v):
        return pltpu.roll(v, 1, 1)

    def prepare(i):
        q_e[i] = jnp.exp(-lp_e[i])
        s = sat_e[i]
        r = 1.0 - s
        m = s * s + 0.25 * (r * r)
        m_e[i] = m
        f_e[i] = s * s / m

    def face(f):
        return (m_e[f] + m_e[f + 1]) / (q_e[f] + q_e[f + 1])

    def first_sweep(e, kind, kx, slot):
        q = q_e[e + 1]
        m = m_e[e + 1]
        t_y = jnp.where(row < ny - 1, (m + yn(m)) / (q + yn(q)), 0.0)
        t_z = jnp.where(lane < nz - 1, (m + zn(m)) / (q + zn(q)), 0.0)
        ty[e] = t_y
        tz[e] = t_z
        t_ym = yp(t_y)
        t_zm = zp(t_z)
        txm, txp = tx[e], tx[e + 1]
        bits = bits_e[e]
        b_y = jnp.where(y_top, t_y, jnp.where(y_bot, t_ym, 0.0))
        b_z = jnp.where(z_top, t_z, jnp.where(z_bot, t_zm, 0.0))
        inner = (t_y + t_ym - b_y) + (t_z + t_zm - b_z)
        diag = 0.02 * por_e[e] + txm + txp + (t_y + t_ym) + (t_z + t_zm)
        scale = RELAX / diag
        wd[e] = scale
        if kind is None:
            inner = inner + txm + txp
        elif kind == "lo":
            inner = inner + txp
        else:
            inner = inner + txm
        h = keep(bits, yz_bit(0, 0), kx, THIRD + scale * inner)
        by = keep(bits, yz_bit(1, 0), kx, scale * b_y)
        bz = keep(bits, yz_bit(0, 1), kx, scale * b_z)
        total = h + by + bz
        if kind is not None:
            bx = keep(bits, yz_bit(0, 0), 1 - kx, scale * (txm if kind == "lo" else txp))
            total = total + bx
        inv = 1.0 / total
        h1[e] = h * inv
        y1[e] = by * inv
        z1[e] = bz * inv
        if kind is not None:
            x1[slot] = bx * inv

    px = lax.rem(me, 2)

    for c in own:
        c.wait()

    def loop(lo, hi, fn):
        def body(i, _):
            fn(i)
            return 0

        lax.fori_loop(lo, hi, body, 0)

    loop(2, w + 2, prepare)

    def set_face(f):
        tx[f] = face(f)

    loop(2, w + 1, set_face)
    loop(2, w, lambda e: first_sweep(e, None, px, 0))

    for k in range(8):
        xbuf[k] = jnp.zeros((8, nz), f32)

    @pl.when(has_lo)
    def _():
        for c in up_copies:
            c.wait_recv()

    @pl.when(has_hi)
    def _():
        for c in dn_copies:
            c.wait_recv()

    for i in (0, 1, w + 2, w + 3):
        prepare(i)
    for f in (0, 1, w + 1, w + 2):
        t = face(f)
        if f == 1:
            t = jnp.where(has_lo, t, 0.0)
        if f == w + 1:
            t = jnp.where(has_hi, t, 0.0)
        tx[f] = t
    first_sweep(0, "hi", 1 - px, 0)
    first_sweep(1, "lo", px, 1)
    first_sweep(w, "hi", px, 2)
    first_sweep(w + 1, "lo", 1 - px, 3)

    def second_sweep(e, kind):
        t_y, t_z, scale, bits = ty[e], tz[e], wd[e], bits_e[e]
        t_ym, t_zm = yp(t_y), zp(t_z)
        txm, txp = tx[e], tx[e + 1]

        def shifts(v):
            a, b = t_y * yn(v), t_ym * yp(v)
            c, d = t_z * zn(v), t_zm * zp(v)
            yb = jnp.where(y_top, a, jnp.where(y_bot, b, 0.0))
            zb = jnp.where(z_top, c, jnp.where(z_bot, d, 0.0))
            yi = jnp.where(y_top, 0.0, a) + jnp.where(y_bot, 0.0, b)
            zi = jnp.where(z_top, 0.0, c) + jnp.where(z_bot, 0.0, d)
            return yi, yb, zi, zb

        h, y, z = h1[e], y1[e], z1[e]
        h_yi, h_yb, h_zi, h_zb = shifts(h)
        y_yi, y_yb, y_zi, y_zb = shifts(y)
        z_yi, z_yb, z_zi, z_zb = shifts(z)

        pull_h = h_yi + h_zi + y_yb + z_zb
        pull_y = y_yi + y_zi + h_yb
        pull_z = z_yi + z_zi + h_zb
        if kind != 0:
            pull_h = pull_h + txm * h1[e - 1]
            pull_y = pull_y + txm * y1[e - 1]
            pull_z = pull_z + txm * z1[e - 1]
        else:
            pull_h = pull_h + txm * x1[0]
        if kind != w - 1:
            pull_h = pull_h + txp * h1[e + 1]
            pull_y = pull_y + txp * y1[e + 1]
            pull_z = pull_z + txp * z1[e + 1]
        else:
            pull_h = pull_h + txp * x1[3]
        nh = keep(bits, yz_bit(0, 0), px, THIRD * h + scale * pull_h)
        nyy = keep(bits, yz_bit(1, 0), px, THIRD * y + scale * pull_y)
        nzz = keep(bits, yz_bit(0, 1), px, THIRD * z + scale * pull_z)
        nyz = keep(bits, yz_bit(1, 1), px, scale * (y_zb + z_yb))
        total = (nh + nyy) + (nzz + nyz)
        rest = []
        if kind is not None:
            qx = 1 - px
            if kind in (0, w - 1):
                xo = x1[1] if kind == 0 else x1[2]
                t_out = txm if kind == 0 else txp
                other = e - 1 if kind == 0 else e + 1
                x_yi, x_yb, x_zi, x_zb = shifts(xo)
                nx = THIRD * xo + scale * (x_yi + x_zi + t_out * h1[other])
                rest = [
                    keep(bits, yz_bit(0, 0), qx, nx),
                    keep(bits, yz_bit(1, 0), qx, scale * (x_yb + t_out * y1[other])),
                    keep(bits, yz_bit(0, 1), qx, scale * (x_zb + t_out * z1[other])),
                ]
            else:
                nx = scale * (txm * x1[1] if kind == 1 else txp * x1[2])
                rest = [keep(bits, yz_bit(0, 0), qx, nx)]
            for v in rest:
                total = total + v
        inv = 1.0 / total
        fields = [nh * inv, nyy * inv, nzz * inv, nyz * inv]
        rest = [v * inv for v in rest]
        x = e - 1
        h2[x], y2[x], z2[x], yz2[x] = fields
        b_y = jnp.where(y_top, t_y, jnp.where(y_bot, t_ym, 0.0))
        b_z = jnp.where(z_top, t_z, jnp.where(z_bot, t_zm, 0.0))
        share = 0.02 * por_e[e] + b_y + b_z
        if kind == 0:
            share = share + txm
        if kind == w - 1:
            share = share + txp
        return fields, rest, share, b_y, b_z

    def parts(fields, share, b_y, b_z):
        h, y, z, yz = fields
        own_row = [share * v if v is not None else None for v in fields]
        y_face = [b_y * v if v is not None else None for v in fields]
        z_face = [b_z * v if v is not None else None for v in fields]
        return own_row + y_face + z_face

    def inner_plane(e, acc):
        fields, _, share, b_y, b_z = second_sweep(e, None)
        new = parts(fields, share, b_y, b_z) + [src[e - 1]]
        return tuple(a + b for a, b in zip(acc, new))

    acc = lax.fori_loop(3, w - 1, inner_plane, tuple(zero for _ in range(13)))
    acc = list(acc)
    cross = {}
    sides = {}
    for kind in (0, 1, w - 2, w - 1):
        fields, rest, share, b_y, b_z = second_sweep(kind + 1, kind)
        new = parts(fields, share, b_y, b_z) + [src[kind]]
        acc = [a + b for a, b in zip(acc, new)]
        if kind in (0, w - 1):
            k = 0 if kind == 0 else 1
            for j, v in enumerate(fields + rest):
                edge[k, j] = v
            t_out = tx[1] if kind == 0 else tx[w + 1]
            cross[k] = [t_out * v for v in fields], [t_out * v for v in rest]
        else:
            k = 0 if kind == 1 else 1
            x2[k] = rest[0]
        padded = rest + [None] * (4 - len(rest))
        more = parts(padded, share, b_y, b_z)
        if k in sides:
            sides[k] = [
                b if a is None else (a if b is None else a + b) for a, b in zip(sides[k], more)
            ]
        else:
            sides[k] = more

    def halves(v):
        return [jnp.sum(v[j * BY : (j + 1) * BY], axis=0, keepdims=True) for j in range(ny // BY)]

    def put(index, slot, value):
        for j, r in enumerate(value):
            xbuf[index, 2 * slot + j : 2 * slot + j + 1, :] = r

    def add(a, b, sign, swap):
        if b is None:
            return a
        hb = halves(b)
        if swap:
            hb = [hb[1], hb[0]]
        if a is None:
            return [sign * v for v in hb]
        return [u + sign * v for u, v in zip(a, hb)]

    def fill_slot(slot, sums):
        o, yf, zf = sums[0:4], sums[4:8], sums[8:12]
        same0 = add(add(None, o[0], 1.0, False), yf[1], -1.0, True)
        same1 = add(add(None, o[2], 1.0, False), yf[3], -1.0, True)
        oth0 = add(add(None, o[1], 1.0, False), yf[0], -1.0, True)
        oth1 = add(add(None, o[3], 1.0, False), yf[2], -1.0, True)
        for index, v in ((0, same0), (1, same1), (4, oth0), (5, oth1)):
            if v is not None:
                put(index, slot, v)
        for index, v in ((2, zf[0]), (3, zf[2]), (6, zf[1]), (7, zf[3])):
            if v is not None:
                put(index, slot, [-u for u in halves(v)])

    fill_slot(1, acc[0:12])
    fill_slot(0, sides[0])
    fill_slot(2, sides[1])
    put(0, 3, halves(acc[12]))

    gi = lax.broadcasted_iota(jnp.int32, (nz, nz), 0)
    gc = lax.broadcasted_iota(jnp.int32, (nz, nz), 1)
    nodes_z = nz // BZ
    gk = gi >> 3
    gu = (gi & 7) >= 4
    ck = gc & (nodes_z - 1)
    same_k = gk == ck
    up_k = gu & (gk + 1 == ck)
    dn_k = jnp.logical_not(gu) & (gk - 1 == ck)
    one = lambda c: jnp.where(c, 1.0, 0.0).astype(f32)
    g_all = one(same_k)
    g_lo = one(same_k & jnp.logical_not(gu))
    g_hi = one(same_k & gu)
    g_up = one(up_k)
    g_dn = one(dn_k)
    sub8 = lax.broadcasted_iota(jnp.int32, (8, nz), 0)
    lane8 = lax.broadcasted_iota(jnp.int32, (8, nz), 1)
    pick = sub8 == (lane8 >> 4)

    def dot(a, b):
        return jnp.dot(a, b, precision=HI, preferred_element_type=f32)

    def reduce_rows(base):
        rows = []
        for yo in (0, 1):
            p0, p1, q0, q1 = (xbuf[4 * yo + k] for k in range(4))
            rows.append(dot(p1, g_lo) + dot(q0, g_up))
            rows.append(dot(p0, g_all) + dot(q1, g_up + g_dn))
            rows.append(dot(p1, g_hi) + dot(q0, g_dn))
        for r, v in enumerate(rows):
            gsend[base + r : base + r + 1, :] = jnp.sum(
                jnp.where(pick, v, 0.0), axis=0, keepdims=True
            )

    gsend[...] = jnp.zeros((16, nz), f32)
    reduce_rows(0)
    for k in range(8):
        xbuf[k] = jnp.zeros((8, nz), f32)

    def fill_cross(slot, values):
        for index, v in zip((0, 4, 1, 5), values):
            put(index, slot, [-u for u in halves(v)])

    fill_cross(2, cross[0][0])
    fill_cross(1, cross[0][1])
    fill_cross(0, cross[1][0])
    fill_cross(3, cross[1][1])
    reduce_rows(6)

    def gather(d):
        to = lax.rem(me + d, n)
        return pltpu.make_async_remote_copy(
            src_ref=gsend,
            dst_ref=gbuf.at[pl.ds(pl.multiple_of(me * 16, 16), 16)],
            send_sem=g_send.at[d],
            recv_sem=g_recv.at[me],
            device_id={"gx": to},
        )

    def gather_from(d):
        frm = lax.rem(me + n - d, n)
        return pltpu.make_async_remote_copy(
            src_ref=gsend,
            dst_ref=gbuf.at[pl.ds(pl.multiple_of(frm * 16, 16), 16)],
            send_sem=g_send.at[d],
            recv_sem=g_recv.at[frm],
            device_id={"gx": frm},
        )

    for d in range(1, n):
        gather(d).start()
    gbuf[pl.ds(pl.multiple_of(me * 16, 16), 16), :] = gsend[...]

    up_edge = pltpu.make_async_remote_copy(
        src_ref=edge.at[1], dst_ref=halo.at[0], send_sem=es_send.at[0], recv_sem=es_recv.at[0],
        device_id={"gx": lax.rem(me + 1, n)},
    )
    dn_edge = pltpu.make_async_remote_copy(
        src_ref=edge.at[0], dst_ref=halo.at[1], send_sem=es_send.at[1], recv_sem=es_recv.at[1],
        device_id={"gx": lax.rem(me + n - 1, n)},
    )

    @pl.when(has_hi)
    def _():
        up_edge.start()

    @pl.when(has_lo)
    def _():
        dn_edge.start()

    for d in range(1, n):
        gather_from(d).wait_recv()

    lane_n = lax.broadcasted_iota(jnp.int32, (n, nz), 1)
    sub_n = lax.broadcasted_iota(jnp.int32, (n, nz), 0)
    slot = lane_n >> 5

    def rolls(v, s, axis):
        return pltpu.roll(v, s % v.shape[axis], axis)

    def every(v):
        v = v + rolls(v, 32, 1)
        return v + rolls(v, 64, 1)

    mats = []
    rhs = None
    for r in range(6):
        o = gbuf[pl.ds(r, n, stride=16), :]
        b = gbuf[pl.ds(6 + r, n, stride=16), :]
        if r == 1:
            rhs = every(jnp.where(slot == 3, o, 0.0))
        left = rolls(b, -1, 0)
        right = rolls(b, 1, 0)
        moved = rolls(right, 64, 1)
        m = jnp.where(slot == 3, 0.0, o)
        m = m + jnp.where((slot == 1) | (slot == 2), left, 0.0)
        m = m + jnp.where(slot == 0, right, 0.0) + jnp.where(slot == 1, moved, 0.0)
        mats.append(m)
    weight = every(sum(jnp.abs(m) for m in mats))
    inv_weight = 1.0 / weight

    def apply_op(v):
        a = jnp.where(slot == 0, rolls(v, 1, 0), jnp.where(slot == 2, rolls(v, -1, 0), v))
        b = jnp.where((lane_n & 16) == 0, rolls(a, -16, 1), rolls(a, 16, 1))
        total = mats[1] * a + mats[4] * b
        total = total + mats[0] * rolls(a, 1, 1) + mats[2] * rolls(a, -1, 1)
        total = total + mats[3] * rolls(b, 1, 1) + mats[5] * rolls(b, -1, 1)
        return every(total)

    def mean_square(v):
        s = jnp.sum(jnp.sum(v * v, axis=0, keepdims=True), axis=1, keepdims=True)
        return s / (4.0 * (n * 32))

    first = apply_op(rhs) * inv_weight
    second = apply_op(first) * inv_weight
    spectral = jnp.sqrt(mean_square(second) / (mean_square(first) + 1e-6))
    upper = 1.25 * spectral
    lower = 0.1 * upper
    centre = 0.5 * (upper + lower)
    half = 0.5 * (upper - lower)
    ratio = centre / half
    damping = 1.0 / ratio
    residual = rhs
    update = residual * inv_weight / centre
    sol = jnp.zeros_like(rhs)
    for sweep in range(CHEBY):
        sol = sol + update
        if sweep + 1 < CHEBY:
            residual = residual - apply_op(update)
            following = 1.0 / (2.0 * ratio - damping)
            update = following * damping * update + 2.0 * following / half * residual * inv_weight
            damping = following

    def sol_row(x):
        return jnp.sum(jnp.where(sub_n == x, sol, 0.0), axis=0, keepdims=True)

    rows3 = jnp.where(
        sub8 == 0,
        sol_row(me - 1),
        jnp.where(sub8 == 1, sol_row(me), jnp.where(sub8 == 2, sol_row(me + 1), 0.0)),
    )
    ek = gc >> 3
    eb = jnp.where((gc & 7) >= 4, ek + 1, ek - 1)
    eb_ok = (eb >= 0) & (eb < nodes_z)
    maps = {}
    for j in range(2):
        maps[j, 0] = dot(rows3, one(gi == j * nodes_z + ek))
        maps[j, 1] = dot(rows3, one((gi == j * nodes_z + eb) & eb_ok))
    for x in range(3):
        for jz in range(2):
            a, b = maps[0, jz][x : x + 1], maps[1, jz][x : x + 1]
            sbuf[x, 2 * jz] = jnp.where(row < BY, a, b)
            sbuf[x, 2 * jz + 1] = jnp.where(row < BY, b, a)

    def base_pressure(h, y, z, yz, node):
        return (
            h * sbuf[node, 0] + y * sbuf[node, 1] + z * sbuf[node, 2] + yz * sbuf[node, 3]
        )

    def plane_pressure(x):
        p = base_pressure(h2[x], y2[x], z2[x], yz2[x], 1)
        p_e[x + 1] = p
        pres[x] = p

    loop(2, w - 2, plane_pressure)

    @pl.when(has_lo)
    def _():
        up_edge.wait_recv()

    @pl.when(has_hi)
    def _():
        dn_edge.wait_recv()

    def edge_pressure(ref, k, home, beside):
        p = base_pressure(ref[k, 0], ref[k, 1], ref[k, 2], ref[k, 3], home)
        return p + ref[k, 4] * sbuf[beside, 0] + ref[k, 5] * sbuf[beside, 1] + ref[k, 6] * sbuf[
            beside, 2
        ]

    for x, k, beside in ((0, 0, 0), (w - 1, 1, 2)):
        p = edge_pressure(edge, k, 1, beside)
        p_e[x + 1] = p
        pres[x] = p
    for x, k, beside in ((1, 0, 0), (w - 2, 1, 2)):
        p = base_pressure(h2[x], y2[x], z2[x], yz2[x], 1) + x2[k] * sbuf[beside, 0]
        p_e[x + 1] = p
        pres[x] = p
    p_e[0] = edge_pressure(halo, 0, 0, 1)
    p_e[w + 1] = edge_pressure(halo, 1, 2, 1)

    def flow(t, p, pn, f, fn):
        v = t * (p - pn)
        return v, jnp.where(v > 0, f, fn) * v

    def transport(x, carry):
        vx, wx, top = carry
        e, i = x + 1, x + 2
        p, f = p_e[e], f_e[i]
        vn, wn = flow(tx[e + 1], p, p_e[e + 1], f, f_e[i + 1])
        vy, wy = flow(ty[e], p, yn(p), f, yn(f))
        vz, wz = flow(tz[e], p, zn(p), f, zn(f))
        net = (wn - wx) + (wy - yp(wy)) + (wz - zp(wz))
        s = src[x]
        leaving = jnp.maximum(vn, 0.0) + jnp.maximum(-vx, 0.0)
        leaving = leaving + jnp.maximum(vy, 0.0) + jnp.maximum(-yp(vy), 0.0)
        leaving = leaving + jnp.maximum(vz, 0.0) + jnp.maximum(-zp(vz), 0.0)
        leaving = leaving + jnp.maximum(-s, 0.0)
        gain = jnp.maximum(s, 0.0) + jnp.minimum(s, 0.0) * f - net
        inv = 1.0 / por_e[e]
        new_sat[x] = gain * inv
        return vn, wn, jnp.maximum(top, leaving * inv)

    v0, w0 = flow(tx[1], p_e[0], p_e[1], f_e[1], f_e[2])
    _, _, top = lax.fori_loop(0, w, transport, (v0, w0, zero))
    top = jnp.max(jnp.max(top, axis=0, keepdims=True), axis=1, keepdims=True)
    msend[...] = jnp.broadcast_to(top, (8, nz))

    def spread(d):
        return pltpu.make_async_remote_copy(
            src_ref=msend,
            dst_ref=mbuf.at[pl.ds(pl.multiple_of(me * 8, 8), 8)],
            send_sem=m_send.at[d],
            recv_sem=m_recv.at[me],
            device_id={"gx": lax.rem(me + d, n)},
        )

    def spread_from(d):
        frm = lax.rem(me + n - d, n)
        return pltpu.make_async_remote_copy(
            src_ref=msend,
            dst_ref=mbuf.at[pl.ds(pl.multiple_of(frm * 8, 8), 8)],
            send_sem=m_send.at[d],
            recv_sem=m_recv.at[frm],
            device_id={"gx": frm},
        )

    for d in range(1, n):
        spread(d).start()
    mbuf[pl.ds(pl.multiple_of(me * 8, 8), 8), :] = msend[...]
    for d in range(1, n):
        spread_from(d).wait_recv()
    best = mbuf[0:8, :]
    for k in range(1, n):
        best = jnp.maximum(best, mbuf[8 * k : 8 * k + 8, :])
    step = 0.5 / best[0:1, :]

    def finish(x):
        new_sat[x] = sat_e[x + 2] + step * new_sat[x]

    loop(0, w, finish)

    @pl.when(has_hi)
    def _():
        for c in up_copies:
            c.wait_send()
        up_edge.wait_send()

    @pl.when(has_lo)
    def _():
        for c in dn_copies:
            c.wait_send()
        dn_edge.wait_send()

    for d in range(1, n):
        gather(d).wait_send()
        spread(d).wait_send()


def solution(mesh):
    n = mesh.shape["gx"]

    def on_device(log_perm, saturation, porosity, source, support_bits):
        w, ny, nz = log_perm.shape
        plane = (ny, nz)
        f32 = jnp.float32

        def v(*lead):
            return pltpu.VMEM(lead + plane, f32)

        dma = lambda k: pltpu.SemaphoreType.DMA((k,))
        out = jax.ShapeDtypeStruct(log_perm.shape, f32)
        return pl.pallas_call(
            lambda *refs: kernel(n, *refs),
            name="multiscale_step",
            out_shape=(out, out),
            in_specs=[pl.BlockSpec(memory_space=pl.ANY)] * 5,
            out_specs=(pl.BlockSpec(memory_space=pltpu.VMEM),) * 2,
            scratch_shapes=[
                v(w + 4), v(w + 4), v(w + 2), pltpu.VMEM((w + 2,) + plane, jnp.int32), v(w),
                v(w + 4), v(w + 4), v(w + 4), v(w + 3), v(w + 2), v(w + 2), v(w + 2),
                v(w + 2), v(w + 2), v(w + 2), v(4), v(w), v(w), v(w), v(w), v(2), v(2, 7), v(2, 7),
                pltpu.VMEM((8, 8, nz), f32), pltpu.VMEM((16, nz), f32),
                pltpu.VMEM((16 * n, nz), f32), v(3, 4), v(w + 2),
                pltpu.VMEM((8, nz), f32), pltpu.VMEM((8 * n, nz), f32),
                dma(5), dma(8), dma(8), dma(2), dma(2), dma(n), dma(n), dma(n), dma(n),
            ],
            compiler_params=pltpu.CompilerParams(
                collective_id=0, has_side_effects=True, vmem_limit_bytes=32 * 1024 * 1024
            ),
        )(log_perm, saturation, porosity, source, support_bits)

    spec = P(("groups", "gx"), None, None)
    return jax.shard_map(
        on_device, mesh=mesh, in_specs=(spec,) * 5, out_specs=(spec, spec), check_vma=False
    )
```

```python
import jax
import jax.numpy as jnp
from jax import lax
from jax.experimental import pallas as pl
from jax.experimental.pallas import tpu as pltpu
from jax.sharding import PartitionSpec as P

BX = 16
BY = 16
BZ = 8
CHEBY = 4
THIRD = 1.0 / 3.0
RELAX = 2.0 / 3.0
HI = lax.Precision.HIGHEST


def kernel(
    n, lp_h, sat_h, por_h, src_h, bits_h, pres, new_sat,
    lp_e, sat_e, por_e, bits_e, src, q_e, m_e, f_e, tx, ty, tz, wd,
    h1, y1, z1, x1, h2, y2, z2, yz2, x2, edge, halo, xbuf, gsend, gbuf, sbuf, p_e,
    msend, mbuf, lsem, hs_send, hs_recv, es_send, es_recv, g_send, g_recv, m_send, m_recv,
):
    f32 = jnp.float32
    me = lax.axis_index("gx")
    w = lp_h.shape[0]
    ny, nz = lp_h.shape[1], lp_h.shape[2]
    has_lo = me > 0
    has_hi = me < n - 1

    barrier = pltpu.get_barrier_semaphore()
    for d in range(1, n):
        pl.semaphore_signal(barrier, inc=1, device_id={"gx": lax.rem(me + d, n)})

    own = [
        pltpu.make_async_copy(lp_h, lp_e.at[pl.ds(2, w)], lsem.at[0]),
        pltpu.make_async_copy(sat_h, sat_e.at[pl.ds(2, w)], lsem.at[1]),
        pltpu.make_async_copy(por_h, por_e.at[pl.ds(1, w)], lsem.at[2]),
        pltpu.make_async_copy(bits_h, bits_e.at[pl.ds(1, w)], lsem.at[3]),
        pltpu.make_async_copy(src_h, src, lsem.at[4]),
    ]
    for c in own:
        c.start()

    def halo_copies(up):
        base = 0 if up else 4
        to = lax.rem(me + (1 if up else n - 1), n)
        out = []
        for k, (a, b, width) in enumerate(
            ((lp_h, lp_e, 2), (sat_h, sat_e, 2), (por_h, por_e, 1), (bits_h, bits_e, 1))
        ):
            s0 = w - width if up else 0
            d0 = 0 if up else w + width
            out.append(
                pltpu.make_async_remote_copy(
                    src_ref=a.at[pl.ds(s0, width)],
                    dst_ref=b.at[pl.ds(d0, width)],
                    send_sem=hs_send.at[base + k],
                    recv_sem=hs_recv.at[base + k],
                    device_id={"gx": to},
                )
            )
        return out

    up_copies = halo_copies(True)
    dn_copies = halo_copies(False)

    pl.semaphore_wait(barrier, n - 1)

    @pl.when(has_hi)
    def _():
        for c in up_copies:
            c.start()

    @pl.when(has_lo)
    def _():
        for c in dn_copies:
            c.start()

    def fill(lo):
        e2 = pl.ds(0 if lo else w + 2, 2)
        e1 = pl.ds(0 if lo else w + 1, 1)
        lp_e[e2] = jnp.zeros((2, ny, nz), f32)
        sat_e[e2] = jnp.full((2, ny, nz), 0.5, f32)
        por_e[e1] = jnp.full((1, ny, nz), 0.2, f32)
        bits_e[e1] = jnp.full((1, ny, nz), 255, jnp.int32)
        halo[0 if lo else 1] = jnp.zeros((7, ny, nz), f32)

    @pl.when(jnp.logical_not(has_lo))
    def _():
        fill(True)

    @pl.when(jnp.logical_not(has_hi))
    def _():
        fill(False)

    row = lax.broadcasted_iota(jnp.int32, (ny, nz), 0)
    lane = lax.broadcasted_iota(jnp.int32, (ny, nz), 1)
    y_top = (row & (BY - 1)) == BY - 1
    y_bot = (row & (BY - 1)) == 0
    z_top = (lane & (BZ - 1)) == BZ - 1
    z_bot = (lane & (BZ - 1)) == 0
    py = (row >> 4) & 1
    pz = (lane >> 3) & 1

    def yz_bit(jy, jz):
        return jnp.left_shift(jnp.int32(1), 2 * (py ^ jy) + 4 * (pz ^ jz))

    zero = jnp.zeros((ny, nz), f32)

    def keep(bits, bit_yz, kx, value):
        return jnp.where((bits & (bit_yz * (1 + kx))) != 0, value, zero)

    def yn(v):
        return pltpu.roll(v, ny - 1, 0)

    def yp(v):
        return pltpu.roll(v, 1, 0)

    def zn(v):
        return pltpu.roll(v, nz - 1, 1)

    def zp(v):
        return pltpu.roll(v, 1, 1)

    def prepare(i):
        q_e[i] = jnp.exp(-lp_e[i])
        s = sat_e[i]
        r = 1.0 - s
        m = s * s + 0.25 * (r * r)
        m_e[i] = m
        f_e[i] = s * s / m

    def face(f):
        return (m_e[f] + m_e[f + 1]) / (q_e[f] + q_e[f + 1])

    def first_sweep(e, kind, kx, slot):
        q = q_e[e + 1]
        m = m_e[e + 1]
        t_y = jnp.where(row < ny - 1, (m + yn(m)) / (q + yn(q)), 0.0)
        t_z = jnp.where(lane < nz - 1, (m + zn(m)) / (q + zn(q)), 0.0)
        ty[e] = t_y
        tz[e] = t_z
        t_ym = yp(t_y)
        t_zm = zp(t_z)
        txm, txp = tx[e], tx[e + 1]
        bits = bits_e[e]
        b_y = jnp.where(y_top, t_y, jnp.where(y_bot, t_ym, 0.0))
        b_z = jnp.where(z_top, t_z, jnp.where(z_bot, t_zm, 0.0))
        inner = (t_y + t_ym - b_y) + (t_z + t_zm - b_z)
        diag = 0.02 * por_e[e] + txm + txp + (t_y + t_ym) + (t_z + t_zm)
        scale = RELAX / diag
        wd[e] = scale
        if kind is None:
            inner = inner + txm + txp
        elif kind == "lo":
            inner = inner + txp
        else:
            inner = inner + txm
        h = keep(bits, yz_bit(0, 0), kx, THIRD + scale * inner)
        by = keep(bits, yz_bit(1, 0), kx, scale * b_y)
        bz = keep(bits, yz_bit(0, 1), kx, scale * b_z)
        total = h + by + bz
        if kind is not None:
            bx = keep(bits, yz_bit(0, 0), 1 - kx, scale * (txm if kind == "lo" else txp))
            total = total + bx
        inv = 1.0 / total
        h1[e] = h * inv
        y1[e] = by * inv
        z1[e] = bz * inv
        if kind is not None:
            x1[slot] = bx * inv

    px = lax.rem(me, 2)

    for c in own:
        c.wait()

    def loop(lo, hi, fn):
        def body(i, _):
            fn(i)
            return 0

        lax.fori_loop(lo, hi, body, 0)

    loop(2, w + 2, prepare)

    def set_face(f):
        tx[f] = face(f)

    loop(2, w + 1, set_face)
    loop(2, w, lambda e: first_sweep(e, None, px, 0))

    for k in range(8):
        xbuf[k] = jnp.zeros((8, nz), f32)

    @pl.when(has_lo)
    def _():
        for c in up_copies:
            c.wait_recv()

    @pl.when(has_hi)
    def _():
        for c in dn_copies:
            c.wait_recv()

    for i in (0, 1, w + 2, w + 3):
        prepare(i)
    for f in (0, 1, w + 1, w + 2):
        t = face(f)
        if f == 1:
            t = jnp.where(has_lo, t, 0.0)
        if f == w + 1:
            t = jnp.where(has_hi, t, 0.0)
        tx[f] = t
    first_sweep(0, "hi", 1 - px, 0)
    first_sweep(1, "lo", px, 1)
    first_sweep(w, "hi", px, 2)
    first_sweep(w + 1, "lo", 1 - px, 3)

    def second_sweep(e, kind):
        t_y, t_z, scale, bits = ty[e], tz[e], wd[e], bits_e[e]
        t_ym, t_zm = yp(t_y), zp(t_z)
        txm, txp = tx[e], tx[e + 1]

        def shifts(v):
            a, b = t_y * yn(v), t_ym * yp(v)
            c, d = t_z * zn(v), t_zm * zp(v)
            yb = jnp.where(y_top, a, jnp.where(y_bot, b, 0.0))
            zb = jnp.where(z_top, c, jnp.where(z_bot, d, 0.0))
            yi = jnp.where(y_top, 0.0, a) + jnp.where(y_bot, 0.0, b)
            zi = jnp.where(z_top, 0.0, c) + jnp.where(z_bot, 0.0, d)
            return yi, yb, zi, zb

        h, y, z = h1[e], y1[e], z1[e]
        h_yi, h_yb, h_zi, h_zb = shifts(h)
        y_yi, y_yb, y_zi, y_zb = shifts(y)
        z_yi, z_yb, z_zi, z_zb = shifts(z)

        pull_h = h_yi + h_zi + y_yb + z_zb
        pull_y = y_yi + y_zi + h_yb
        pull_z = z_yi + z_zi + h_zb
        if kind != 0:
            pull_h = pull_h + txm * h1[e - 1]
            pull_y = pull_y + txm * y1[e - 1]
            pull_z = pull_z + txm * z1[e - 1]
        else:
            pull_h = pull_h + txm * x1[0]
        if kind != w - 1:
            pull_h = pull_h + txp * h1[e + 1]
            pull_y = pull_y + txp * y1[e + 1]
            pull_z = pull_z + txp * z1[e + 1]
        else:
            pull_h = pull_h + txp * x1[3]
        nh = keep(bits, yz_bit(0, 0), px, THIRD * h + scale * pull_h)
        nyy = keep(bits, yz_bit(1, 0), px, THIRD * y + scale * pull_y)
        nzz = keep(bits, yz_bit(0, 1), px, THIRD * z + scale * pull_z)
        nyz = keep(bits, yz_bit(1, 1), px, scale * (y_zb + z_yb))
        total = (nh + nyy) + (nzz + nyz)
        rest = []
        if kind is not None:
            qx = 1 - px
            if kind in (0, w - 1):
                xo = x1[1] if kind == 0 else x1[2]
                t_out = txm if kind == 0 else txp
                other = e - 1 if kind == 0 else e + 1
                x_yi, x_yb, x_zi, x_zb = shifts(xo)
                nx = THIRD * xo + scale * (x_yi + x_zi + t_out * h1[other])
                rest = [
                    keep(bits, yz_bit(0, 0), qx, nx),
                    keep(bits, yz_bit(1, 0), qx, scale * (x_yb + t_out * y1[other])),
                    keep(bits, yz_bit(0, 1), qx, scale * (x_zb + t_out * z1[other])),
                ]
            else:
                nx = scale * (txm * x1[1] if kind == 1 else txp * x1[2])
                rest = [keep(bits, yz_bit(0, 0), qx, nx)]
            for v in rest:
                total = total + v
        inv = 1.0 / total
        fields = [nh * inv, nyy * inv, nzz * inv, nyz * inv]
        rest = [v * inv for v in rest]
        x = e - 1
        h2[x], y2[x], z2[x], yz2[x] = fields
        b_y = jnp.where(y_top, t_y, jnp.where(y_bot, t_ym, 0.0))
        b_z = jnp.where(z_top, t_z, jnp.where(z_bot, t_zm, 0.0))
        share = 0.02 * por_e[e] + b_y + b_z
        if kind == 0:
            share = share + txm
        if kind == w - 1:
            share = share + txp
        return fields, rest, share, b_y, b_z

    def parts(fields, share, b_y, b_z):
        h, y, z, yz = fields
        own_row = [share * v if v is not None else None for v in fields]
        y_face = [b_y * v if v is not None else None for v in fields]
        z_face = [b_z * v if v is not None else None for v in fields]
        return own_row + y_face + z_face

    def inner_plane(e, acc):
        fields, _, share, b_y, b_z = second_sweep(e, None)
        new = parts(fields, share, b_y, b_z) + [src[e - 1]]
        return tuple(a + b for a, b in zip(acc, new))

    acc = lax.fori_loop(3, w - 1, inner_plane, tuple(zero for _ in range(13)))
    acc = list(acc)
    cross = {}
    sides = {}
    for kind in (0, 1, w - 2, w - 1):
        fields, rest, share, b_y, b_z = second_sweep(kind + 1, kind)
        new = parts(fields, share, b_y, b_z) + [src[kind]]
        acc = [a + b for a, b in zip(acc, new)]
        if kind in (0, w - 1):
            k = 0 if kind == 0 else 1
            for j, v in enumerate(fields + rest):
                edge[k, j] = v
            t_out = tx[1] if kind == 0 else tx[w + 1]
            cross[k] = [t_out * v for v in fields], [t_out * v for v in rest]
        else:
            k = 0 if kind == 1 else 1
            x2[k] = rest[0]
        padded = rest + [None] * (4 - len(rest))
        more = parts(padded, share, b_y, b_z)
        if k in sides:
            sides[k] = [
                b if a is None else (a if b is None else a + b) for a, b in zip(sides[k], more)
            ]
        else:
            sides[k] = more

    def halves(v):
        return [jnp.sum(v[j * BY : (j + 1) * BY], axis=0, keepdims=True) for j in range(ny // BY)]

    def put(index, slot, value):
        for j, r in enumerate(value):
            xbuf[index, 2 * slot + j : 2 * slot + j + 1, :] = r

    def add(a, b, sign, swap):
        if b is None:
            return a
        hb = halves(b)
        if swap:
            hb = [hb[1], hb[0]]
        if a is None:
            return [sign * v for v in hb]
        return [u + sign * v for u, v in zip(a, hb)]

    def fill_slot(slot, sums):
        o, yf, zf = sums[0:4], sums[4:8], sums[8:12]
        same0 = add(add(None, o[0], 1.0, False), yf[1], -1.0, True)
        same1 = add(add(None, o[2], 1.0, False), yf[3], -1.0, True)
        oth0 = add(add(None, o[1], 1.0, False), yf[0], -1.0, True)
        oth1 = add(add(None, o[3], 1.0, False), yf[2], -1.0, True)
        for index, v in ((0, same0), (1, same1), (4, oth0), (5, oth1)):
            if v is not None:
                put(index, slot, v)
        for index, v in ((2, zf[0]), (3, zf[2]), (6, zf[1]), (7, zf[3])):
            if v is not None:
                put(index, slot, [-u for u in halves(v)])

    fill_slot(1, acc[0:12])
    fill_slot(0, sides[0])
    fill_slot(2, sides[1])
    put(0, 3, halves(acc[12]))

    gi = lax.broadcasted_iota(jnp.int32, (nz, nz), 0)
    gc = lax.broadcasted_iota(jnp.int32, (nz, nz), 1)
    nodes_z = nz // BZ
    gk = gi >> 3
    gu = (gi & 7) >= 4
    ck = gc & (nodes_z - 1)
    same_k = gk == ck
    up_k = gu & (gk + 1 == ck)
    dn_k = jnp.logical_not(gu) & (gk - 1 == ck)
    one = lambda c: jnp.where(c, 1.0, 0.0).astype(f32)
    g_all = one(same_k)
    g_lo = one(same_k & jnp.logical_not(gu))
    g_hi = one(same_k & gu)
    g_up = one(up_k)
    g_dn = one(dn_k)
    sub8 = lax.broadcasted_iota(jnp.int32, (8, nz), 0)
    lane8 = lax.broadcasted_iota(jnp.int32, (8, nz), 1)
    pick = sub8 == (lane8 >> 4)

    def dot(a, b):
        return jnp.dot(a, b, precision=HI, preferred_element_type=f32)

    def reduce_rows(base):
        rows = []
        for yo in (0, 1):
            p0, p1, q0, q1 = (xbuf[4 * yo + k] for k in range(4))
            rows.append(dot(p1, g_lo) + dot(q0, g_up))
            rows.append(dot(p0, g_all) + dot(q1, g_up + g_dn))
            rows.append(dot(p1, g_hi) + dot(q0, g_dn))
        for r, v in enumerate(rows):
            gsend[base + r : base + r + 1, :] = jnp.sum(
                jnp.where(pick, v, 0.0), axis=0, keepdims=True
            )

    gsend[...] = jnp.zeros((16, nz), f32)
    reduce_rows(0)
    for k in range(8):
        xbuf[k] = jnp.zeros((8, nz), f32)

    def fill_cross(slot, values):
        for index, v in zip((0, 4, 1, 5), values):
            put(index, slot, [-u for u in halves(v)])

    fill_cross(2, cross[0][0])
    fill_cross(1, cross[0][1])
    fill_cross(0, cross[1][0])
    fill_cross(3, cross[1][1])
    reduce_rows(6)

    def gather(d):
        to = lax.rem(me + d, n)
        return pltpu.make_async_remote_copy(
            src_ref=gsend,
            dst_ref=gbuf.at[pl.ds(pl.multiple_of(me * 16, 16), 16)],
            send_sem=g_send.at[d],
            recv_sem=g_recv.at[me],
            device_id={"gx": to},
        )

    def gather_from(d):
        frm = lax.rem(me + n - d, n)
        return pltpu.make_async_remote_copy(
            src_ref=gsend,
            dst_ref=gbuf.at[pl.ds(pl.multiple_of(frm * 16, 16), 16)],
            send_sem=g_send.at[d],
            recv_sem=g_recv.at[frm],
            device_id={"gx": frm},
        )

    for d in range(1, n):
        gather(d).start()
    gbuf[pl.ds(pl.multiple_of(me * 16, 16), 16), :] = gsend[...]

    up_edge = pltpu.make_async_remote_copy(
        src_ref=edge.at[1], dst_ref=halo.at[0], send_sem=es_send.at[0], recv_sem=es_recv.at[0],
        device_id={"gx": lax.rem(me + 1, n)},
    )
    dn_edge = pltpu.make_async_remote_copy(
        src_ref=edge.at[0], dst_ref=halo.at[1], send_sem=es_send.at[1], recv_sem=es_recv.at[1],
        device_id={"gx": lax.rem(me + n - 1, n)},
    )

    @pl.when(has_hi)
    def _():
        up_edge.start()

    @pl.when(has_lo)
    def _():
        dn_edge.start()

    for d in range(1, n):
        gather_from(d).wait_recv()

    lane_n = lax.broadcasted_iota(jnp.int32, (n, nz), 1)
    sub_n = lax.broadcasted_iota(jnp.int32, (n, nz), 0)
    slot = lane_n >> 5

    def rolls(v, s, axis):
        return pltpu.roll(v, s % v.shape[axis], axis)

    def every(v):
        v = v + rolls(v, 32, 1)
        return v + rolls(v, 64, 1)

    mats = []
    rhs = None
    for r in range(6):
        o = gbuf[pl.ds(r, n, stride=16), :]
        b = gbuf[pl.ds(6 + r, n, stride=16), :]
        if r == 1:
            rhs = every(jnp.where(slot == 3, o, 0.0))
        left = rolls(b, -1, 0)
        right = rolls(b, 1, 0)
        moved = rolls(right, 64, 1)
        m = jnp.where(slot == 3, 0.0, o)
        m = m + jnp.where((slot == 1) | (slot == 2), left, 0.0)
        m = m + jnp.where(slot == 0, right, 0.0) + jnp.where(slot == 1, moved, 0.0)
        mats.append(m)
    weight = every(sum(jnp.abs(m) for m in mats))
    inv_weight = 1.0 / weight

    def apply_op(v):
        a = jnp.where(slot == 0, rolls(v, 1, 0), jnp.where(slot == 2, rolls(v, -1, 0), v))
        b = jnp.where((lane_n & 16) == 0, rolls(a, -16, 1), rolls(a, 16, 1))
        total = mats[1] * a + mats[4] * b
        total = total + mats[0] * rolls(a, 1, 1) + mats[2] * rolls(a, -1, 1)
        total = total + mats[3] * rolls(b, 1, 1) + mats[5] * rolls(b, -1, 1)
        return every(total)

    def mean_square(v):
        s = jnp.sum(jnp.sum(v * v, axis=0, keepdims=True), axis=1, keepdims=True)
        return s / (4.0 * (n * 32))

    first = apply_op(rhs) * inv_weight
    second = apply_op(first) * inv_weight
    spectral = jnp.sqrt(mean_square(second) / (mean_square(first) + 1e-6))
    upper = 1.25 * spectral
    lower = 0.1 * upper
    centre = 0.5 * (upper + lower)
    half = 0.5 * (upper - lower)
    ratio = centre / half
    damping = 1.0 / ratio
    residual = rhs
    update = residual * inv_weight / centre
    sol = jnp.zeros_like(rhs)
    for sweep in range(CHEBY):
        sol = sol + update
        if sweep + 1 < CHEBY:
            residual = residual - apply_op(update)
            following = 1.0 / (2.0 * ratio - damping)
            update = following * damping * update + 2.0 * following / half * residual * inv_weight
            damping = following

    def sol_row(x):
        return jnp.sum(jnp.where(sub_n == x, sol, 0.0), axis=0, keepdims=True)

    rows3 = jnp.where(
        sub8 == 0,
        sol_row(me - 1),
        jnp.where(sub8 == 1, sol_row(me), jnp.where(sub8 == 2, sol_row(me + 1), 0.0)),
    )
    ek = gc >> 3
    eb = jnp.where((gc & 7) >= 4, ek + 1, ek - 1)
    eb_ok = (eb >= 0) & (eb < nodes_z)
    maps = {}
    for j in range(2):
        maps[j, 0] = dot(rows3, one(gi == j * nodes_z + ek))
        maps[j, 1] = dot(rows3, one((gi == j * nodes_z + eb) & eb_ok))
    for x in range(3):
        for jz in range(2):
            a, b = maps[0, jz][x : x + 1], maps[1, jz][x : x + 1]
            sbuf[x, 2 * jz] = jnp.where(row < BY, a, b)
            sbuf[x, 2 * jz + 1] = jnp.where(row < BY, b, a)

    def base_pressure(h, y, z, yz, node):
        return (
            h * sbuf[node, 0] + y * sbuf[node, 1] + z * sbuf[node, 2] + yz * sbuf[node, 3]
        )

    def plane_pressure(x):
        p = base_pressure(h2[x], y2[x], z2[x], yz2[x], 1)
        p_e[x + 1] = p
        pres[x] = p

    loop(2, w - 2, plane_pressure)

    @pl.when(has_lo)
    def _():
        up_edge.wait_recv()

    @pl.when(has_hi)
    def _():
        dn_edge.wait_recv()

    def edge_pressure(ref, k, home, beside):
        p = base_pressure(ref[k, 0], ref[k, 1], ref[k, 2], ref[k, 3], home)
        return p + ref[k, 4] * sbuf[beside, 0] + ref[k, 5] * sbuf[beside, 1] + ref[k, 6] * sbuf[
            beside, 2
        ]

    for x, k, beside in ((0, 0, 0), (w - 1, 1, 2)):
        p = edge_pressure(edge, k, 1, beside)
        p_e[x + 1] = p
        pres[x] = p
    for x, k, beside in ((1, 0, 0), (w - 2, 1, 2)):
        p = base_pressure(h2[x], y2[x], z2[x], yz2[x], 1) + x2[k] * sbuf[beside, 0]
        p_e[x + 1] = p
        pres[x] = p
    p_e[0] = edge_pressure(halo, 0, 0, 1)
    p_e[w + 1] = edge_pressure(halo, 1, 2, 1)

    def flow(t, p, pn, f, fn):
        v = t * (p - pn)
        return v, jnp.where(v > 0, f, fn) * v

    def transport(x, carry):
        vx, wx, top = carry
        e, i = x + 1, x + 2
        p, f = p_e[e], f_e[i]
        vn, wn = flow(tx[e + 1], p, p_e[e + 1], f, f_e[i + 1])
        vy, wy = flow(ty[e], p, yn(p), f, yn(f))
        vz, wz = flow(tz[e], p, zn(p), f, zn(f))
        net = (wn - wx) + (wy - yp(wy)) + (wz - zp(wz))
        s = src[x]
        leaving = jnp.maximum(vn, 0.0) + jnp.maximum(-vx, 0.0)
        leaving = leaving + jnp.maximum(vy, 0.0) + jnp.maximum(-yp(vy), 0.0)
        leaving = leaving + jnp.maximum(vz, 0.0) + jnp.maximum(-zp(vz), 0.0)
        leaving = leaving + jnp.maximum(-s, 0.0)
        gain = jnp.maximum(s, 0.0) + jnp.minimum(s, 0.0) * f - net
        inv = 1.0 / por_e[e]
        new_sat[x] = gain * inv
        return vn, wn, jnp.maximum(top, leaving * inv)

    v0, w0 = flow(tx[1], p_e[0], p_e[1], f_e[1], f_e[2])
    _, _, top = lax.fori_loop(0, w, transport, (v0, w0, zero))
    top = jnp.max(jnp.max(top, axis=0, keepdims=True), axis=1, keepdims=True)
    msend[...] = jnp.broadcast_to(top, (8, nz))

    def spread(d):
        return pltpu.make_async_remote_copy(
            src_ref=msend,
            dst_ref=mbuf.at[pl.ds(pl.multiple_of(me * 8, 8), 8)],
            send_sem=m_send.at[d],
            recv_sem=m_recv.at[me],
            device_id={"gx": lax.rem(me + d, n)},
        )

    def spread_from(d):
        frm = lax.rem(me + n - d, n)
        return pltpu.make_async_remote_copy(
            src_ref=msend,
            dst_ref=mbuf.at[pl.ds(pl.multiple_of(frm * 8, 8), 8)],
            send_sem=m_send.at[d],
            recv_sem=m_recv.at[frm],
            device_id={"gx": frm},
        )

    for d in range(1, n):
        spread(d).start()
    mbuf[pl.ds(pl.multiple_of(me * 8, 8), 8), :] = msend[...]
    for d in range(1, n):
        spread_from(d).wait_recv()
    best = mbuf[0:8, :]
    for k in range(1, n):
        best = jnp.maximum(best, mbuf[8 * k : 8 * k + 8, :])
    step = 0.5 / best[0:1, :]

    def finish(x):
        new_sat[x] = sat_e[x + 2] + step * new_sat[x]

    loop(0, w, finish)

    @pl.when(has_hi)
    def _():
        for c in up_copies:
            c.wait_send()
        up_edge.wait_send()

    @pl.when(has_lo)
    def _():
        for c in dn_copies:
            c.wait_send()
        dn_edge.wait_send()

    for d in range(1, n):
        gather(d).wait_send()
        spread(d).wait_send()


def solution(mesh):
    n = mesh.shape["gx"]

    def on_device(log_perm, saturation, porosity, source, support_bits):
        w, ny, nz = log_perm.shape
        plane = (ny, nz)
        f32 = jnp.float32

        def v(*lead):
            return pltpu.VMEM(lead + plane, f32)

        dma = lambda k: pltpu.SemaphoreType.DMA((k,))
        out = jax.ShapeDtypeStruct(log_perm.shape, f32)
        return pl.pallas_call(
            lambda *refs: kernel(n, *refs),
            name="multiscale_step",
            out_shape=(out, out),
            in_specs=[pl.BlockSpec(memory_space=pltpu.HBM)] * 5,
            out_specs=(pl.BlockSpec(memory_space=pltpu.VMEM),) * 2,
            scratch_shapes=[
                v(w + 4), v(w + 4), v(w + 2), pltpu.VMEM((w + 2,) + plane, jnp.int32), v(w),
                v(w + 4), v(w + 4), v(w + 4), v(w + 3), v(w + 2), v(w + 2), v(w + 2),
                v(w + 2), v(w + 2), v(w + 2), v(4), v(w), v(w), v(w), v(w), v(2), v(2, 7), v(2, 7),
                pltpu.VMEM((8, 8, nz), f32), pltpu.VMEM((16, nz), f32),
                pltpu.VMEM((16 * n, nz), f32), v(3, 4), v(w + 2),
                pltpu.VMEM((8, nz), f32), pltpu.VMEM((8 * n, nz), f32),
                dma(5), dma(8), dma(8), dma(2), dma(2), dma(n), dma(n), dma(n), dma(n),
            ],
            compiler_params=pltpu.CompilerParams(
                collective_id=0, has_side_effects=True, vmem_limit_bytes=67043328
            ),
        )(log_perm, saturation, porosity, source, support_bits)

    spec = P(("groups", "gx"), None, None)
    return jax.shard_map(
        on_device, mesh=mesh, in_specs=(spec,) * 5, out_specs=(spec, spec), check_vma=False
    )
```

```python
import jax
import jax.numpy as jnp
from jax import lax
from jax.experimental import pallas as pl
from jax.experimental.pallas import tpu as pltpu
from jax.sharding import PartitionSpec as P

BX = 16
BY = 16
BZ = 8
CHEBY = 4
THIRD = 1.0 / 3.0
RELAX = 2.0 / 3.0
ROWS = 12


def kernel(
    n, lp_h, sat_h, por_h, src_h, bits_h, pres, new_sat,
    lp_e, sat_e, por_e, bits_e, src, q_e, m_e, f_e, tx, ty, tz, wd,
    h1, y1, z1, x1, h2, y2, z2, yz2, x2, edge, halo, pa, pb, ga, gb, ge, gsend, gbuf, sbuf, p_e,
    msend, mbuf, lsem, hs_send, hs_recv, es_send, es_recv, g_send, g_recv, m_send, m_recv,
):
    f32 = jnp.float32
    me = lax.axis_index("gx")
    w = lp_h.shape[0]
    ny, nz = lp_h.shape[1], lp_h.shape[2]
    has_lo = me > 0
    has_hi = me < n - 1

    barrier = pltpu.get_barrier_semaphore()
    for d in range(1, n):
        pl.semaphore_signal(barrier, inc=1, device_id={"gx": lax.rem(me + d, n)})

    own = [
        pltpu.make_async_copy(lp_h, lp_e.at[pl.ds(2, w)], lsem.at[0]),
        pltpu.make_async_copy(sat_h, sat_e.at[pl.ds(2, w)], lsem.at[1]),
        pltpu.make_async_copy(por_h, por_e.at[pl.ds(1, w)], lsem.at[2]),
        pltpu.make_async_copy(bits_h, bits_e.at[pl.ds(1, w)], lsem.at[3]),
        pltpu.make_async_copy(src_h, src, lsem.at[4]),
    ]
    for c in own:
        c.start()

    def halo_copies(up):
        base = 0 if up else 4
        to = lax.rem(me + (1 if up else n - 1), n)
        out = []
        for k, (a, b, width) in enumerate(
            ((lp_h, lp_e, 2), (sat_h, sat_e, 2), (por_h, por_e, 1), (bits_h, bits_e, 1))
        ):
            s0 = w - width if up else 0
            d0 = 0 if up else w + width
            out.append(
                pltpu.make_async_remote_copy(
                    src_ref=a.at[pl.ds(s0, width)],
                    dst_ref=b.at[pl.ds(d0, width)],
                    send_sem=hs_send.at[base + k],
                    recv_sem=hs_recv.at[base + k],
                    device_id={"gx": to},
                )
            )
        return out

    up_copies = halo_copies(True)
    dn_copies = halo_copies(False)

    def fill(lo):
        e2 = pl.ds(0 if lo else w + 2, 2)
        e1 = pl.ds(0 if lo else w + 1, 1)
        lp_e[e2] = jnp.zeros((2, ny, nz), f32)
        sat_e[e2] = jnp.full((2, ny, nz), 0.5, f32)
        por_e[e1] = jnp.full((1, ny, nz), 0.2, f32)
        bits_e[e1] = jnp.full((1, ny, nz), 255, jnp.int32)
        halo[0 if lo else 1] = jnp.zeros((7, ny, nz), f32)

    @pl.when(jnp.logical_not(has_lo))
    def _():
        fill(True)

    @pl.when(jnp.logical_not(has_hi))
    def _():
        fill(False)

    row = lax.broadcasted_iota(jnp.int32, (ny, nz), 0)
    lane = lax.broadcasted_iota(jnp.int32, (ny, nz), 1)
    y_top = (row & (BY - 1)) == BY - 1
    y_bot = (row & (BY - 1)) == 0
    z_top = (lane & (BZ - 1)) == BZ - 1
    z_bot = (lane & (BZ - 1)) == 0
    py = (row >> 4) & 1
    pz = (lane >> 3) & 1

    def yz_bit(jy, jz):
        return jnp.left_shift(jnp.int32(1), 2 * (py ^ jy) + 4 * (pz ^ jz))

    zero = jnp.zeros((ny, nz), f32)

    def keep(bits, bit_yz, kx, value):
        return jnp.where((bits & (bit_yz * (1 + kx))) != 0, value, zero)

    def yn(v):
        return pltpu.roll(v, ny - 1, 0)

    def yp(v):
        return pltpu.roll(v, 1, 0)

    def zn(v):
        return pltpu.roll(v, nz - 1, 1)

    def zp(v):
        return pltpu.roll(v, 1, 1)

    def prepare(i):
        q_e[i] = jnp.exp(-lp_e[i])
        s = sat_e[i]
        r = 1.0 - s
        m = s * s + 0.25 * (r * r)
        m_e[i] = m
        f_e[i] = s * s / m

    def face(f):
        return (m_e[f] + m_e[f + 1]) / (q_e[f] + q_e[f + 1])

    def first_sweep(e, kind, kx, slot):
        q = q_e[e + 1]
        m = m_e[e + 1]
        t_y = jnp.where(row < ny - 1, (m + yn(m)) / (q + yn(q)), 0.0)
        t_z = jnp.where(lane < nz - 1, (m + zn(m)) / (q + zn(q)), 0.0)
        ty[e] = t_y
        tz[e] = t_z
        t_ym = yp(t_y)
        t_zm = zp(t_z)
        txm, txp = tx[e], tx[e + 1]
        bits = bits_e[e]
        b_y = jnp.where(y_top, t_y, jnp.where(y_bot, t_ym, 0.0))
        b_z = jnp.where(z_top, t_z, jnp.where(z_bot, t_zm, 0.0))
        inner = (t_y + t_ym - b_y) + (t_z + t_zm - b_z)
        diag = 0.02 * por_e[e] + txm + txp + (t_y + t_ym) + (t_z + t_zm)
        scale = RELAX / diag
        wd[e] = scale
        if kind is None:
            inner = inner + txm + txp
        elif kind == "lo":
            inner = inner + txp
        else:
            inner = inner + txm
        h = keep(bits, yz_bit(0, 0), kx, THIRD + scale * inner)
        by = keep(bits, yz_bit(1, 0), kx, scale * b_y)
        bz = keep(bits, yz_bit(0, 1), kx, scale * b_z)
        total = h + by + bz
        if kind is not None:
            bx = keep(bits, yz_bit(0, 0), 1 - kx, scale * (txm if kind == "lo" else txp))
            total = total + bx
        inv = 1.0 / total
        h1[e] = h * inv
        y1[e] = by * inv
        z1[e] = bz * inv
        if kind is not None:
            x1[slot] = bx * inv

    gi = lax.broadcasted_iota(jnp.int32, (nz, nz), 0)
    gc = lax.broadcasted_iota(jnp.int32, (nz, nz), 1)
    nodes_z = nz // BZ
    gk = gi >> 3
    gu = (gi & 7) >= 4
    ck = gc & (nodes_z - 1)
    same_k = gk == ck
    up_k = gu & (gk + 1 == ck)
    dn_k = jnp.logical_not(gu) & (gk - 1 == ck)
    one = lambda c: jnp.where(c, 1.0, 0.0).astype(jnp.bfloat16)
    ga[0:nz, 0:nz] = one(same_k & jnp.logical_not(gu))
    ga[0:nz, nz:] = one(same_k & gu)
    ga[nz:, 0:nz] = one(up_k)
    ga[nz:, nz:] = one(dn_k)
    gb[0:nz, :] = one(same_k)
    gb[nz:, :] = one(up_k | dn_k)
    ek = gc >> 3
    eb = jnp.where((gc & 7) >= 4, ek + 1, ek - 1)
    eb_ok = (eb >= 0) & (eb < nodes_z)
    for j in range(2):
        ge[:, 2 * j * nz : (2 * j + 1) * nz] = one(gi == j * nodes_z + ek)
        ge[:, (2 * j + 1) * nz : (2 * j + 2) * nz] = one((gi == j * nodes_z + eb) & eb_ok)
    pa[...] = jnp.zeros(pa.shape, f32)
    pb[...] = jnp.zeros(pb.shape, f32)

    def exact_dot(a, b):
        a1 = a.astype(jnp.bfloat16)
        r1 = a - a1.astype(f32)
        a2 = r1.astype(jnp.bfloat16)
        a3 = (r1 - a2.astype(f32)).astype(jnp.bfloat16)
        m = a.shape[0]
        out = jnp.dot(jnp.concatenate([a1, a2, a3], axis=0), b, preferred_element_type=f32)
        return (out[2 * m :] + out[m : 2 * m]) + out[:m]

    px = lax.rem(me, 2)

    for c in own:
        c.wait()

    def loop(lo, hi, fn):
        def body(i, _):
            fn(i)
            return 0

        lax.fori_loop(lo, hi, body, 0)

    loop(2, w + 2, prepare)

    def set_face(f):
        tx[f] = face(f)

    loop(2, w + 1, set_face)
    loop(2, w, lambda e: first_sweep(e, None, px, 0))

    pl.semaphore_wait(barrier, n - 1)

    @pl.when(has_hi)
    def _():
        for c in up_copies:
            c.start()

    @pl.when(has_lo)
    def _():
        for c in dn_copies:
            c.start()

    def second_sweep(e, kind):
        t_y, t_z, scale, bits = ty[e], tz[e], wd[e], bits_e[e]
        t_ym, t_zm = yp(t_y), zp(t_z)
        txm, txp = tx[e], tx[e + 1]

        def shifts(v):
            a, b = t_y * yn(v), t_ym * yp(v)
            c, d = t_z * zn(v), t_zm * zp(v)
            yb = jnp.where(y_top, a, jnp.where(y_bot, b, 0.0))
            zb = jnp.where(z_top, c, jnp.where(z_bot, d, 0.0))
            yi = jnp.where(y_top, 0.0, a) + jnp.where(y_bot, 0.0, b)
            zi = jnp.where(z_top, 0.0, c) + jnp.where(z_bot, 0.0, d)
            return yi, yb, zi, zb

        h, y, z = h1[e], y1[e], z1[e]
        h_yi, h_yb, h_zi, h_zb = shifts(h)
        y_yi, y_yb, y_zi, y_zb = shifts(y)
        z_yi, z_yb, z_zi, z_zb = shifts(z)

        pull_h = h_yi + h_zi + y_yb + z_zb
        pull_y = y_yi + y_zi + h_yb
        pull_z = z_yi + z_zi + h_zb
        if kind != 0:
            pull_h = pull_h + txm * h1[e - 1]
            pull_y = pull_y + txm * y1[e - 1]
            pull_z = pull_z + txm * z1[e - 1]
        else:
            pull_h = pull_h + txm * x1[0]
        if kind != w - 1:
            pull_h = pull_h + txp * h1[e + 1]
            pull_y = pull_y + txp * y1[e + 1]
            pull_z = pull_z + txp * z1[e + 1]
        else:
            pull_h = pull_h + txp * x1[3]
        nh = keep(bits, yz_bit(0, 0), px, THIRD * h + scale * pull_h)
        nyy = keep(bits, yz_bit(1, 0), px, THIRD * y + scale * pull_y)
        nzz = keep(bits, yz_bit(0, 1), px, THIRD * z + scale * pull_z)
        nyz = keep(bits, yz_bit(1, 1), px, scale * (y_zb + z_yb))
        total = (nh + nyy) + (nzz + nyz)
        rest = []
        if kind is not None:
            qx = 1 - px
            if kind in (0, w - 1):
                xo = x1[1] if kind == 0 else x1[2]
                t_out = txm if kind == 0 else txp
                other = e - 1 if kind == 0 else e + 1
                x_yi, x_yb, x_zi, x_zb = shifts(xo)
                nx = THIRD * xo + scale * (x_yi + x_zi + t_out * h1[other])
                rest = [
                    keep(bits, yz_bit(0, 0), qx, nx),
                    keep(bits, yz_bit(1, 0), qx, scale * (x_yb + t_out * y1[other])),
                    keep(bits, yz_bit(0, 1), qx, scale * (x_zb + t_out * z1[other])),
                ]
            else:
                nx = scale * (txm * x1[1] if kind == 1 else txp * x1[2])
                rest = [keep(bits, yz_bit(0, 0), qx, nx)]
            for v in rest:
                total = total + v
        inv = 1.0 / total
        fields = [nh * inv, nyy * inv, nzz * inv, nyz * inv]
        rest = [v * inv for v in rest]
        x = e - 1
        h2[x], y2[x], z2[x], yz2[x] = fields
        b_y = jnp.where(y_top, t_y, jnp.where(y_bot, t_ym, 0.0))
        b_z = jnp.where(z_top, t_z, jnp.where(z_bot, t_zm, 0.0))
        share = 0.02 * por_e[e] + b_y + b_z
        if kind == 0:
            share = share + txm
        if kind == w - 1:
            share = share + txp
        return fields, rest, share, b_y, b_z

    def parts(fields, share, b_y, b_z):
        h, y, z, yz = fields
        own_row = [share * v if v is not None else None for v in fields]
        y_face = [b_y * v if v is not None else None for v in fields]
        z_face = [b_z * v if v is not None else None for v in fields]
        return own_row + y_face + z_face

    def inner_plane(e, acc):
        fields, _, share, b_y, b_z = second_sweep(e, None)
        new = parts(fields, share, b_y, b_z) + [src[e - 1]]
        return tuple(a + b for a, b in zip(acc, new))

    acc = lax.fori_loop(3, w - 1, inner_plane, tuple(zero for _ in range(13)))

    @pl.when(has_lo)
    def _():
        for c in up_copies:
            c.wait_recv()

    @pl.when(has_hi)
    def _():
        for c in dn_copies:
            c.wait_recv()

    for i in (0, 1, w + 2, w + 3):
        prepare(i)
    for f in (0, 1, w + 1, w + 2):
        t = face(f)
        if f == 1:
            t = jnp.where(has_lo, t, 0.0)
        if f == w + 1:
            t = jnp.where(has_hi, t, 0.0)
        tx[f] = t
    first_sweep(0, "hi", 1 - px, 0)
    first_sweep(1, "lo", px, 1)
    first_sweep(w, "hi", px, 2)
    first_sweep(w + 1, "lo", 1 - px, 3)

    acc = list(acc)
    cross = {}
    sides = {}
    for kind in (0, 1, w - 2, w - 1):
        fields, rest, share, b_y, b_z = second_sweep(kind + 1, kind)
        new = parts(fields, share, b_y, b_z) + [src[kind]]
        acc = [a + b for a, b in zip(acc, new)]
        if kind in (0, w - 1):
            k = 0 if kind == 0 else 1
            for j, v in enumerate(fields + rest):
                edge[k, j] = v
            t_out = tx[1] if kind == 0 else tx[w + 1]
            cross[k] = [t_out * v for v in fields], [t_out * v for v in rest]
        else:
            k = 0 if kind == 1 else 1
            x2[k] = rest[0]
        padded = rest + [None] * (4 - len(rest))
        more = parts(padded, share, b_y, b_z)
        if k in sides:
            sides[k] = [
                b if a is None else (a if b is None else a + b) for a, b in zip(sides[k], more)
            ]
        else:
            sides[k] = more

    def halves(v):
        return [jnp.sum(v[j * BY : (j + 1) * BY], axis=0, keepdims=True) for j in range(ny // BY)]

    def put(index, slot, value, group=0):
        for j, r in enumerate(value):
            ref, col = ((pb, 0), (pa, 0), (pa, nz), (pb, nz))[index % 4]
            at = 16 * group + 8 * (index // 4) + 2 * slot + j
            ref[at : at + 1, col : col + nz] = r

    def add(a, b, sign, swap):
        if b is None:
            return a
        hb = halves(b)
        if swap:
            hb = [hb[1], hb[0]]
        if a is None:
            return [sign * v for v in hb]
        return [u + sign * v for u, v in zip(a, hb)]

    def fill_slot(slot, sums):
        o, yf, zf = sums[0:4], sums[4:8], sums[8:12]
        same0 = add(add(None, o[0], 1.0, False), yf[1], -1.0, True)
        same1 = add(add(None, o[2], 1.0, False), yf[3], -1.0, True)
        oth0 = add(add(None, o[1], 1.0, False), yf[0], -1.0, True)
        oth1 = add(add(None, o[3], 1.0, False), yf[2], -1.0, True)
        for index, v in ((0, same0), (1, same1), (4, oth0), (5, oth1)):
            if v is not None:
                put(index, slot, v)
        for index, v in ((2, zf[0]), (3, zf[2]), (6, zf[1]), (7, zf[3])):
            if v is not None:
                put(index, slot, [-u for u in halves(v)])

    fill_slot(1, acc[0:12])
    fill_slot(0, sides[0])
    fill_slot(2, sides[1])
    put(0, 3, halves(acc[12]))

    sub8 = lax.broadcasted_iota(jnp.int32, (8, nz), 0)
    lane8 = lax.broadcasted_iota(jnp.int32, (8, nz), 1)
    pick = sub8 == (lane8 >> 4)

    def fill_cross(slot, values):
        for index, v in zip((0, 4, 1, 5), values):
            put(index, slot, [-u for u in halves(v)], 1)

    fill_cross(2, cross[0][0])
    fill_cross(1, cross[0][1])
    fill_cross(0, cross[1][0])
    fill_cross(3, cross[1][1])
    out_a = exact_dot(pa[...], ga[...])
    out_b = exact_dot(pb[...], gb[...])
    for group in range(2):
        for yo in range(2):
            at = 16 * group + 8 * yo
            three = (out_a[at : at + 8, 0:nz], out_b[at : at + 8], out_a[at : at + 8, nz:])
            for z, v in enumerate(three):
                r = 6 * group + 3 * yo + z
                gsend[r : r + 1, :] = jnp.sum(jnp.where(pick, v, 0.0), axis=0, keepdims=True)

    def gather(d):
        to = lax.rem(me + d, n)
        return pltpu.make_async_remote_copy(
            src_ref=gsend.at[pl.ds(0, ROWS)],
            dst_ref=gbuf.at[pl.ds(pl.multiple_of(me * 16, 16), ROWS)],
            send_sem=g_send.at[d],
            recv_sem=g_recv.at[me],
            device_id={"gx": to},
        )

    def gather_from(d):
        frm = lax.rem(me + n - d, n)
        return pltpu.make_async_remote_copy(
            src_ref=gsend.at[pl.ds(0, ROWS)],
            dst_ref=gbuf.at[pl.ds(pl.multiple_of(frm * 16, 16), ROWS)],
            send_sem=g_send.at[d],
            recv_sem=g_recv.at[frm],
            device_id={"gx": frm},
        )

    for d in range(1, n):
        gather(d).start()
    gbuf[pl.ds(pl.multiple_of(me * 16, 16), ROWS), :] = gsend[0:ROWS, :]

    up_edge = pltpu.make_async_remote_copy(
        src_ref=edge.at[1], dst_ref=halo.at[0], send_sem=es_send.at[0], recv_sem=es_recv.at[0],
        device_id={"gx": lax.rem(me + 1, n)},
    )
    dn_edge = pltpu.make_async_remote_copy(
        src_ref=edge.at[0], dst_ref=halo.at[1], send_sem=es_send.at[1], recv_sem=es_recv.at[1],
        device_id={"gx": lax.rem(me + n - 1, n)},
    )

    @pl.when(has_hi)
    def _():
        up_edge.start()

    @pl.when(has_lo)
    def _():
        dn_edge.start()

    for d in range(1, n):
        gather_from(d).wait_recv()

    lane_n = lax.broadcasted_iota(jnp.int32, (n, nz), 1)
    sub_n = lax.broadcasted_iota(jnp.int32, (n, nz), 0)
    slot = lane_n >> 5

    def rolls(v, s, axis):
        return pltpu.roll(v, s % v.shape[axis], axis)

    def every(v):
        v = v + rolls(v, 32, 1)
        return v + rolls(v, 64, 1)

    mats = []
    rhs = None
    for r in range(6):
        o = gbuf[pl.ds(r, n, stride=16), :]
        b = gbuf[pl.ds(6 + r, n, stride=16), :]
        if r == 1:
            rhs = every(jnp.where(slot == 3, o, 0.0))
        left = rolls(b, -1, 0)
        right = rolls(b, 1, 0)
        moved = rolls(right, 64, 1)
        m = jnp.where(slot == 3, 0.0, o)
        m = m + jnp.where((slot == 1) | (slot == 2), left, 0.0)
        m = m + jnp.where(slot == 0, right, 0.0) + jnp.where(slot == 1, moved, 0.0)
        mats.append(m)
    weight = every(sum(jnp.abs(m) for m in mats))
    inv_weight = 1.0 / weight

    def apply_op(v):
        a = jnp.where(slot == 0, rolls(v, 1, 0), jnp.where(slot == 2, rolls(v, -1, 0), v))
        b = jnp.where((lane_n & 16) == 0, rolls(a, -16, 1), rolls(a, 16, 1))
        total = mats[1] * a + mats[4] * b
        total = total + mats[0] * rolls(a, 1, 1) + mats[2] * rolls(a, -1, 1)
        total = total + mats[3] * rolls(b, 1, 1) + mats[5] * rolls(b, -1, 1)
        return every(total)

    def mean_square(v):
        s = jnp.sum(jnp.sum(v * v, axis=0, keepdims=True), axis=1, keepdims=True)
        return s / (4.0 * (n * 32))

    first = apply_op(rhs) * inv_weight
    second = apply_op(first) * inv_weight
    spectral = jnp.sqrt(mean_square(second) / (mean_square(first) + 1e-6))
    upper = 1.25 * spectral
    lower = 0.1 * upper
    centre = 0.5 * (upper + lower)
    half = 0.5 * (upper - lower)
    ratio = centre / half
    damping = 1.0 / ratio
    residual = rhs
    update = residual * inv_weight / centre
    sol = jnp.zeros_like(rhs)
    for sweep in range(CHEBY):
        sol = sol + update
        if sweep + 1 < CHEBY:
            residual = residual - apply_op(update)
            following = 1.0 / (2.0 * ratio - damping)
            update = following * damping * update + 2.0 * following / half * residual * inv_weight
            damping = following

    def sol_row(x):
        return jnp.sum(jnp.where(sub_n == x, sol, 0.0), axis=0, keepdims=True)

    rows3 = jnp.where(
        sub8 == 0,
        sol_row(me - 1),
        jnp.where(sub8 == 1, sol_row(me), jnp.where(sub8 == 2, sol_row(me + 1), 0.0)),
    )
    spread_out = exact_dot(rows3, ge[...])
    maps = {
        (j, k): spread_out[:, (2 * j + k) * nz : (2 * j + k + 1) * nz]
        for j in range(2)
        for k in range(2)
    }
    for x in range(3):
        for jz in range(2):
            a, b = maps[0, jz][x : x + 1], maps[1, jz][x : x + 1]
            sbuf[x, 2 * jz] = jnp.where(row < BY, a, b)
            sbuf[x, 2 * jz + 1] = jnp.where(row < BY, b, a)

    def base_pressure(h, y, z, yz, node):
        return (
            h * sbuf[node, 0] + y * sbuf[node, 1] + z * sbuf[node, 2] + yz * sbuf[node, 3]
        )

    def plane_pressure(x):
        p = base_pressure(h2[x], y2[x], z2[x], yz2[x], 1)
        p_e[x + 1] = p
        pres[x] = p

    loop(2, w - 2, plane_pressure)

    @pl.when(has_lo)
    def _():
        up_edge.wait_recv()

    @pl.when(has_hi)
    def _():
        dn_edge.wait_recv()

    def edge_pressure(ref, k, home, beside):
        p = base_pressure(ref[k, 0], ref[k, 1], ref[k, 2], ref[k, 3], home)
        return p + ref[k, 4] * sbuf[beside, 0] + ref[k, 5] * sbuf[beside, 1] + ref[k, 6] * sbuf[
            beside, 2
        ]

    for x, k, beside in ((0, 0, 0), (w - 1, 1, 2)):
        p = edge_pressure(edge, k, 1, beside)
        p_e[x + 1] = p
        pres[x] = p
    for x, k, beside in ((1, 0, 0), (w - 2, 1, 2)):
        p = base_pressure(h2[x], y2[x], z2[x], yz2[x], 1) + x2[k] * sbuf[beside, 0]
        p_e[x + 1] = p
        pres[x] = p
    p_e[0] = edge_pressure(halo, 0, 0, 1)
    p_e[w + 1] = edge_pressure(halo, 1, 2, 1)

    def flow(t, p, pn, f, fn):
        v = t * (p - pn)
        return v, jnp.where(v > 0, f, fn) * v

    def transport(x, carry):
        vx, wx, top = carry
        e, i = x + 1, x + 2
        p, f = p_e[e], f_e[i]
        vn, wn = flow(tx[e + 1], p, p_e[e + 1], f, f_e[i + 1])
        vy, wy = flow(ty[e], p, yn(p), f, yn(f))
        vz, wz = flow(tz[e], p, zn(p), f, zn(f))
        net = (wn - wx) + (wy - yp(wy)) + (wz - zp(wz))
        s = src[x]
        leaving = jnp.maximum(vn, 0.0) + jnp.maximum(-vx, 0.0)
        leaving = leaving + jnp.maximum(vy, 0.0) + jnp.maximum(-yp(vy), 0.0)
        leaving = leaving + jnp.maximum(vz, 0.0) + jnp.maximum(-zp(vz), 0.0)
        leaving = leaving + jnp.maximum(-s, 0.0)
        gain = jnp.maximum(s, 0.0) + jnp.minimum(s, 0.0) * f - net
        inv = 1.0 / por_e[e]
        new_sat[x] = gain * inv
        return vn, wn, jnp.maximum(top, leaving * inv)

    v0, w0 = flow(tx[1], p_e[0], p_e[1], f_e[1], f_e[2])
    _, _, top = lax.fori_loop(0, w, transport, (v0, w0, zero))
    top = jnp.max(jnp.max(top, axis=0, keepdims=True), axis=1, keepdims=True)
    msend[...] = jnp.broadcast_to(top, (1, nz))

    def spread(d):
        return pltpu.make_async_remote_copy(
            src_ref=msend,
            dst_ref=mbuf.at[me],
            send_sem=m_send.at[d],
            recv_sem=m_recv.at[me],
            device_id={"gx": lax.rem(me + d, n)},
        )

    def spread_from(d):
        frm = lax.rem(me + n - d, n)
        return pltpu.make_async_remote_copy(
            src_ref=msend,
            dst_ref=mbuf.at[frm],
            send_sem=m_send.at[d],
            recv_sem=m_recv.at[frm],
            device_id={"gx": frm},
        )

    for d in range(1, n):
        spread(d).start()
    mbuf[me] = msend[...]
    for d in range(1, n):
        spread_from(d).wait_recv()
    best = mbuf[0]
    for k in range(1, n):
        best = jnp.maximum(best, mbuf[k])
    step = 0.5 / best

    def finish(x):
        new_sat[x] = sat_e[x + 2] + step * new_sat[x]

    loop(0, w, finish)

    @pl.when(has_hi)
    def _():
        for c in up_copies:
            c.wait_send()
        up_edge.wait_send()

    @pl.when(has_lo)
    def _():
        for c in dn_copies:
            c.wait_send()
        dn_edge.wait_send()

    for d in range(1, n):
        gather(d).wait_send()
        spread(d).wait_send()


def solution(mesh):
    n = mesh.shape["gx"]

    def on_device(log_perm, saturation, porosity, source, support_bits):
        w, ny, nz = log_perm.shape
        plane = (ny, nz)
        f32 = jnp.float32

        def v(*lead):
            return pltpu.VMEM(lead + plane, f32)

        dma = lambda k: pltpu.SemaphoreType.DMA((k,))
        out = jax.ShapeDtypeStruct(log_perm.shape, f32)
        return pl.pallas_call(
            lambda *refs: kernel(n, *refs),
            name="multiscale_step",
            out_shape=(out, out),
            in_specs=[pl.BlockSpec(memory_space=pltpu.HBM)] * 5,
            out_specs=(pl.BlockSpec(memory_space=pltpu.VMEM),) * 2,
            scratch_shapes=[
                v(w + 4), v(w + 4), v(w + 2), pltpu.VMEM((w + 2,) + plane, jnp.int32), v(w),
                v(w + 4), v(w + 4), v(w + 4), v(w + 3), v(w + 2), v(w + 2), v(w + 2),
                v(w + 2), v(w + 2), v(w + 2), v(4), v(w), v(w), v(w), v(w), v(2), v(2, 7), v(2, 7),
                pltpu.VMEM((32, 2 * nz), f32), pltpu.VMEM((32, 2 * nz), f32),
                pltpu.VMEM((2 * nz, 2 * nz), jnp.bfloat16), pltpu.VMEM((2 * nz, nz), jnp.bfloat16),
                pltpu.VMEM((nz, 4 * nz), jnp.bfloat16), pltpu.VMEM((16, nz), f32),
                pltpu.VMEM((16 * n, nz), f32), v(3, 4), v(w + 2),
                pltpu.VMEM((1, nz), f32), pltpu.VMEM((n, 1, nz), f32),
                dma(5), dma(8), dma(8), dma(2), dma(2), dma(n), dma(n), dma(n), dma(n),
            ],
            compiler_params=pltpu.CompilerParams(
                collective_id=0, has_side_effects=True, vmem_limit_bytes=67043328
            ),
        )(log_perm, saturation, porosity, source, support_bits)

    spec = P(("groups", "gx"), None, None)
    return jax.shard_map(
        on_device, mesh=mesh, in_specs=(spec,) * 5, out_specs=(spec, spec), check_vma=False
    )
```

```python
import jax
import jax.numpy as jnp
from jax import lax
from jax.experimental import pallas as pl
from jax.experimental.pallas import tpu as pltpu
from jax.sharding import PartitionSpec as P

BX = 16
BY = 16
BZ = 8
CHEBY = 4
THIRD = 1.0 / 3.0
RELAX = 2.0 / 3.0
ROWS = 12


def kernel(
    n, lp_h, sat_h, por_h, src_h, bits_h, pres, new_sat,
    lp_e, sat_e, por_e, bits_e, src, q_e, m_e, f_e, tx, ty, tz, wd,
    h1, y1, z1, x1, h2, y2, z2, yz2, x2, edge, halo, pa, pb, ga, gb, ge, gsend, gbuf, sbuf, p_e,
    msend, mbuf, lsem, hs_send, hs_recv, es_send, es_recv, g_send, g_recv, m_send, m_recv,
):
    f32 = jnp.float32
    me = lax.axis_index("gx")
    w = lp_h.shape[0]
    ny, nz = lp_h.shape[1], lp_h.shape[2]
    has_lo = me > 0
    has_hi = me < n - 1

    barrier = pltpu.get_barrier_semaphore()
    for d in range(1, n):
        pl.semaphore_signal(barrier, inc=1, device_id={"gx": lax.rem(me + d, n)})

    own = [
        pltpu.make_async_copy(lp_h, lp_e.at[pl.ds(2, w)], lsem.at[0]),
        pltpu.make_async_copy(sat_h, sat_e.at[pl.ds(2, w)], lsem.at[1]),
        pltpu.make_async_copy(por_h, por_e.at[pl.ds(1, w)], lsem.at[2]),
        pltpu.make_async_copy(bits_h, bits_e.at[pl.ds(1, w)], lsem.at[3]),
        pltpu.make_async_copy(src_h, src, lsem.at[4]),
    ]
    for c in own:
        c.start()

    def halo_copies(up):
        base = 0 if up else 4
        to = lax.rem(me + (1 if up else n - 1), n)
        out = []
        for k, (a, b, width) in enumerate(
            ((lp_h, lp_e, 2), (sat_h, sat_e, 2), (por_h, por_e, 1), (bits_h, bits_e, 1))
        ):
            s0 = w - width if up else 0
            d0 = 0 if up else w + width
            out.append(
                pltpu.make_async_remote_copy(
                    src_ref=a.at[pl.ds(s0, width)],
                    dst_ref=b.at[pl.ds(d0, width)],
                    send_sem=hs_send.at[base + k],
                    recv_sem=hs_recv.at[base + k],
                    device_id={"gx": to},
                )
            )
        return out

    up_copies = halo_copies(True)
    dn_copies = halo_copies(False)

    def fill(lo):
        e2 = pl.ds(0 if lo else w + 2, 2)
        e1 = pl.ds(0 if lo else w + 1, 1)
        lp_e[e2] = jnp.zeros((2, ny, nz), f32)
        sat_e[e2] = jnp.full((2, ny, nz), 0.5, f32)
        por_e[e1] = jnp.full((1, ny, nz), 0.2, f32)
        bits_e[e1] = jnp.full((1, ny, nz), 255, jnp.int32)
        halo[0 if lo else 1] = jnp.zeros((7, ny, nz), f32)

    @pl.when(jnp.logical_not(has_lo))
    def _():
        fill(True)

    @pl.when(jnp.logical_not(has_hi))
    def _():
        fill(False)

    row = lax.broadcasted_iota(jnp.int32, (ny, nz), 0)
    lane = lax.broadcasted_iota(jnp.int32, (ny, nz), 1)
    y_top = (row & (BY - 1)) == BY - 1
    y_bot = (row & (BY - 1)) == 0
    z_top = (lane & (BZ - 1)) == BZ - 1
    z_bot = (lane & (BZ - 1)) == 0
    py = (row >> 4) & 1
    pz = (lane >> 3) & 1

    def yz_bit(jy, jz):
        return jnp.left_shift(jnp.int32(1), 2 * (py ^ jy) + 4 * (pz ^ jz))

    zero = jnp.zeros((ny, nz), f32)

    def keep(bits, bit_yz, kx, value):
        return jnp.where((bits & (bit_yz * (1 + kx))) != 0, value, zero)

    def yn(v):
        return pltpu.roll(v, ny - 1, 0)

    def yp(v):
        return pltpu.roll(v, 1, 0)

    def zn(v):
        return pltpu.roll(v, nz - 1, 1)

    def zp(v):
        return pltpu.roll(v, 1, 1)

    def prepare(i):
        q_e[i] = jnp.exp(-lp_e[i])
        s = sat_e[i]
        r = 1.0 - s
        m = s * s + 0.25 * (r * r)
        m_e[i] = m
        f_e[i] = s * s / m

    def face(f):
        return (m_e[f] + m_e[f + 1]) / (q_e[f] + q_e[f + 1])

    def first_sweep(e, kind, kx, slot):
        q = q_e[e + 1]
        m = m_e[e + 1]
        t_y = jnp.where(row < ny - 1, (m + yn(m)) / (q + yn(q)), 0.0)
        t_z = jnp.where(lane < nz - 1, (m + zn(m)) / (q + zn(q)), 0.0)
        ty[e] = t_y
        tz[e] = t_z
        t_ym = yp(t_y)
        t_zm = zp(t_z)
        txm, txp = tx[e], tx[e + 1]
        bits = bits_e[e]
        b_y = jnp.where(y_top, t_y, jnp.where(y_bot, t_ym, 0.0))
        b_z = jnp.where(z_top, t_z, jnp.where(z_bot, t_zm, 0.0))
        inner = (t_y + t_ym - b_y) + (t_z + t_zm - b_z)
        diag = 0.02 * por_e[e] + txm + txp + (t_y + t_ym) + (t_z + t_zm)
        scale = RELAX / diag
        wd[e] = scale
        if kind is None:
            inner = inner + txm + txp
        elif kind == "lo":
            inner = inner + txp
        else:
            inner = inner + txm
        h = keep(bits, yz_bit(0, 0), kx, THIRD + scale * inner)
        by = keep(bits, yz_bit(1, 0), kx, scale * b_y)
        bz = keep(bits, yz_bit(0, 1), kx, scale * b_z)
        total = h + by + bz
        if kind is not None:
            bx = keep(bits, yz_bit(0, 0), 1 - kx, scale * (txm if kind == "lo" else txp))
            total = total + bx
        inv = 1.0 / total
        h1[e] = h * inv
        y1[e] = by * inv
        z1[e] = bz * inv
        if kind is not None:
            x1[slot] = bx * inv

    gi = lax.broadcasted_iota(jnp.int32, (nz, nz), 0)
    gc = lax.broadcasted_iota(jnp.int32, (nz, nz), 1)
    nodes_z = nz // BZ
    gk = gi >> 3
    gu = (gi & 7) >= 4
    ck = gc & (nodes_z - 1)
    same_k = gk == ck
    up_k = gu & (gk + 1 == ck)
    dn_k = jnp.logical_not(gu) & (gk - 1 == ck)
    one = lambda c: jnp.where(c, 1.0, 0.0).astype(jnp.bfloat16)
    ga[0:nz, 0:nz] = one(same_k & jnp.logical_not(gu))
    ga[0:nz, nz:] = one(same_k & gu)
    ga[nz:, 0:nz] = one(up_k)
    ga[nz:, nz:] = one(dn_k)
    gb[0:nz, :] = one(same_k)
    gb[nz:, :] = one(up_k | dn_k)
    ek = gc >> 3
    eb = jnp.where((gc & 7) >= 4, ek + 1, ek - 1)
    eb_ok = (eb >= 0) & (eb < nodes_z)
    for j in range(2):
        ge[:, 2 * j * nz : (2 * j + 1) * nz] = one(gi == j * nodes_z + ek)
        ge[:, (2 * j + 1) * nz : (2 * j + 2) * nz] = one((gi == j * nodes_z + eb) & eb_ok)
    pa[...] = jnp.zeros(pa.shape, f32)
    pb[...] = jnp.zeros(pb.shape, f32)

    def exact_dot(a, b):
        a1 = a.astype(jnp.bfloat16)
        r1 = a - a1.astype(f32)
        a2 = r1.astype(jnp.bfloat16)
        a3 = (r1 - a2.astype(f32)).astype(jnp.bfloat16)
        m = a.shape[0]
        out = jnp.dot(jnp.concatenate([a1, a2, a3], axis=0), b, preferred_element_type=f32)
        return (out[2 * m :] + out[m : 2 * m]) + out[:m]

    px = lax.rem(me, 2)

    for c in own:
        c.wait()

    def loop(lo, hi, fn):
        def body(i, _):
            fn(i)
            return 0

        lax.fori_loop(lo, hi, body, 0)

    loop(2, w + 2, prepare)

    def set_face(f):
        tx[f] = face(f)

    loop(2, w + 1, set_face)
    loop(2, w, lambda e: first_sweep(e, None, px, 0))

    pl.semaphore_wait(barrier, n - 1)

    @pl.when(has_hi)
    def _():
        for c in up_copies:
            c.start()

    @pl.when(has_lo)
    def _():
        for c in dn_copies:
            c.start()

    def second_sweep(e, kind):
        t_y, t_z, scale, bits = ty[e], tz[e], wd[e], bits_e[e]
        t_ym, t_zm = yp(t_y), zp(t_z)
        txm, txp = tx[e], tx[e + 1]

        def shifts(v):
            a, b = t_y * yn(v), t_ym * yp(v)
            c, d = t_z * zn(v), t_zm * zp(v)
            yb = jnp.where(y_top, a, jnp.where(y_bot, b, 0.0))
            zb = jnp.where(z_top, c, jnp.where(z_bot, d, 0.0))
            yi = jnp.where(y_top, 0.0, a) + jnp.where(y_bot, 0.0, b)
            zi = jnp.where(z_top, 0.0, c) + jnp.where(z_bot, 0.0, d)
            return yi, yb, zi, zb

        h, y, z = h1[e], y1[e], z1[e]
        h_yi, h_yb, h_zi, h_zb = shifts(h)
        y_yi, y_yb, y_zi, y_zb = shifts(y)
        z_yi, z_yb, z_zi, z_zb = shifts(z)

        pull_h = h_yi + h_zi + y_yb + z_zb
        pull_y = y_yi + y_zi + h_yb
        pull_z = z_yi + z_zi + h_zb
        if kind != 0:
            pull_h = pull_h + txm * h1[e - 1]
            pull_y = pull_y + txm * y1[e - 1]
            pull_z = pull_z + txm * z1[e - 1]
        else:
            pull_h = pull_h + txm * x1[0]
        if kind != w - 1:
            pull_h = pull_h + txp * h1[e + 1]
            pull_y = pull_y + txp * y1[e + 1]
            pull_z = pull_z + txp * z1[e + 1]
        else:
            pull_h = pull_h + txp * x1[3]
        nh = keep(bits, yz_bit(0, 0), px, THIRD * h + scale * pull_h)
        nyy = keep(bits, yz_bit(1, 0), px, THIRD * y + scale * pull_y)
        nzz = keep(bits, yz_bit(0, 1), px, THIRD * z + scale * pull_z)
        nyz = keep(bits, yz_bit(1, 1), px, scale * (y_zb + z_yb))
        total = (nh + nyy) + (nzz + nyz)
        rest = []
        if kind is not None:
            qx = 1 - px
            if kind in (0, w - 1):
                xo = x1[1] if kind == 0 else x1[2]
                t_out = txm if kind == 0 else txp
                other = e - 1 if kind == 0 else e + 1
                x_yi, x_yb, x_zi, x_zb = shifts(xo)
                nx = THIRD * xo + scale * (x_yi + x_zi + t_out * h1[other])
                rest = [
                    keep(bits, yz_bit(0, 0), qx, nx),
                    keep(bits, yz_bit(1, 0), qx, scale * (x_yb + t_out * y1[other])),
                    keep(bits, yz_bit(0, 1), qx, scale * (x_zb + t_out * z1[other])),
                ]
            else:
                nx = scale * (txm * x1[1] if kind == 1 else txp * x1[2])
                rest = [keep(bits, yz_bit(0, 0), qx, nx)]
            for v in rest:
                total = total + v
        inv = 1.0 / total
        fields = [nh * inv, nyy * inv, nzz * inv, nyz * inv]
        rest = [v * inv for v in rest]
        x = e - 1
        h2[x], y2[x], z2[x], yz2[x] = fields
        b_y = jnp.where(y_top, t_y, jnp.where(y_bot, t_ym, 0.0))
        b_z = jnp.where(z_top, t_z, jnp.where(z_bot, t_zm, 0.0))
        share = 0.02 * por_e[e] + b_y + b_z
        if kind == 0:
            share = share + txm
        if kind == w - 1:
            share = share + txp
        return fields, rest, share, b_y, b_z

    def parts(fields, share, b_y, b_z):
        h, y, z, yz = fields
        own_row = [share * v if v is not None else None for v in fields]
        y_face = [b_y * v if v is not None else None for v in fields]
        z_face = [b_z * v if v is not None else None for v in fields]
        return own_row + y_face + z_face

    def inner_plane(e, acc):
        fields, _, share, b_y, b_z = second_sweep(e, None)
        new = parts(fields, share, b_y, b_z) + [src[e - 1]]
        return tuple(a + b for a, b in zip(acc, new))

    acc = lax.fori_loop(3, w - 1, inner_plane, tuple(zero for _ in range(13)))

    @pl.when(has_lo)
    def _():
        for c in up_copies:
            c.wait_recv()

    @pl.when(has_hi)
    def _():
        for c in dn_copies:
            c.wait_recv()

    for i in (0, 1, w + 2, w + 3):
        prepare(i)
    for f in (0, 1, w + 1, w + 2):
        t = face(f)
        if f == 1:
            t = jnp.where(has_lo, t, 0.0)
        if f == w + 1:
            t = jnp.where(has_hi, t, 0.0)
        tx[f] = t
    first_sweep(0, "hi", 1 - px, 0)
    first_sweep(1, "lo", px, 1)
    first_sweep(w, "hi", px, 2)
    first_sweep(w + 1, "lo", 1 - px, 3)

    acc = list(acc)
    cross = {}
    sides = {}
    for kind in (0, 1, w - 2, w - 1):
        fields, rest, share, b_y, b_z = second_sweep(kind + 1, kind)
        new = parts(fields, share, b_y, b_z) + [src[kind]]
        acc = [a + b for a, b in zip(acc, new)]
        if kind in (0, w - 1):
            k = 0 if kind == 0 else 1
            for j, v in enumerate(fields + rest):
                edge[k, j] = v
            t_out = tx[1] if kind == 0 else tx[w + 1]
            cross[k] = [t_out * v for v in fields], [t_out * v for v in rest]
        else:
            k = 0 if kind == 1 else 1
            x2[k] = rest[0]
        padded = rest + [None] * (4 - len(rest))
        more = parts(padded, share, b_y, b_z)
        if k in sides:
            sides[k] = [
                b if a is None else (a if b is None else a + b) for a, b in zip(sides[k], more)
            ]
        else:
            sides[k] = more

    def halves(v):
        return [jnp.sum(v[j * BY : (j + 1) * BY], axis=0, keepdims=True) for j in range(ny // BY)]

    def put(index, slot, value, group=0):
        for j, r in enumerate(value):
            ref, col = ((pb, 0), (pa, 0), (pa, nz), (pb, nz))[index % 4]
            at = 16 * group + 8 * (index // 4) + 2 * slot + j
            ref[at : at + 1, col : col + nz] = r

    def add(a, b, sign, swap):
        if b is None:
            return a
        hb = halves(b)
        if swap:
            hb = [hb[1], hb[0]]
        if a is None:
            return [sign * v for v in hb]
        return [u + sign * v for u, v in zip(a, hb)]

    def fill_slot(slot, sums):
        o, yf, zf = sums[0:4], sums[4:8], sums[8:12]
        same0 = add(add(None, o[0], 1.0, False), yf[1], -1.0, True)
        same1 = add(add(None, o[2], 1.0, False), yf[3], -1.0, True)
        oth0 = add(add(None, o[1], 1.0, False), yf[0], -1.0, True)
        oth1 = add(add(None, o[3], 1.0, False), yf[2], -1.0, True)
        for index, v in ((0, same0), (1, same1), (4, oth0), (5, oth1)):
            if v is not None:
                put(index, slot, v)
        for index, v in ((2, zf[0]), (3, zf[2]), (6, zf[1]), (7, zf[3])):
            if v is not None:
                put(index, slot, [-u for u in halves(v)])

    fill_slot(1, acc[0:12])
    fill_slot(0, sides[0])
    fill_slot(2, sides[1])
    put(0, 3, halves(acc[12]))

    sub8 = lax.broadcasted_iota(jnp.int32, (8, nz), 0)
    lane8 = lax.broadcasted_iota(jnp.int32, (8, nz), 1)
    pick = sub8 == (lane8 >> 4)

    def fill_cross(slot, values):
        for index, v in zip((0, 4, 1, 5), values):
            put(index, slot, [-u for u in halves(v)], 1)

    fill_cross(2, cross[0][0])
    fill_cross(1, cross[0][1])
    fill_cross(0, cross[1][0])
    fill_cross(3, cross[1][1])
    out_a = exact_dot(pa[...], ga[...])
    out_b = exact_dot(pb[...], gb[...])
    for group in range(2):
        for yo in range(2):
            at = 16 * group + 8 * yo
            three = (out_a[at : at + 8, 0:nz], out_b[at : at + 8], out_a[at : at + 8, nz:])
            for z, v in enumerate(three):
                r = 6 * group + 3 * yo + z
                gsend[r : r + 1, :] = jnp.sum(jnp.where(pick, v, 0.0), axis=0, keepdims=True)

    def gather(d):
        to = lax.rem(me + d, n)
        return pltpu.make_async_remote_copy(
            src_ref=gsend.at[pl.ds(0, ROWS)],
            dst_ref=gbuf.at[pl.ds(pl.multiple_of(me * 16, 16), ROWS)],
            send_sem=g_send.at[d],
            recv_sem=g_recv.at[me],
            device_id={"gx": to},
        )

    def gather_from(d):
        frm = lax.rem(me + n - d, n)
        return pltpu.make_async_remote_copy(
            src_ref=gsend.at[pl.ds(0, ROWS)],
            dst_ref=gbuf.at[pl.ds(pl.multiple_of(frm * 16, 16), ROWS)],
            send_sem=g_send.at[d],
            recv_sem=g_recv.at[frm],
            device_id={"gx": frm},
        )

    for d in range(1, n):
        gather(d).start()
    gbuf[pl.ds(pl.multiple_of(me * 16, 16), ROWS), :] = gsend[0:ROWS, :]

    up_edge = pltpu.make_async_remote_copy(
        src_ref=edge.at[1], dst_ref=halo.at[0], send_sem=es_send.at[0], recv_sem=es_recv.at[0],
        device_id={"gx": lax.rem(me + 1, n)},
    )
    dn_edge = pltpu.make_async_remote_copy(
        src_ref=edge.at[0], dst_ref=halo.at[1], send_sem=es_send.at[1], recv_sem=es_recv.at[1],
        device_id={"gx": lax.rem(me + n - 1, n)},
    )

    @pl.when(has_hi)
    def _():
        up_edge.start()

    @pl.when(has_lo)
    def _():
        dn_edge.start()

    for d in range(1, n):
        gather_from(d).wait_recv()

    lane_n = lax.broadcasted_iota(jnp.int32, (n, nz), 1)
    sub_n = lax.broadcasted_iota(jnp.int32, (n, nz), 0)
    slot = lane_n >> 5

    def rolls(v, s, axis):
        return pltpu.roll(v, s % v.shape[axis], axis)

    def every(v):
        v = v + rolls(v, 32, 1)
        return v + rolls(v, 64, 1)

    mats = []
    rhs = None
    for r in range(6):
        o = gbuf[pl.ds(r, n, stride=16), :]
        b = gbuf[pl.ds(6 + r, n, stride=16), :]
        if r == 1:
            rhs = every(jnp.where(slot == 3, o, 0.0))
        left = rolls(b, -1, 0)
        right = rolls(b, 1, 0)
        moved = rolls(right, 64, 1)
        m = jnp.where(slot == 3, 0.0, o)
        m = m + jnp.where((slot == 1) | (slot == 2), left, 0.0)
        m = m + jnp.where(slot == 0, right, 0.0) + jnp.where(slot == 1, moved, 0.0)
        mats.append(m)
    weight = every(sum(jnp.abs(m) for m in mats))
    inv_weight = 1.0 / weight

    def apply_op(v):
        a = jnp.where(slot == 0, rolls(v, 1, 0), jnp.where(slot == 2, rolls(v, -1, 0), v))
        b = jnp.where((lane_n & 16) == 0, rolls(a, -16, 1), rolls(a, 16, 1))
        total = mats[1] * a + mats[4] * b
        total = total + mats[0] * rolls(a, 1, 1) + mats[2] * rolls(a, -1, 1)
        total = total + mats[3] * rolls(b, 1, 1) + mats[5] * rolls(b, -1, 1)
        return every(total)

    def mean_square(v):
        s = jnp.sum(jnp.sum(v * v, axis=0, keepdims=True), axis=1, keepdims=True)
        return s / (4.0 * (n * 32))

    first = apply_op(rhs) * inv_weight
    second = apply_op(first) * inv_weight
    spectral = jnp.sqrt(mean_square(second) / (mean_square(first) + 1e-6))
    upper = 1.25 * spectral
    lower = 0.1 * upper
    centre = 0.5 * (upper + lower)
    half = 0.5 * (upper - lower)
    ratio = centre / half
    damping = 1.0 / ratio
    residual = rhs
    update = residual * inv_weight / centre
    sol = jnp.zeros_like(rhs)
    for sweep in range(CHEBY):
        sol = sol + update
        if sweep + 1 < CHEBY:
            residual = residual - apply_op(update)
            following = 1.0 / (2.0 * ratio - damping)
            update = following * damping * update + 2.0 * following / half * residual * inv_weight
            damping = following

    def sol_row(x):
        return jnp.sum(jnp.where(sub_n == x, sol, 0.0), axis=0, keepdims=True)

    rows3 = jnp.where(
        sub8 == 0,
        sol_row(me - 1),
        jnp.where(sub8 == 1, sol_row(me), jnp.where(sub8 == 2, sol_row(me + 1), 0.0)),
    )
    spread_out = exact_dot(rows3, ge[...])
    maps = {
        (j, k): spread_out[:, (2 * j + k) * nz : (2 * j + k + 1) * nz]
        for j in range(2)
        for k in range(2)
    }
    for x in range(3):
        for jz in range(2):
            a, b = maps[0, jz][x : x + 1], maps[1, jz][x : x + 1]
            sbuf[x, 2 * jz] = jnp.where(row < BY, a, b)
            sbuf[x, 2 * jz + 1] = jnp.where(row < BY, b, a)

    def base_pressure(h, y, z, yz, node):
        return (
            h * sbuf[node, 0] + y * sbuf[node, 1] + z * sbuf[node, 2] + yz * sbuf[node, 3]
        )

    def plane_pressure(x):
        p = base_pressure(h2[x], y2[x], z2[x], yz2[x], 1)
        p_e[x + 1] = p
        pres[x] = p

    loop(2, w - 2, plane_pressure)

    @pl.when(has_lo)
    def _():
        up_edge.wait_recv()

    @pl.when(has_hi)
    def _():
        dn_edge.wait_recv()

    def edge_pressure(ref, k, home, beside):
        p = base_pressure(ref[k, 0], ref[k, 1], ref[k, 2], ref[k, 3], home)
        return p + ref[k, 4] * sbuf[beside, 0] + ref[k, 5] * sbuf[beside, 1] + ref[k, 6] * sbuf[
            beside, 2
        ]

    for x, k, beside in ((0, 0, 0), (w - 1, 1, 2)):
        p = edge_pressure(edge, k, 1, beside)
        p_e[x + 1] = p
        pres[x] = p
    for x, k, beside in ((1, 0, 0), (w - 2, 1, 2)):
        p = base_pressure(h2[x], y2[x], z2[x], yz2[x], 1) + x2[k] * sbuf[beside, 0]
        p_e[x + 1] = p
        pres[x] = p
    p_e[0] = edge_pressure(halo, 0, 0, 1)
    p_e[w + 1] = edge_pressure(halo, 1, 2, 1)

    def flow(t, p, pn, f, fn):
        v = t * (p - pn)
        return v, jnp.where(v > 0, f, fn) * v

    def transport(x, carry):
        vx, wx, top = carry
        e, i = x + 1, x + 2
        p, f = p_e[e], f_e[i]
        vn, wn = flow(tx[e + 1], p, p_e[e + 1], f, f_e[i + 1])
        vy, wy = flow(ty[e], p, yn(p), f, yn(f))
        vz, wz = flow(tz[e], p, zn(p), f, zn(f))
        net = (wn - wx) + (wy - yp(wy)) + (wz - zp(wz))
        s = src[x]
        leaving = jnp.maximum(vn, 0.0) + jnp.maximum(-vx, 0.0)
        leaving = leaving + jnp.maximum(vy, 0.0) + jnp.maximum(-yp(vy), 0.0)
        leaving = leaving + jnp.maximum(vz, 0.0) + jnp.maximum(-zp(vz), 0.0)
        leaving = leaving + jnp.maximum(-s, 0.0)
        gain = jnp.maximum(s, 0.0) + jnp.minimum(s, 0.0) * f - net
        inv = 1.0 / por_e[e]
        new_sat[x] = gain * inv
        return vn, wn, jnp.maximum(top, leaving * inv)

    v0, w0 = flow(tx[1], p_e[0], p_e[1], f_e[1], f_e[2])
    _, _, top = lax.fori_loop(0, w, transport, (v0, w0, zero))
    top = jnp.max(jnp.max(top, axis=0, keepdims=True), axis=1, keepdims=True)
    msend[...] = jnp.broadcast_to(top, (1, nz))

    def spread(d):
        return pltpu.make_async_remote_copy(
            src_ref=msend,
            dst_ref=mbuf.at[me],
            send_sem=m_send.at[d],
            recv_sem=m_recv.at[me],
            device_id={"gx": lax.rem(me + d, n)},
        )

    def spread_from(d):
        frm = lax.rem(me + n - d, n)
        return pltpu.make_async_remote_copy(
            src_ref=msend,
            dst_ref=mbuf.at[frm],
            send_sem=m_send.at[d],
            recv_sem=m_recv.at[frm],
            device_id={"gx": frm},
        )

    for d in range(1, n):
        spread(d).start()
    mbuf[me] = msend[...]
    for d in range(1, n):
        spread_from(d).wait_recv()
    best = mbuf[0]
    for k in range(1, n):
        best = jnp.maximum(best, mbuf[k])
    step = 0.5 / best

    def finish(x):
        new_sat[x] = sat_e[x + 2] + step * new_sat[x]

    loop(0, w, finish)

    @pl.when(has_hi)
    def _():
        for c in up_copies:
            c.wait_send()
        up_edge.wait_send()

    @pl.when(has_lo)
    def _():
        for c in dn_copies:
            c.wait_send()
        dn_edge.wait_send()

    for d in range(1, n):
        gather(d).wait_send()
        spread(d).wait_send()


def copy_kernel(a, b, out_a, out_b, sem):
    copies = [
        pltpu.make_async_copy(a, out_a, sem.at[0]),
        pltpu.make_async_copy(b, out_b, sem.at[1]),
    ]
    for c in copies:
        c.start()
    for c in copies:
        c.wait()


def write_out(a, b):
    shape = jax.ShapeDtypeStruct(a.shape, a.dtype)
    return pl.pallas_call(
        copy_kernel,
        name="write_out",
        out_shape=(shape, shape),
        in_specs=[pl.BlockSpec(memory_space=pltpu.VMEM)] * 2,
        out_specs=(pl.BlockSpec(memory_space=pltpu.HBM),) * 2,
        scratch_shapes=[pltpu.SemaphoreType.DMA((2,))],
        compiler_params=pltpu.CompilerParams(vmem_limit_bytes=4 * 1024 * 1024),
    )(a, b)


def solution(mesh):
    n = mesh.shape["gx"]

    def on_device(log_perm, saturation, porosity, source, support_bits):
        w, ny, nz = log_perm.shape
        plane = (ny, nz)
        f32 = jnp.float32

        def v(*lead):
            return pltpu.VMEM(lead + plane, f32)

        dma = lambda k: pltpu.SemaphoreType.DMA((k,))
        out = jax.ShapeDtypeStruct(log_perm.shape, f32)
        pinned = [
            pltpu.with_memory_space_constraint(a, pltpu.HBM)
            for a in (log_perm, saturation, porosity, source, support_bits)
        ]
        results = pl.pallas_call(
            lambda *refs: kernel(n, *refs),
            name="multiscale_step",
            out_shape=(out, out),
            in_specs=[pl.BlockSpec(memory_space=pltpu.HBM)] * 5,
            out_specs=(pl.BlockSpec(memory_space=pltpu.VMEM),) * 2,
            scratch_shapes=[
                v(w + 4), v(w + 4), v(w + 2), pltpu.VMEM((w + 2,) + plane, jnp.int32), v(w),
                v(w + 4), v(w + 4), v(w + 4), v(w + 3), v(w + 2), v(w + 2), v(w + 2),
                v(w + 2), v(w + 2), v(w + 2), v(4), v(w), v(w), v(w), v(w), v(2), v(2, 7), v(2, 7),
                pltpu.VMEM((32, 2 * nz), f32), pltpu.VMEM((32, 2 * nz), f32),
                pltpu.VMEM((2 * nz, 2 * nz), jnp.bfloat16), pltpu.VMEM((2 * nz, nz), jnp.bfloat16),
                pltpu.VMEM((nz, 4 * nz), jnp.bfloat16), pltpu.VMEM((16, nz), f32),
                pltpu.VMEM((16 * n, nz), f32), v(3, 4), v(w + 2),
                pltpu.VMEM((1, nz), f32), pltpu.VMEM((n, 1, nz), f32),
                dma(5), dma(8), dma(8), dma(2), dma(2), dma(n), dma(n), dma(n), dma(n),
            ],
            compiler_params=pltpu.CompilerParams(
                collective_id=0, has_side_effects=True, vmem_limit_bytes=33554432
            ),
        )(*pinned)
        return write_out(*results)

    spec = P(("groups", "gx"), None, None)
    return jax.shard_map(
        on_device, mesh=mesh, in_specs=(spec,) * 5, out_specs=(spec, spec), check_vma=False
    )
```

```python
import jax
import jax.numpy as jnp
from jax import lax
from jax.experimental import pallas as pl
from jax.experimental.pallas import tpu as pltpu
from jax.sharding import PartitionSpec as P

BX = 16
BY = 16
BZ = 8
CHEBY = 4
THIRD = 1.0 / 3.0
RELAX = 2.0 / 3.0
ROWS = 12
EDGE = (0, 128, 32, 144, 64, 160, 96)


def kernel(
    n, lp_h, sat_h, por_h, src_h, bits_h, pres, new_sat,
    lp_e, sat_e, por_e, bits_e, src, q_e, m_e, f_e, tx, ty, tz, wd,
    h1, y1, z1, x1, h2, y2, z2, yz2, x2, edge, halo, pa, pb, ga, gb, ge, gsend, gbuf, sbuf, p_e,
    msend, mbuf, lsem, hs_send, hs_recv, es_send, es_recv, g_send, g_recv, m_send, m_recv,
):
    f32 = jnp.float32
    me = lax.axis_index("gx")
    w = lp_h.shape[0]
    ny, nz = lp_h.shape[1], lp_h.shape[2]
    has_lo = me > 0

    def wrap(t):
        return jnp.where(t >= n, t - n, t)

    has_hi = me < n - 1

    barrier = pltpu.get_barrier_semaphore()
    for d in range(1, n):
        pl.semaphore_signal(barrier, inc=1, device_id={"gx": wrap(me + d)})

    own = [
        pltpu.make_async_copy(lp_h, lp_e.at[pl.ds(2, w)], lsem.at[0]),
        pltpu.make_async_copy(sat_h, sat_e.at[pl.ds(2, w)], lsem.at[1]),
        pltpu.make_async_copy(por_h, por_e.at[pl.ds(1, w)], lsem.at[2]),
        pltpu.make_async_copy(bits_h, bits_e.at[pl.ds(1, w)], lsem.at[3]),
        pltpu.make_async_copy(src_h, src, lsem.at[4]),
    ]
    for c in own:
        c.start()

    def halo_copies(up):
        base = 0 if up else 4
        to = wrap(me + (1 if up else n - 1))
        out = []
        for k, (a, b, width) in enumerate(
            ((lp_h, lp_e, 2), (sat_h, sat_e, 2), (por_h, por_e, 1), (bits_h, bits_e, 1))
        ):
            s0 = w - width if up else 0
            d0 = 0 if up else w + width
            out.append(
                pltpu.make_async_remote_copy(
                    src_ref=a.at[pl.ds(s0, width)],
                    dst_ref=b.at[pl.ds(d0, width)],
                    send_sem=hs_send.at[base + k],
                    recv_sem=hs_recv.at[base + k],
                    device_id={"gx": to},
                )
            )
        return out

    up_copies = halo_copies(True)
    dn_copies = halo_copies(False)

    def fill(lo):
        e2 = pl.ds(0 if lo else w + 2, 2)
        e1 = pl.ds(0 if lo else w + 1, 1)
        lp_e[e2] = jnp.zeros((2, ny, nz), f32)
        sat_e[e2] = jnp.full((2, ny, nz), 0.5, f32)
        por_e[e1] = jnp.full((1, ny, nz), 0.2, f32)
        bits_e[e1] = jnp.full((1, ny, nz), 255, jnp.int32)
        halo[0 if lo else 1] = jnp.zeros((176, nz), f32)

    @pl.when(jnp.logical_not(has_lo))
    def _():
        fill(True)

    @pl.when(jnp.logical_not(has_hi))
    def _():
        fill(False)

    row = lax.broadcasted_iota(jnp.int32, (ny, nz), 0)
    lane = lax.broadcasted_iota(jnp.int32, (ny, nz), 1)
    y_top = (row & (BY - 1)) == BY - 1
    y_bot = (row & (BY - 1)) == 0
    z_top = (lane & (BZ - 1)) == BZ - 1
    z_bot = (lane & (BZ - 1)) == 0
    py = (row >> 4) & 1
    pz = (lane >> 3) & 1

    def yz_bit(jy, jz):
        return jnp.left_shift(jnp.int32(1), 2 * (py ^ jy) + 4 * (pz ^ jz))

    zero = jnp.zeros((ny, nz), f32)
    lo_r, hi_r = BY - 8, BY + 8
    row_r = lax.broadcasted_iota(jnp.int32, (16, nz), 0)
    lane_r = lax.broadcasted_iota(jnp.int32, (16, nz), 1)
    y_top_r = row_r == 7
    y_bot_r = row_r == 8
    z_top_r = (lane_r & (BZ - 1)) == BZ - 1
    z_bot_r = (lane_r & (BZ - 1)) == 0
    py_r = row_r >> 3
    pz_r = (lane_r >> 3) & 1

    def yz_bit_r(jy, jz):
        return jnp.left_shift(jnp.int32(1), 2 * (py_r ^ jy) + 4 * (pz_r ^ jz))

    def near(v):
        return v[lo_r:hi_r]

    def patch(v, part):
        return jnp.concatenate([v[:lo_r], part, v[hi_r:]], axis=0)

    def fold(v):
        return jnp.concatenate([v[0:8] + v[8:16], v[16:24] + v[24:32]], axis=0)

    def keep(bits, bit_yz, kx, value):
        return jnp.where((bits & (bit_yz * (1 + kx))) != 0, value, 0.0)

    def yn(v):
        return pltpu.roll(v, v.shape[0] - 1, 0)

    def yp(v):
        return pltpu.roll(v, 1, 0)

    def zn(v):
        return pltpu.roll(v, nz - 1, 1)

    def zp(v):
        return pltpu.roll(v, 1, 1)

    def prepare(i):
        q_e[i] = jnp.exp(-lp_e[i])
        s = sat_e[i]
        r = 1.0 - s
        m = s * s + 0.25 * (r * r)
        m_e[i] = m
        f_e[i] = s * s / m

    def face(f):
        return (m_e[f] + m_e[f + 1]) / (q_e[f] + q_e[f + 1])

    def first_sweep(e, kind, kx, slot):
        q = q_e[e + 1]
        m = m_e[e + 1]
        t_y = jnp.where(row < ny - 1, (m + yn(m)) / (q + yn(q)), 0.0)
        t_z = jnp.where(lane < nz - 1, (m + zn(m)) / (q + zn(q)), 0.0)
        ty[e] = t_y
        tz[e] = t_z
        t_ym = yp(t_y)
        t_zm = zp(t_z)
        txm, txp = tx[e], tx[e + 1]
        bits = bits_e[e]
        b_y = jnp.where(y_top_r, near(t_y), jnp.where(y_bot_r, near(t_ym), 0.0))
        b_z = jnp.where(z_top, t_z, jnp.where(z_bot, t_zm, 0.0))
        all_y, all_z = t_y + t_ym, t_z + t_zm
        inner = patch(all_y, near(all_y) - b_y) + (all_z - b_z)
        diag = 0.02 * por_e[e] + txm + txp + all_y + all_z
        scale = RELAX / diag
        wd[e] = scale
        if kind is None:
            inner = inner + txm + txp
        elif kind == "lo":
            inner = inner + txp
        else:
            inner = inner + txm
        h = keep(bits, yz_bit(0, 0), kx, THIRD + scale * inner)
        by = keep(near(bits), yz_bit_r(1, 0), kx, near(scale) * b_y)
        bz = keep(bits, yz_bit(0, 1), kx, scale * b_z)
        total = h + bz
        total = patch(total, near(total) + by)
        if kind is not None:
            bx = keep(bits, yz_bit(0, 0), 1 - kx, scale * (txm if kind == "lo" else txp))
            total = total + bx
        inv = 1.0 / total
        h1[e] = h * inv
        y1[e] = by * near(inv)
        z1[e] = bz * inv
        if kind is not None:
            x1[slot] = bx * inv

    gi = lax.broadcasted_iota(jnp.int32, (nz, nz), 0)
    gc = lax.broadcasted_iota(jnp.int32, (nz, nz), 1)
    nodes_z = nz // BZ
    gk = gi >> 3
    gu = (gi & 7) >= 4
    ck = gc & (nodes_z - 1)
    same_k = gk == ck
    up_k = gu & (gk + 1 == ck)
    dn_k = jnp.logical_not(gu) & (gk - 1 == ck)
    one = lambda c: jnp.where(c, 1.0, 0.0).astype(jnp.bfloat16)
    ga[0:nz, 0:nz] = one(same_k & jnp.logical_not(gu))
    ga[0:nz, nz:] = one(same_k & gu)
    ga[nz:, 0:nz] = one(up_k)
    ga[nz:, nz:] = one(dn_k)
    gb[0:nz, :] = one(same_k)
    gb[nz:, :] = one(up_k | dn_k)
    ek = gc >> 3
    eb = jnp.where((gc & 7) >= 4, ek + 1, ek - 1)
    eb_ok = (eb >= 0) & (eb < nodes_z)
    for j in range(2):
        ge[:, 2 * j * nz : (2 * j + 1) * nz] = one(gi == j * nodes_z + ek)
        ge[:, (2 * j + 1) * nz : (2 * j + 2) * nz] = one((gi == j * nodes_z + eb) & eb_ok)
    pa[...] = jnp.zeros(pa.shape, f32)
    pb[...] = jnp.zeros(pb.shape, f32)

    def exact_dot(a, b):
        a1 = a.astype(jnp.bfloat16)
        r1 = a - a1.astype(f32)
        a2 = r1.astype(jnp.bfloat16)
        a3 = (r1 - a2.astype(f32)).astype(jnp.bfloat16)
        m = a.shape[0]
        out = jnp.dot(jnp.concatenate([a1, a2, a3], axis=0), b, preferred_element_type=f32)
        return (out[2 * m :] + out[m : 2 * m]) + out[:m]

    px = lax.rem(me, 2)

    for c in own:
        c.wait()

    def loop(lo, hi, fn):
        def body(i, _):
            fn(i)
            return 0

        lax.fori_loop(lo, hi, body, 0)

    loop(2, w + 2, prepare)

    def set_face(f):
        tx[f] = face(f)

    loop(2, w + 1, set_face)
    pl.semaphore_wait(barrier, n - 1)

    @pl.when(has_hi)
    def _():
        for c in up_copies:
            c.start()

    @pl.when(has_lo)
    def _():
        for c in dn_copies:
            c.start()

    loop(2, w, lambda e: first_sweep(e, None, px, 0))

    def second_sweep(e, kind):
        t_y, t_z, scale, bits = ty[e], tz[e], wd[e], bits_e[e]
        t_ym, t_zm = yp(t_y), zp(t_z)
        txm, txp = tx[e], tx[e + 1]

        t_yr, t_ymr, t_zr, t_zmr = near(t_y), near(t_ym), near(t_z), near(t_zm)
        txmr, txpr, scale_r, bits_r = near(txm), near(txp), near(scale), near(bits)

        def shift_z(v, t, tm, top, bot):
            c, d = t * zn(v), tm * zp(v)
            zb = jnp.where(top, c, jnp.where(bot, d, 0.0))
            return jnp.where(top, d, jnp.where(bot, c, c + d)), zb

        def shift_y(a, b):
            yb = jnp.where(y_top_r, a, jnp.where(y_bot_r, b, 0.0))
            return jnp.where(y_top_r, b, jnp.where(y_bot_r, a, a + b)), yb

        def shifts(v):
            a, b = t_y * yn(v), t_ym * yp(v)
            yi, yb = shift_y(near(a), near(b))
            return (patch(a + b, yi), yb) + shift_z(v, t_z, t_zm, z_top, z_bot)

        def shifts_r(v):
            yi, yb = shift_y(t_yr * yn(v), t_ymr * yp(v))
            return (yi, yb) + shift_z(v, t_zr, t_zmr, z_top_r, z_bot_r)

        h, y, z = h1[e], y1[e], z1[e]
        h_yi, h_yb, h_zi, h_zb = shifts(h)
        y_yi, y_yb, y_zi, y_zb = shifts_r(y)
        z_yi, z_yb, z_zi, z_zb = shifts(z)

        pull_h = h_yi + h_zi + z_zb
        pull_h = patch(pull_h, near(pull_h) + y_yb)
        pull_y = y_yi + y_zi + h_yb
        pull_z = z_yi + z_zi + h_zb
        if kind != 0:
            pull_h = pull_h + txm * h1[e - 1]
            pull_y = pull_y + txmr * y1[e - 1]
            pull_z = pull_z + txm * z1[e - 1]
        else:
            pull_h = pull_h + txm * x1[0]
        if kind != w - 1:
            pull_h = pull_h + txp * h1[e + 1]
            pull_y = pull_y + txpr * y1[e + 1]
            pull_z = pull_z + txp * z1[e + 1]
        else:
            pull_h = pull_h + txp * x1[3]
        nh = keep(bits, yz_bit(0, 0), px, THIRD * h + scale * pull_h)
        nyy = keep(bits_r, yz_bit_r(1, 0), px, THIRD * y + scale_r * pull_y)
        nzz = keep(bits, yz_bit(0, 1), px, THIRD * z + scale * pull_z)
        nyz = keep(bits_r, yz_bit_r(1, 1), px, scale_r * (y_zb + z_yb))
        total = nh + nzz
        part = nyy + nyz
        rest = []
        if kind is not None:
            qx = 1 - px
            if kind in (0, w - 1):
                xo = x1[1] if kind == 0 else x1[2]
                t_out = txm if kind == 0 else txp
                other = e - 1 if kind == 0 else e + 1
                x_yi, x_yb, x_zi, x_zb = shifts(xo)
                nx = THIRD * xo + scale * (x_yi + x_zi + t_out * h1[other])
                nxy = scale_r * (x_yb + near(t_out) * y1[other])
                rest = [
                    keep(bits, yz_bit(0, 0), qx, nx),
                    keep(bits_r, yz_bit_r(1, 0), qx, nxy),
                    keep(bits, yz_bit(0, 1), qx, scale * (x_zb + t_out * z1[other])),
                ]
                total = total + rest[0] + rest[2]
                part = part + rest[1]
            else:
                nx = scale * (txm * x1[1] if kind == 1 else txp * x1[2])
                rest = [keep(bits, yz_bit(0, 0), qx, nx)]
                total = total + rest[0]
        inv = 1.0 / patch(total, near(total) + part)
        inv_r = near(inv)
        fields = [nh * inv, nyy * inv_r, nzz * inv, nyz * inv_r]
        rest = [v * (inv_r if j == 1 else inv) for j, v in enumerate(rest)]
        x = e - 1
        h2[x], y2[x], z2[x], yz2[x] = fields
        b_y = jnp.where(y_top_r, t_yr, jnp.where(y_bot_r, t_ymr, 0.0))
        b_z = jnp.where(z_top, t_z, jnp.where(z_bot, t_zm, 0.0))
        share = 0.02 * por_e[e] + b_z
        share = patch(share, near(share) + b_y)
        if kind == 0:
            share = share + txm
        if kind == w - 1:
            share = share + txp
        return fields, rest, share, b_y, b_z

    def times(coef, fields):
        return [
            None if v is None else (near(coef) * v if j % 2 else fold(coef * v))
            for j, v in enumerate(fields)
        ]

    def parts(fields, share, b_y, b_z):
        y_face = [
            None if v is None else b_y * (v if j % 2 else near(v)) for j, v in enumerate(fields)
        ]
        return times(share, fields) + y_face + times(b_z, fields)

    def inner_plane(e, acc):
        fields, _, share, b_y, b_z = second_sweep(e, None)
        new = parts(fields, share, b_y, b_z) + [fold(src[e - 1])]
        return tuple(a + b for a, b in zip(acc, new))

    acc = lax.fori_loop(3, w - 1, inner_plane, (jnp.zeros((16, nz), f32),) * 13)

    @pl.when(has_lo)
    def _():
        for c in up_copies:
            c.wait_recv()

    @pl.when(has_hi)
    def _():
        for c in dn_copies:
            c.wait_recv()

    for i in (0, 1, w + 2, w + 3):
        prepare(i)
    for f in (0, 1, w + 1, w + 2):
        t = face(f)
        if f == 1:
            t = jnp.where(has_lo, t, 0.0)
        if f == w + 1:
            t = jnp.where(has_hi, t, 0.0)
        tx[f] = t
    first_sweep(0, "hi", 1 - px, 0)
    first_sweep(1, "lo", px, 1)
    first_sweep(w, "hi", px, 2)
    first_sweep(w + 1, "lo", 1 - px, 3)

    acc = list(acc)
    cross = {}
    sides = {}
    for kind in (0, 1, w - 2, w - 1):
        fields, rest, share, b_y, b_z = second_sweep(kind + 1, kind)
        new = parts(fields, share, b_y, b_z) + [fold(src[kind])]
        acc = [a + b for a, b in zip(acc, new)]
        if kind in (0, w - 1):
            k = 0 if kind == 0 else 1
            both = fields + rest
            for j in range(7):
                edge[k, EDGE[j] : EDGE[j] + both[j].shape[0], :] = both[j]
            t_out = tx[1] if kind == 0 else tx[w + 1]
            cross[k] = times(t_out, fields), times(t_out, rest)
        else:
            k = 0 if kind == 1 else 1
            x2[k] = rest[0]
        padded = rest + [None] * (4 - len(rest))
        more = parts(padded, share, b_y, b_z)
        if k in sides:
            sides[k] = [
                b if a is None else (a if b is None else a + b) for a, b in zip(sides[k], more)
            ]
        else:
            sides[k] = more

    def halves(v):
        return [jnp.sum(v[8 * j : 8 * j + 8], axis=0, keepdims=True) for j in range(2)]

    def put(index, slot, value, group=0):
        for j, r in enumerate(value):
            ref, col = ((pb, 0), (pa, 0), (pa, nz), (pb, nz))[index % 4]
            at = 16 * group + 8 * (index // 4) + 2 * slot + j
            ref[at : at + 1, col : col + nz] = r

    def add(a, b, sign, swap):
        if b is None:
            return a
        hb = halves(b)
        if swap:
            hb = [hb[1], hb[0]]
        if a is None:
            return [sign * v for v in hb]
        return [u + sign * v for u, v in zip(a, hb)]

    def fill_slot(slot, sums):
        o, yf, zf = sums[0:4], sums[4:8], sums[8:12]
        same0 = add(add(None, o[0], 1.0, False), yf[1], -1.0, True)
        same1 = add(add(None, o[2], 1.0, False), yf[3], -1.0, True)
        oth0 = add(add(None, o[1], 1.0, False), yf[0], -1.0, True)
        oth1 = add(add(None, o[3], 1.0, False), yf[2], -1.0, True)
        for index, v in ((0, same0), (1, same1), (4, oth0), (5, oth1)):
            if v is not None:
                put(index, slot, v)
        for index, v in ((2, zf[0]), (3, zf[2]), (6, zf[1]), (7, zf[3])):
            if v is not None:
                put(index, slot, [-u for u in halves(v)])

    fill_slot(1, acc[0:12])
    fill_slot(0, sides[0])
    fill_slot(2, sides[1])
    put(0, 3, halves(acc[12]))

    sub8 = lax.broadcasted_iota(jnp.int32, (8, nz), 0)
    lane8 = lax.broadcasted_iota(jnp.int32, (8, nz), 1)
    pick = sub8 == (lane8 >> 4)

    def fill_cross(slot, values):
        for index, v in zip((0, 4, 1, 5), values):
            put(index, slot, [-u for u in halves(v)], 1)

    fill_cross(2, cross[0][0])
    fill_cross(1, cross[0][1])
    fill_cross(0, cross[1][0])
    fill_cross(3, cross[1][1])
    out_a = exact_dot(pa[...], ga[...])
    out_b = exact_dot(pb[...], gb[...])
    for group in range(2):
        for yo in range(2):
            at = 16 * group + 8 * yo
            three = (out_a[at : at + 8, 0:nz], out_b[at : at + 8], out_a[at : at + 8, nz:])
            for z, v in enumerate(three):
                r = 6 * group + 3 * yo + z
                gsend[r : r + 1, :] = jnp.sum(jnp.where(pick, v, 0.0), axis=0, keepdims=True)

    def gather(d):
        to = wrap(me + d)
        return pltpu.make_async_remote_copy(
            src_ref=gsend.at[pl.ds(0, ROWS)],
            dst_ref=gbuf.at[pl.ds(pl.multiple_of(me * 16, 16), ROWS)],
            send_sem=g_send.at[d],
            recv_sem=g_recv.at[me],
            device_id={"gx": to},
        )

    def gather_from(d):
        frm = wrap(me + n - d)
        return pltpu.make_async_remote_copy(
            src_ref=gsend.at[pl.ds(0, ROWS)],
            dst_ref=gbuf.at[pl.ds(pl.multiple_of(frm * 16, 16), ROWS)],
            send_sem=g_send.at[d],
            recv_sem=g_recv.at[frm],
            device_id={"gx": frm},
        )

    for d in range(1, n):
        gather(d).start()
    gbuf[pl.ds(pl.multiple_of(me * 16, 16), ROWS), :] = gsend[0:ROWS, :]

    up_edge = pltpu.make_async_remote_copy(
        src_ref=edge.at[1], dst_ref=halo.at[0], send_sem=es_send.at[0], recv_sem=es_recv.at[0],
        device_id={"gx": wrap(me + 1)},
    )
    dn_edge = pltpu.make_async_remote_copy(
        src_ref=edge.at[0], dst_ref=halo.at[1], send_sem=es_send.at[1], recv_sem=es_recv.at[1],
        device_id={"gx": wrap(me + n - 1)},
    )

    @pl.when(has_hi)
    def _():
        up_edge.start()

    @pl.when(has_lo)
    def _():
        dn_edge.start()

    for d in range(1, n):
        gather_from(d).wait_recv()

    lane_n = lax.broadcasted_iota(jnp.int32, (n, nz), 1)
    sub_n = lax.broadcasted_iota(jnp.int32, (n, nz), 0)
    slot = lane_n >> 5

    def rolls(v, s, axis):
        return pltpu.roll(v, s % v.shape[axis], axis)

    def every(v):
        v = v + rolls(v, 32, 1)
        return v + rolls(v, 64, 1)

    mats = []
    rhs = None
    for r in range(6):
        o = gbuf[pl.ds(r, n, stride=16), :]
        b = gbuf[pl.ds(6 + r, n, stride=16), :]
        if r == 1:
            rhs = every(jnp.where(slot == 3, o, 0.0))
        left = rolls(b, -1, 0)
        right = rolls(b, 1, 0)
        moved = rolls(right, 64, 1)
        m = jnp.where(slot == 3, 0.0, o)
        m = m + jnp.where((slot == 1) | (slot == 2), left, 0.0)
        m = m + jnp.where(slot == 0, right, 0.0) + jnp.where(slot == 1, moved, 0.0)
        mats.append(m)
    weight = every(sum(jnp.abs(m) for m in mats))
    inv_weight = 1.0 / weight

    def apply_op(v):
        a = jnp.where(slot == 0, rolls(v, 1, 0), jnp.where(slot == 2, rolls(v, -1, 0), v))
        b = jnp.where((lane_n & 16) == 0, rolls(a, -16, 1), rolls(a, 16, 1))
        total = mats[1] * a + mats[4] * b
        total = total + mats[0] * rolls(a, 1, 1) + mats[2] * rolls(a, -1, 1)
        total = total + mats[3] * rolls(b, 1, 1) + mats[5] * rolls(b, -1, 1)
        return every(total)

    def mean_square(v):
        s = jnp.sum(jnp.sum(v * v, axis=0, keepdims=True), axis=1, keepdims=True)
        return s / (4.0 * (n * 32))

    first = apply_op(rhs) * inv_weight
    second = apply_op(first) * inv_weight
    spectral = jnp.sqrt(mean_square(second) / (mean_square(first) + 1e-6))
    upper = 1.25 * spectral
    lower = 0.1 * upper
    centre = 0.5 * (upper + lower)
    half = 0.5 * (upper - lower)
    ratio = centre / half
    damping = 1.0 / ratio
    residual = rhs
    update = residual * inv_weight / centre
    sol = jnp.zeros_like(rhs)
    for sweep in range(CHEBY):
        sol = sol + update
        if sweep + 1 < CHEBY:
            residual = residual - apply_op(update)
            following = 1.0 / (2.0 * ratio - damping)
            update = following * damping * update + 2.0 * following / half * residual * inv_weight
            damping = following

    def sol_row(x):
        return jnp.sum(jnp.where(sub_n == x, sol, 0.0), axis=0, keepdims=True)

    rows3 = jnp.where(
        sub8 == 0,
        sol_row(me - 1),
        jnp.where(sub8 == 1, sol_row(me), jnp.where(sub8 == 2, sol_row(me + 1), 0.0)),
    )
    spread_out = exact_dot(rows3, ge[...])
    maps = {
        (j, k): spread_out[:, (2 * j + k) * nz : (2 * j + k + 1) * nz]
        for j in range(2)
        for k in range(2)
    }
    for x in range(3):
        for jz in range(2):
            a, b = maps[0, jz][x : x + 1], maps[1, jz][x : x + 1]
            sbuf[x, 2 * jz] = jnp.where(row < BY, a, b)
            sbuf[x, 2 * jz + 1] = jnp.where(row < BY, b, a)

    def base_pressure(h, y, z, yz, node):
        p = h * sbuf[node, 0] + z * sbuf[node, 2]
        q = y * near(sbuf[node, 1]) + yz * near(sbuf[node, 3])
        return patch(p, near(p) + q)

    def plane_pressure(x):
        p = base_pressure(h2[x], y2[x], z2[x], yz2[x], 1)
        p_e[x + 1] = p
        pres[x] = p

    loop(2, w - 2, plane_pressure)

    @pl.when(has_lo)
    def _():
        up_edge.wait_recv()

    @pl.when(has_hi)
    def _():
        dn_edge.wait_recv()

    def edge_pressure(ref, k, home, beside):
        v = [ref[k, EDGE[j] : EDGE[j] + (16 if j in (1, 3, 5) else 32), :] for j in range(7)]
        p = base_pressure(v[0], v[1], v[2], v[3], home)
        p = p + v[4] * sbuf[beside, 0] + v[6] * sbuf[beside, 2]
        return patch(p, near(p) + v[5] * near(sbuf[beside, 1]))

    for x, k, beside in ((0, 0, 0), (w - 1, 1, 2)):
        p = edge_pressure(edge, k, 1, beside)
        p_e[x + 1] = p
        pres[x] = p
    for x, k, beside in ((1, 0, 0), (w - 2, 1, 2)):
        p = base_pressure(h2[x], y2[x], z2[x], yz2[x], 1) + x2[k] * sbuf[beside, 0]
        p_e[x + 1] = p
        pres[x] = p
    p_e[0] = edge_pressure(halo, 0, 0, 1)
    p_e[w + 1] = edge_pressure(halo, 1, 2, 1)

    def flow(t, p, pn, f, fn):
        v = t * (p - pn)
        return v, jnp.where(v > 0, f, fn) * v

    def transport(x, carry):
        vx, wx, top = carry
        e, i = x + 1, x + 2
        p, f = p_e[e], f_e[i]
        vn, wn = flow(tx[e + 1], p, p_e[e + 1], f, f_e[i + 1])
        vy, wy = flow(ty[e], p, yn(p), f, yn(f))
        vz, wz = flow(tz[e], p, zn(p), f, zn(f))
        net = (wn - wx) + (wy - yp(wy)) + (wz - zp(wz))
        s = src[x]
        leaving = jnp.maximum(vn, 0.0) + jnp.maximum(-vx, 0.0)
        leaving = leaving + jnp.maximum(vy, 0.0) + jnp.maximum(-yp(vy), 0.0)
        leaving = leaving + jnp.maximum(vz, 0.0) + jnp.maximum(-zp(vz), 0.0)
        leaving = leaving + jnp.maximum(-s, 0.0)
        gain = jnp.maximum(s, 0.0) + jnp.minimum(s, 0.0) * f - net
        inv = 1.0 / por_e[e]
        new_sat[x] = gain * inv
        return vn, wn, jnp.maximum(top, leaving * inv)

    v0, w0 = flow(tx[1], p_e[0], p_e[1], f_e[1], f_e[2])
    _, _, top = lax.fori_loop(0, w, transport, (v0, w0, zero))
    top = jnp.max(jnp.max(top, axis=0, keepdims=True), axis=1, keepdims=True)
    msend[...] = jnp.broadcast_to(top, (1, nz))

    def spread(d):
        return pltpu.make_async_remote_copy(
            src_ref=msend,
            dst_ref=mbuf.at[me],
            send_sem=m_send.at[d],
            recv_sem=m_recv.at[me],
            device_id={"gx": wrap(me + d)},
        )

    def spread_from(d):
        frm = wrap(me + n - d)
        return pltpu.make_async_remote_copy(
            src_ref=msend,
            dst_ref=mbuf.at[frm],
            send_sem=m_send.at[d],
            recv_sem=m_recv.at[frm],
            device_id={"gx": frm},
        )

    for d in range(1, n):
        spread(d).start()
    mbuf[me] = msend[...]
    for d in range(1, n):
        spread_from(d).wait_recv()
    best = mbuf[0]
    for k in range(1, n):
        best = jnp.maximum(best, mbuf[k])
    step = 0.5 / best

    def finish(x):
        new_sat[x] = sat_e[x + 2] + step * new_sat[x]

    loop(0, w, finish)

    @pl.when(has_hi)
    def _():
        for c in up_copies:
            c.wait_send()
        up_edge.wait_send()

    @pl.when(has_lo)
    def _():
        for c in dn_copies:
            c.wait_send()
        dn_edge.wait_send()

    for d in range(1, n):
        gather(d).wait_send()
        spread(d).wait_send()


def copy_kernel(a, b, out_a, out_b, sem):
    copies = [
        pltpu.make_async_copy(a, out_a, sem.at[0]),
        pltpu.make_async_copy(b, out_b, sem.at[1]),
    ]
    for c in copies:
        c.start()
    for c in copies:
        c.wait()


def write_out(a, b):
    shape = jax.ShapeDtypeStruct(a.shape, a.dtype)
    return pl.pallas_call(
        copy_kernel,
        name="write_out",
        out_shape=(shape, shape),
        in_specs=[pl.BlockSpec(memory_space=pltpu.VMEM)] * 2,
        out_specs=(pl.BlockSpec(memory_space=pltpu.HBM),) * 2,
        scratch_shapes=[pltpu.SemaphoreType.DMA((2,))],
        compiler_params=pltpu.CompilerParams(vmem_limit_bytes=4 * 1024 * 1024),
    )(a, b)


def solution(mesh):
    n = mesh.shape["gx"]

    def on_device(log_perm, saturation, porosity, source, support_bits):
        w, ny, nz = log_perm.shape
        plane = (ny, nz)
        f32 = jnp.float32

        def v(*lead):
            return pltpu.VMEM(lead + plane, f32)

        r = lambda k: pltpu.VMEM((k, 16, nz), f32)
        dma = lambda k: pltpu.SemaphoreType.DMA((k,))
        out = jax.ShapeDtypeStruct(log_perm.shape, f32)
        pinned = [
            pltpu.with_memory_space_constraint(a, pltpu.HBM)
            for a in (log_perm, saturation, porosity, source, support_bits)
        ]
        results = pl.pallas_call(
            lambda *refs: kernel(n, *refs),
            name="multiscale_step",
            out_shape=(out, out),
            in_specs=[pl.BlockSpec(memory_space=pltpu.HBM)] * 5,
            out_specs=(pl.BlockSpec(memory_space=pltpu.VMEM),) * 2,
            scratch_shapes=[
                v(w + 4), v(w + 4), v(w + 2), pltpu.VMEM((w + 2,) + plane, jnp.int32), v(w),
                v(w + 4), v(w + 4), v(w + 4), v(w + 3), v(w + 2), v(w + 2), v(w + 2),
                v(w + 2), r(w + 2), v(w + 2), v(4), v(w), r(w), v(w), r(w), v(2),
                pltpu.VMEM((2, 176, nz), f32), pltpu.VMEM((2, 176, nz), f32),
                pltpu.VMEM((32, 2 * nz), f32), pltpu.VMEM((32, 2 * nz), f32),
                pltpu.VMEM((2 * nz, 2 * nz), jnp.bfloat16), pltpu.VMEM((2 * nz, nz), jnp.bfloat16),
                pltpu.VMEM((nz, 4 * nz), jnp.bfloat16), pltpu.VMEM((16, nz), f32),
                pltpu.VMEM((16 * n, nz), f32), v(3, 4), v(w + 2),
                pltpu.VMEM((1, nz), f32), pltpu.VMEM((n, 1, nz), f32),
                dma(5), dma(8), dma(8), dma(2), dma(2), dma(n), dma(n), dma(n), dma(n),
            ],
            compiler_params=pltpu.CompilerParams(
                collective_id=0, has_side_effects=True, vmem_limit_bytes=33554432
            ),
        )(*pinned)
        return write_out(*results)

    spec = P(("groups", "gx"), None, None)
    return jax.shard_map(
        on_device, mesh=mesh, in_specs=(spec,) * 5, out_specs=(spec, spec), check_vma=False
    )
```

```python
import jax
import jax.numpy as jnp
from jax import lax
from jax.experimental import pallas as pl
from jax.experimental.pallas import tpu as pltpu
from jax.sharding import PartitionSpec as P

BX = 16
BY = 16
BZ = 8
CHEBY = 4
THIRD = 1.0 / 3.0
RELAX = 2.0 / 3.0
ROWS = 12
EDGE = (0, 128, 32, 144, 64, 160, 96)


def kernel(
    n, lp_h, sat_h, por_h, src_h, bits_h, pres, new_sat,
    lp_e, sat_e, por_e, bits_e, src, q_e, m_e, f_e, tx, ty, tz, wd,
    h1, y1, z1, x1, h2, y2, z2, yz2, x2, edge, halo, pa, pb, ga, gb, ge, gsend, gbuf, sbuf, p_e,
    msend, mbuf, lsem, hs_send, hs_recv, es_send, es_recv, g_send, g_recv, m_send, m_recv,
):
    f32 = jnp.float32
    me = lax.axis_index("gx")
    w = lp_h.shape[0]
    ny, nz = lp_h.shape[1], lp_h.shape[2]
    has_lo = me > 0

    def wrap(t):
        return jnp.where(t >= n, t - n, t)

    has_hi = me < n - 1

    barrier = pltpu.get_barrier_semaphore()
    for d in range(1, n):
        pl.semaphore_signal(barrier, inc=1, device_id={"gx": wrap(me + d)})

    own = [
        pltpu.make_async_copy(lp_h, lp_e.at[pl.ds(2, w)], lsem.at[0]),
        pltpu.make_async_copy(sat_h, sat_e.at[pl.ds(2, w)], lsem.at[1]),
        pltpu.make_async_copy(por_h, por_e.at[pl.ds(1, w)], lsem.at[2]),
        pltpu.make_async_copy(bits_h, bits_e.at[pl.ds(1, w)], lsem.at[3]),
        pltpu.make_async_copy(src_h, src, lsem.at[4]),
    ]
    for c in own:
        c.start()

    def halo_copies(up):
        base = 0 if up else 4
        to = wrap(me + (1 if up else n - 1))
        out = []
        for k, (a, b, width) in enumerate(
            ((lp_h, lp_e, 2), (sat_h, sat_e, 2), (por_h, por_e, 1), (bits_h, bits_e, 1))
        ):
            s0 = w - width if up else 0
            d0 = 0 if up else w + width
            out.append(
                pltpu.make_async_remote_copy(
                    src_ref=a.at[pl.ds(s0, width)],
                    dst_ref=b.at[pl.ds(d0, width)],
                    send_sem=hs_send.at[base + k],
                    recv_sem=hs_recv.at[base + k],
                    device_id={"gx": to},
                )
            )
        return out

    up_copies = halo_copies(True)
    dn_copies = halo_copies(False)

    def fill(lo):
        e2 = pl.ds(0 if lo else w + 2, 2)
        e1 = pl.ds(0 if lo else w + 1, 1)
        lp_e[e2] = jnp.zeros((2, ny, nz), f32)
        sat_e[e2] = jnp.full((2, ny, nz), 0.5, f32)
        por_e[e1] = jnp.full((1, ny, nz), 0.2, f32)
        bits_e[e1] = jnp.full((1, ny, nz), 255, jnp.int32)
        halo[0 if lo else 1] = jnp.zeros((176, nz), f32)

    @pl.when(jnp.logical_not(has_lo))
    def _():
        fill(True)

    @pl.when(jnp.logical_not(has_hi))
    def _():
        fill(False)

    row = lax.broadcasted_iota(jnp.int32, (ny, nz), 0)
    lane = lax.broadcasted_iota(jnp.int32, (ny, nz), 1)
    y_top = (row & (BY - 1)) == BY - 1
    y_bot = (row & (BY - 1)) == 0
    z_top = (lane & (BZ - 1)) == BZ - 1
    z_bot = (lane & (BZ - 1)) == 0
    py = (row >> 4) & 1
    pz = (lane >> 3) & 1

    def yz_bit(jy, jz):
        return jnp.left_shift(jnp.int32(1), 2 * (py ^ jy) + 4 * (pz ^ jz))

    zero = jnp.zeros((ny, nz), f32)
    lo_r, hi_r = BY - 8, BY + 8
    row_r = lax.broadcasted_iota(jnp.int32, (16, nz), 0)
    lane_r = lax.broadcasted_iota(jnp.int32, (16, nz), 1)
    y_top_r = row_r == 7
    y_bot_r = row_r == 8
    z_top_r = (lane_r & (BZ - 1)) == BZ - 1
    z_bot_r = (lane_r & (BZ - 1)) == 0
    py_r = row_r >> 3
    pz_r = (lane_r >> 3) & 1

    def yz_bit_r(jy, jz):
        return jnp.left_shift(jnp.int32(1), 2 * (py_r ^ jy) + 4 * (pz_r ^ jz))

    def near(v):
        return v[lo_r:hi_r]

    def patch(v, part):
        return jnp.concatenate([v[:lo_r], part, v[hi_r:]], axis=0)

    def fold(v):
        return jnp.concatenate([v[0:8] + v[8:16], v[16:24] + v[24:32]], axis=0)

    def keep(bits, bit_yz, kx, value):
        return jnp.where((bits & (bit_yz * (1 + kx))) != 0, value, 0.0)

    def yn(v):
        return pltpu.roll(v, v.shape[0] - 1, 0)

    def yp(v):
        return pltpu.roll(v, 1, 0)

    def zn(v):
        return pltpu.roll(v, nz - 1, 1)

    def zp(v):
        return pltpu.roll(v, 1, 1)

    def prepare(i):
        q_e[i] = jnp.exp(-lp_e[i])
        s = sat_e[i]
        r = 1.0 - s
        m = s * s + 0.25 * (r * r)
        m_e[i] = m
        f_e[i] = s * s / m

    def face(f):
        return (m_e[f] + m_e[f + 1]) / (q_e[f] + q_e[f + 1])

    def first_sweep(e, kind, kx, slot):
        q = q_e[e + 1]
        m = m_e[e + 1]
        t_y = jnp.where(row < ny - 1, (m + yn(m)) / (q + yn(q)), 0.0)
        t_z = jnp.where(lane < nz - 1, (m + zn(m)) / (q + zn(q)), 0.0)
        ty[e] = t_y
        tz[e] = t_z
        t_ym = yp(t_y)
        t_zm = zp(t_z)
        txm, txp = tx[e], tx[e + 1]
        bits = bits_e[e]
        b_y = jnp.where(y_top_r, near(t_y), jnp.where(y_bot_r, near(t_ym), 0.0))
        b_z = jnp.where(z_top, t_z, jnp.where(z_bot, t_zm, 0.0))
        all_y, all_z = t_y + t_ym, t_z + t_zm
        inner = patch(all_y, near(all_y) - b_y) + (all_z - b_z)
        diag = 0.02 * por_e[e] + txm + txp + all_y + all_z
        scale = RELAX / diag
        wd[e] = scale
        if kind is None:
            inner = inner + txm + txp
        elif kind == "lo":
            inner = inner + txp
        else:
            inner = inner + txm
        h = keep(bits, yz_bit(0, 0), kx, THIRD + scale * inner)
        by = keep(near(bits), yz_bit_r(1, 0), kx, near(scale) * b_y)
        bz = keep(bits, yz_bit(0, 1), kx, scale * b_z)
        total = h + bz
        total = patch(total, near(total) + by)
        if kind is not None:
            bx = keep(bits, yz_bit(0, 0), 1 - kx, scale * (txm if kind == "lo" else txp))
            total = total + bx
        inv = 1.0 / total
        h1[e] = h * inv
        y1[e] = by * near(inv)
        z1[e] = bz * inv
        if kind is not None:
            x1[slot] = bx * inv

    gi = lax.broadcasted_iota(jnp.int32, (nz, nz), 0)
    gc = lax.broadcasted_iota(jnp.int32, (nz, nz), 1)
    nodes_z = nz // BZ
    gk = gi >> 3
    gu = (gi & 7) >= 4
    ck = gc & (nodes_z - 1)
    same_k = gk == ck
    up_k = gu & (gk + 1 == ck)
    dn_k = jnp.logical_not(gu) & (gk - 1 == ck)
    one = lambda c: jnp.where(c, 1.0, 0.0).astype(jnp.bfloat16)
    ga[0:nz, 0:nz] = one(same_k & jnp.logical_not(gu))
    ga[0:nz, nz:] = one(same_k & gu)
    ga[nz:, 0:nz] = one(up_k)
    ga[nz:, nz:] = one(dn_k)
    gb[0:nz, :] = one(same_k)
    gb[nz:, :] = one(up_k | dn_k)
    ek = gc >> 3
    eb = jnp.where((gc & 7) >= 4, ek + 1, ek - 1)
    eb_ok = (eb >= 0) & (eb < nodes_z)
    for j in range(2):
        ge[:, 2 * j * nz : (2 * j + 1) * nz] = one(gi == j * nodes_z + ek)
        ge[:, (2 * j + 1) * nz : (2 * j + 2) * nz] = one((gi == j * nodes_z + eb) & eb_ok)
    pa[...] = jnp.zeros(pa.shape, f32)
    pb[...] = jnp.zeros(pb.shape, f32)

    def exact_dot(a, b):
        a1 = a.astype(jnp.bfloat16)
        r1 = a - a1.astype(f32)
        a2 = r1.astype(jnp.bfloat16)
        a3 = (r1 - a2.astype(f32)).astype(jnp.bfloat16)
        m = a.shape[0]
        out = jnp.dot(jnp.concatenate([a1, a2, a3], axis=0), b, preferred_element_type=f32)
        return (out[2 * m :] + out[m : 2 * m]) + out[:m]

    px = lax.rem(me, 2)

    for c in own:
        c.wait()

    def loop(lo, hi, fn):
        def body(i, _):
            fn(i)
            return 0

        lax.fori_loop(lo, hi, body, 0, unroll=2 if (hi - lo) % 2 == 0 else 1)

    loop(2, w + 2, prepare)

    def set_face(f):
        tx[f] = face(f)

    loop(2, w + 1, set_face)
    pl.semaphore_wait(barrier, n - 1)

    @pl.when(has_hi)
    def _():
        for c in up_copies:
            c.start()

    @pl.when(has_lo)
    def _():
        for c in dn_copies:
            c.start()

    loop(2, w, lambda e: first_sweep(e, None, px, 0))

    def second_sweep(e, kind):
        t_y, t_z, scale, bits = ty[e], tz[e], wd[e], bits_e[e]
        t_ym, t_zm = yp(t_y), zp(t_z)
        txm, txp = tx[e], tx[e + 1]

        t_yr, t_ymr, t_zr, t_zmr = near(t_y), near(t_ym), near(t_z), near(t_zm)
        txmr, txpr, scale_r, bits_r = near(txm), near(txp), near(scale), near(bits)

        def shift_z(v, t, tm, top, bot):
            c, d = t * zn(v), tm * zp(v)
            zb = jnp.where(top, c, jnp.where(bot, d, 0.0))
            return jnp.where(top, d, jnp.where(bot, c, c + d)), zb

        def shift_y(a, b):
            yb = jnp.where(y_top_r, a, jnp.where(y_bot_r, b, 0.0))
            return jnp.where(y_top_r, b, jnp.where(y_bot_r, a, a + b)), yb

        def shifts(v):
            a, b = t_y * yn(v), t_ym * yp(v)
            yi, yb = shift_y(near(a), near(b))
            return (patch(a + b, yi), yb) + shift_z(v, t_z, t_zm, z_top, z_bot)

        def shifts_r(v):
            yi, yb = shift_y(t_yr * yn(v), t_ymr * yp(v))
            return (yi, yb) + shift_z(v, t_zr, t_zmr, z_top_r, z_bot_r)

        h, y, z = h1[e], y1[e], z1[e]
        h_yi, h_yb, h_zi, h_zb = shifts(h)
        y_yi, y_yb, y_zi, y_zb = shifts_r(y)
        z_yi, z_yb, z_zi, z_zb = shifts(z)

        pull_h = h_yi + h_zi + z_zb
        pull_h = patch(pull_h, near(pull_h) + y_yb)
        pull_y = y_yi + y_zi + h_yb
        pull_z = z_yi + z_zi + h_zb
        if kind != 0:
            pull_h = pull_h + txm * h1[e - 1]
            pull_y = pull_y + txmr * y1[e - 1]
            pull_z = pull_z + txm * z1[e - 1]
        else:
            pull_h = pull_h + txm * x1[0]
        if kind != w - 1:
            pull_h = pull_h + txp * h1[e + 1]
            pull_y = pull_y + txpr * y1[e + 1]
            pull_z = pull_z + txp * z1[e + 1]
        else:
            pull_h = pull_h + txp * x1[3]
        nh = keep(bits, yz_bit(0, 0), px, THIRD * h + scale * pull_h)
        nyy = keep(bits_r, yz_bit_r(1, 0), px, THIRD * y + scale_r * pull_y)
        nzz = keep(bits, yz_bit(0, 1), px, THIRD * z + scale * pull_z)
        nyz = keep(bits_r, yz_bit_r(1, 1), px, scale_r * (y_zb + z_yb))
        total = nh + nzz
        part = nyy + nyz
        rest = []
        if kind is not None:
            qx = 1 - px
            if kind in (0, w - 1):
                xo = x1[1] if kind == 0 else x1[2]
                t_out = txm if kind == 0 else txp
                other = e - 1 if kind == 0 else e + 1
                x_yi, x_yb, x_zi, x_zb = shifts(xo)
                nx = THIRD * xo + scale * (x_yi + x_zi + t_out * h1[other])
                nxy = scale_r * (x_yb + near(t_out) * y1[other])
                rest = [
                    keep(bits, yz_bit(0, 0), qx, nx),
                    keep(bits_r, yz_bit_r(1, 0), qx, nxy),
                    keep(bits, yz_bit(0, 1), qx, scale * (x_zb + t_out * z1[other])),
                ]
                total = total + rest[0] + rest[2]
                part = part + rest[1]
            else:
                nx = scale * (txm * x1[1] if kind == 1 else txp * x1[2])
                rest = [keep(bits, yz_bit(0, 0), qx, nx)]
                total = total + rest[0]
        inv = 1.0 / patch(total, near(total) + part)
        inv_r = near(inv)
        fields = [nh * inv, nyy * inv_r, nzz * inv, nyz * inv_r]
        rest = [v * (inv_r if j == 1 else inv) for j, v in enumerate(rest)]
        x = e - 1
        h2[x], y2[x], z2[x], yz2[x] = fields
        b_y = jnp.where(y_top_r, t_yr, jnp.where(y_bot_r, t_ymr, 0.0))
        b_z = jnp.where(z_top, t_z, jnp.where(z_bot, t_zm, 0.0))
        share = 0.02 * por_e[e] + b_z
        share = patch(share, near(share) + b_y)
        if kind == 0:
            share = share + txm
        if kind == w - 1:
            share = share + txp
        return fields, rest, share, b_y, b_z

    def times(coef, fields):
        return [
            None if v is None else (near(coef) * v if j % 2 else fold(coef * v))
            for j, v in enumerate(fields)
        ]

    def parts(fields, share, b_y, b_z):
        y_face = [
            None if v is None else b_y * (v if j % 2 else near(v)) for j, v in enumerate(fields)
        ]
        return times(share, fields) + y_face + times(b_z, fields)

    def inner_plane(e, acc):
        fields, _, share, b_y, b_z = second_sweep(e, None)
        new = parts(fields, share, b_y, b_z) + [fold(src[e - 1])]
        return tuple(a + b for a, b in zip(acc, new))

    acc = lax.fori_loop(3, w - 1, inner_plane, (jnp.zeros((16, nz), f32),) * 13, unroll=2)

    @pl.when(has_lo)
    def _():
        for c in up_copies:
            c.wait_recv()

    @pl.when(has_hi)
    def _():
        for c in dn_copies:
            c.wait_recv()

    for i in (0, 1, w + 2, w + 3):
        prepare(i)
    for f in (0, 1, w + 1, w + 2):
        t = face(f)
        if f == 1:
            t = jnp.where(has_lo, t, 0.0)
        if f == w + 1:
            t = jnp.where(has_hi, t, 0.0)
        tx[f] = t
    first_sweep(0, "hi", 1 - px, 0)
    first_sweep(1, "lo", px, 1)
    first_sweep(w, "hi", px, 2)
    first_sweep(w + 1, "lo", 1 - px, 3)

    acc = list(acc)
    cross = {}
    sides = {}
    for kind in (0, 1, w - 2, w - 1):
        fields, rest, share, b_y, b_z = second_sweep(kind + 1, kind)
        new = parts(fields, share, b_y, b_z) + [fold(src[kind])]
        acc = [a + b for a, b in zip(acc, new)]
        if kind in (0, w - 1):
            k = 0 if kind == 0 else 1
            both = fields + rest
            for j in range(7):
                edge[k, EDGE[j] : EDGE[j] + both[j].shape[0], :] = both[j]
            t_out = tx[1] if kind == 0 else tx[w + 1]
            cross[k] = times(t_out, fields), times(t_out, rest)
        else:
            k = 0 if kind == 1 else 1
            x2[k] = rest[0]
        padded = rest + [None] * (4 - len(rest))
        more = parts(padded, share, b_y, b_z)
        if k in sides:
            sides[k] = [
                b if a is None else (a if b is None else a + b) for a, b in zip(sides[k], more)
            ]
        else:
            sides[k] = more

    def halves(v):
        return [jnp.sum(v[8 * j : 8 * j + 8], axis=0, keepdims=True) for j in range(2)]

    def put(index, slot, value, group=0):
        for j, r in enumerate(value):
            ref, col = ((pb, 0), (pa, 0), (pa, nz), (pb, nz))[index % 4]
            at = 16 * group + 8 * (index // 4) + 2 * slot + j
            ref[at : at + 1, col : col + nz] = r

    def add(a, b, sign, swap):
        if b is None:
            return a
        hb = halves(b)
        if swap:
            hb = [hb[1], hb[0]]
        if a is None:
            return [sign * v for v in hb]
        return [u + sign * v for u, v in zip(a, hb)]

    def fill_slot(slot, sums):
        o, yf, zf = sums[0:4], sums[4:8], sums[8:12]
        same0 = add(add(None, o[0], 1.0, False), yf[1], -1.0, True)
        same1 = add(add(None, o[2], 1.0, False), yf[3], -1.0, True)
        oth0 = add(add(None, o[1], 1.0, False), yf[0], -1.0, True)
        oth1 = add(add(None, o[3], 1.0, False), yf[2], -1.0, True)
        for index, v in ((0, same0), (1, same1), (4, oth0), (5, oth1)):
            if v is not None:
                put(index, slot, v)
        for index, v in ((2, zf[0]), (3, zf[2]), (6, zf[1]), (7, zf[3])):
            if v is not None:
                put(index, slot, [-u for u in halves(v)])

    fill_slot(1, acc[0:12])
    fill_slot(0, sides[0])
    fill_slot(2, sides[1])
    put(0, 3, halves(acc[12]))

    sub8 = lax.broadcasted_iota(jnp.int32, (8, nz), 0)
    lane8 = lax.broadcasted_iota(jnp.int32, (8, nz), 1)
    pick = sub8 == (lane8 >> 4)

    def fill_cross(slot, values):
        for index, v in zip((0, 4, 1, 5), values):
            put(index, slot, [-u for u in halves(v)], 1)

    fill_cross(2, cross[0][0])
    fill_cross(1, cross[0][1])
    fill_cross(0, cross[1][0])
    fill_cross(3, cross[1][1])
    out_a = exact_dot(pa[...], ga[...])
    out_b = exact_dot(pb[...], gb[...])
    for group in range(2):
        for yo in range(2):
            at = 16 * group + 8 * yo
            three = (out_a[at : at + 8, 0:nz], out_b[at : at + 8], out_a[at : at + 8, nz:])
            for z, v in enumerate(three):
                r = 6 * group + 3 * yo + z
                gsend[r : r + 1, :] = jnp.sum(jnp.where(pick, v, 0.0), axis=0, keepdims=True)

    def gather(d):
        to = wrap(me + d)
        return pltpu.make_async_remote_copy(
            src_ref=gsend.at[pl.ds(0, ROWS)],
            dst_ref=gbuf.at[pl.ds(pl.multiple_of(me * 16, 16), ROWS)],
            send_sem=g_send.at[d],
            recv_sem=g_recv.at[me],
            device_id={"gx": to},
        )

    def gather_from(d):
        frm = wrap(me + n - d)
        return pltpu.make_async_remote_copy(
            src_ref=gsend.at[pl.ds(0, ROWS)],
            dst_ref=gbuf.at[pl.ds(pl.multiple_of(frm * 16, 16), ROWS)],
            send_sem=g_send.at[d],
            recv_sem=g_recv.at[frm],
            device_id={"gx": frm},
        )

    for d in range(1, n):
        gather(d).start()
    gbuf[pl.ds(pl.multiple_of(me * 16, 16), ROWS), :] = gsend[0:ROWS, :]

    up_edge = pltpu.make_async_remote_copy(
        src_ref=edge.at[1], dst_ref=halo.at[0], send_sem=es_send.at[0], recv_sem=es_recv.at[0],
        device_id={"gx": wrap(me + 1)},
    )
    dn_edge = pltpu.make_async_remote_copy(
        src_ref=edge.at[0], dst_ref=halo.at[1], send_sem=es_send.at[1], recv_sem=es_recv.at[1],
        device_id={"gx": wrap(me + n - 1)},
    )

    @pl.when(has_hi)
    def _():
        up_edge.start()

    @pl.when(has_lo)
    def _():
        dn_edge.start()

    for d in range(1, n):
        gather_from(d).wait_recv()

    lane_n = lax.broadcasted_iota(jnp.int32, (n, nz), 1)
    sub_n = lax.broadcasted_iota(jnp.int32, (n, nz), 0)
    slot = lane_n >> 5

    def rolls(v, s, axis):
        return pltpu.roll(v, s % v.shape[axis], axis)

    def every(v):
        v = v + rolls(v, 32, 1)
        return v + rolls(v, 64, 1)

    mats = []
    rhs = None
    for r in range(6):
        o = gbuf[pl.ds(r, n, stride=16), :]
        b = gbuf[pl.ds(6 + r, n, stride=16), :]
        if r == 1:
            rhs = every(jnp.where(slot == 3, o, 0.0))
        left = rolls(b, -1, 0)
        right = rolls(b, 1, 0)
        moved = rolls(right, 64, 1)
        m = jnp.where(slot == 3, 0.0, o)
        m = m + jnp.where((slot == 1) | (slot == 2), left, 0.0)
        m = m + jnp.where(slot == 0, right, 0.0) + jnp.where(slot == 1, moved, 0.0)
        mats.append(m)
    weight = every(sum(jnp.abs(m) for m in mats))
    inv_weight = 1.0 / weight

    def apply_op(v):
        a = jnp.where(slot == 0, rolls(v, 1, 0), jnp.where(slot == 2, rolls(v, -1, 0), v))
        b = jnp.where((lane_n & 16) == 0, rolls(a, -16, 1), rolls(a, 16, 1))
        total = mats[1] * a + mats[4] * b
        total = total + mats[0] * rolls(a, 1, 1) + mats[2] * rolls(a, -1, 1)
        total = total + mats[3] * rolls(b, 1, 1) + mats[5] * rolls(b, -1, 1)
        return every(total)

    def mean_square(v):
        s = jnp.sum(jnp.sum(v * v, axis=0, keepdims=True), axis=1, keepdims=True)
        return s / (4.0 * (n * 32))

    first = apply_op(rhs) * inv_weight
    second = apply_op(first) * inv_weight
    spectral = jnp.sqrt(mean_square(second) / (mean_square(first) + 1e-6))
    upper = 1.25 * spectral
    lower = 0.1 * upper
    centre = 0.5 * (upper + lower)
    half = 0.5 * (upper - lower)
    ratio = centre / half
    damping = 1.0 / ratio
    residual = rhs
    update = residual * inv_weight / centre
    sol = jnp.zeros_like(rhs)
    for sweep in range(CHEBY):
        sol = sol + update
        if sweep + 1 < CHEBY:
            residual = residual - apply_op(update)
            following = 1.0 / (2.0 * ratio - damping)
            update = following * damping * update + 2.0 * following / half * residual * inv_weight
            damping = following

    def sol_row(x):
        return jnp.sum(jnp.where(sub_n == x, sol, 0.0), axis=0, keepdims=True)

    rows3 = jnp.where(
        sub8 == 0,
        sol_row(me - 1),
        jnp.where(sub8 == 1, sol_row(me), jnp.where(sub8 == 2, sol_row(me + 1), 0.0)),
    )
    spread_out = exact_dot(rows3, ge[...])
    maps = {
        (j, k): spread_out[:, (2 * j + k) * nz : (2 * j + k + 1) * nz]
        for j in range(2)
        for k in range(2)
    }
    for x in range(3):
        for jz in range(2):
            a, b = maps[0, jz][x : x + 1], maps[1, jz][x : x + 1]
            sbuf[x, 2 * jz] = jnp.where(row < BY, a, b)
            sbuf[x, 2 * jz + 1] = jnp.where(row < BY, b, a)

    def base_pressure(h, y, z, yz, node):
        p = h * sbuf[node, 0] + z * sbuf[node, 2]
        q = y * near(sbuf[node, 1]) + yz * near(sbuf[node, 3])
        return patch(p, near(p) + q)

    def plane_pressure(x):
        p = base_pressure(h2[x], y2[x], z2[x], yz2[x], 1)
        p_e[x + 1] = p
        pres[x] = p

    loop(2, w - 2, plane_pressure)

    @pl.when(has_lo)
    def _():
        up_edge.wait_recv()

    @pl.when(has_hi)
    def _():
        dn_edge.wait_recv()

    def edge_pressure(ref, k, home, beside):
        v = [ref[k, EDGE[j] : EDGE[j] + (16 if j in (1, 3, 5) else 32), :] for j in range(7)]
        p = base_pressure(v[0], v[1], v[2], v[3], home)
        p = p + v[4] * sbuf[beside, 0] + v[6] * sbuf[beside, 2]
        return patch(p, near(p) + v[5] * near(sbuf[beside, 1]))

    for x, k, beside in ((0, 0, 0), (w - 1, 1, 2)):
        p = edge_pressure(edge, k, 1, beside)
        p_e[x + 1] = p
        pres[x] = p
    for x, k, beside in ((1, 0, 0), (w - 2, 1, 2)):
        p = base_pressure(h2[x], y2[x], z2[x], yz2[x], 1) + x2[k] * sbuf[beside, 0]
        p_e[x + 1] = p
        pres[x] = p
    p_e[0] = edge_pressure(halo, 0, 0, 1)
    p_e[w + 1] = edge_pressure(halo, 1, 2, 1)

    def flow(t, p, pn, f, fn):
        v = t * (p - pn)
        return v, jnp.where(v > 0, f, fn) * v

    def transport(x, carry):
        vx, wx, top = carry
        e, i = x + 1, x + 2
        p, f = p_e[e], f_e[i]
        vn, wn = flow(tx[e + 1], p, p_e[e + 1], f, f_e[i + 1])
        vy, wy = flow(ty[e], p, yn(p), f, yn(f))
        vz, wz = flow(tz[e], p, zn(p), f, zn(f))
        net = (wn - wx) + (wy - yp(wy)) + (wz - zp(wz))
        s = src[x]
        leaving = jnp.maximum(vn, 0.0) + jnp.maximum(-vx, 0.0)
        leaving = leaving + jnp.maximum(vy, 0.0) + jnp.maximum(-yp(vy), 0.0)
        leaving = leaving + jnp.maximum(vz, 0.0) + jnp.maximum(-zp(vz), 0.0)
        leaving = leaving + jnp.maximum(-s, 0.0)
        gain = jnp.maximum(s, 0.0) + jnp.minimum(s, 0.0) * f - net
        inv = 1.0 / por_e[e]
        new_sat[x] = gain * inv
        return vn, wn, jnp.maximum(top, leaving * inv)

    v0, w0 = flow(tx[1], p_e[0], p_e[1], f_e[1], f_e[2])
    _, _, top = lax.fori_loop(0, w, transport, (v0, w0, zero), unroll=2)
    top = jnp.max(jnp.max(top, axis=0, keepdims=True), axis=1, keepdims=True)
    msend[...] = jnp.broadcast_to(top, (1, nz))

    def spread(d):
        return pltpu.make_async_remote_copy(
            src_ref=msend,
            dst_ref=mbuf.at[me],
            send_sem=m_send.at[d],
            recv_sem=m_recv.at[me],
            device_id={"gx": wrap(me + d)},
        )

    def spread_from(d):
        frm = wrap(me + n - d)
        return pltpu.make_async_remote_copy(
            src_ref=msend,
            dst_ref=mbuf.at[frm],
            send_sem=m_send.at[d],
            recv_sem=m_recv.at[frm],
            device_id={"gx": frm},
        )

    for d in range(1, n):
        spread(d).start()
    mbuf[me] = msend[...]
    for d in range(1, n):
        spread_from(d).wait_recv()
    best = mbuf[0]
    for k in range(1, n):
        best = jnp.maximum(best, mbuf[k])
    step = 0.5 / best

    def finish(x):
        new_sat[x] = sat_e[x + 2] + step * new_sat[x]

    loop(0, w, finish)

    @pl.when(has_hi)
    def _():
        for c in up_copies:
            c.wait_send()
        up_edge.wait_send()

    @pl.when(has_lo)
    def _():
        for c in dn_copies:
            c.wait_send()
        dn_edge.wait_send()

    for d in range(1, n):
        gather(d).wait_send()
        spread(d).wait_send()


def copy_kernel(a, b, out_a, out_b, sem):
    copies = [
        pltpu.make_async_copy(a, out_a, sem.at[0]),
        pltpu.make_async_copy(b, out_b, sem.at[1]),
    ]
    for c in copies:
        c.start()
    for c in copies:
        c.wait()


def write_out(a, b):
    shape = jax.ShapeDtypeStruct(a.shape, a.dtype)
    return pl.pallas_call(
        copy_kernel,
        name="write_out",
        out_shape=(shape, shape),
        in_specs=[pl.BlockSpec(memory_space=pltpu.VMEM)] * 2,
        out_specs=(pl.BlockSpec(memory_space=pltpu.HBM),) * 2,
        scratch_shapes=[pltpu.SemaphoreType.DMA((2,))],
        compiler_params=pltpu.CompilerParams(vmem_limit_bytes=4 * 1024 * 1024),
    )(a, b)


def solution(mesh):
    n = mesh.shape["gx"]

    def on_device(log_perm, saturation, porosity, source, support_bits):
        w, ny, nz = log_perm.shape
        plane = (ny, nz)
        f32 = jnp.float32

        def v(*lead):
            return pltpu.VMEM(lead + plane, f32)

        r = lambda k: pltpu.VMEM((k, 16, nz), f32)
        dma = lambda k: pltpu.SemaphoreType.DMA((k,))
        out = jax.ShapeDtypeStruct(log_perm.shape, f32)
        pinned = [
            pltpu.with_memory_space_constraint(a, pltpu.HBM)
            for a in (log_perm, saturation, porosity, source, support_bits)
        ]
        results = pl.pallas_call(
            lambda *refs: kernel(n, *refs),
            name="multiscale_step",
            out_shape=(out, out),
            in_specs=[pl.BlockSpec(memory_space=pltpu.HBM)] * 5,
            out_specs=(pl.BlockSpec(memory_space=pltpu.VMEM),) * 2,
            scratch_shapes=[
                v(w + 4), v(w + 4), v(w + 2), pltpu.VMEM((w + 2,) + plane, jnp.int32), v(w),
                v(w + 4), v(w + 4), v(w + 4), v(w + 3), v(w + 2), v(w + 2), v(w + 2),
                v(w + 2), r(w + 2), v(w + 2), v(4), v(w), r(w), v(w), r(w), v(2),
                pltpu.VMEM((2, 176, nz), f32), pltpu.VMEM((2, 176, nz), f32),
                pltpu.VMEM((32, 2 * nz), f32), pltpu.VMEM((32, 2 * nz), f32),
                pltpu.VMEM((2 * nz, 2 * nz), jnp.bfloat16), pltpu.VMEM((2 * nz, nz), jnp.bfloat16),
                pltpu.VMEM((nz, 4 * nz), jnp.bfloat16), pltpu.VMEM((16, nz), f32),
                pltpu.VMEM((16 * n, nz), f32), v(3, 4), v(w + 2),
                pltpu.VMEM((1, nz), f32), pltpu.VMEM((n, 1, nz), f32),
                dma(5), dma(8), dma(8), dma(2), dma(2), dma(n), dma(n), dma(n), dma(n),
            ],
            compiler_params=pltpu.CompilerParams(
                collective_id=0, has_side_effects=True, vmem_limit_bytes=33554432
            ),
        )(*pinned)
        return write_out(*results)

    spec = P(("groups", "gx"), None, None)
    return jax.shard_map(
        on_device, mesh=mesh, in_specs=(spec,) * 5, out_specs=(spec, spec), check_vma=False
    )
```

```python
import jax
import jax.numpy as jnp
from jax import lax
from jax.experimental import pallas as pl
from jax.experimental.pallas import tpu as pltpu
from jax.sharding import PartitionSpec as P

BX = 16
BY = 16
BZ = 8
CHEBY = 4
THIRD = 1.0 / 3.0
RELAX = 2.0 / 3.0
ROWS = 12
EDGE = (0, 128, 32, 144, 64, 160, 96)


def kernel(
    n, lp_h, sat_h, por_h, src_h, bits_h, pres, new_sat,
    lp_e, sat_e, por_e, bits_e, src, q_e, m_e, f_e, tx, ty, tz, wd,
    h1, y1, z1, x1, h2, y2, z2, yz2, x2, edge, halo, pa, pb, ga, gb, ge, gsend, gbuf, sbuf, p_e,
    msend, mbuf, lsem, hs_send, hs_recv, es_send, es_recv, g_send, g_recv, m_send, m_recv,
):
    f32 = jnp.float32
    me = lax.axis_index("gx")
    w = lp_h.shape[0]
    ny, nz = lp_h.shape[1], lp_h.shape[2]
    has_lo = me > 0

    def wrap(t):
        return jnp.where(t >= n, t - n, t)

    has_hi = me < n - 1

    barrier = pltpu.get_barrier_semaphore()
    for d in range(1, n):
        pl.semaphore_signal(barrier, inc=1, device_id={"gx": wrap(me + d)})

    own = [
        pltpu.make_async_copy(lp_h, lp_e.at[pl.ds(2, w)], lsem.at[0]),
        pltpu.make_async_copy(sat_h, sat_e.at[pl.ds(2, w)], lsem.at[1]),
        pltpu.make_async_copy(por_h, por_e.at[pl.ds(1, w)], lsem.at[2]),
        pltpu.make_async_copy(bits_h, bits_e.at[pl.ds(1, w)], lsem.at[3]),
        pltpu.make_async_copy(src_h, src, lsem.at[4]),
    ]
    for c in own:
        c.start()

    def halo_copies(up):
        base = 0 if up else 4
        to = wrap(me + (1 if up else n - 1))
        out = []
        for k, (a, b, width) in enumerate(
            ((lp_h, lp_e, 2), (sat_h, sat_e, 2), (por_h, por_e, 1), (bits_h, bits_e, 1))
        ):
            s0 = w - width if up else 0
            d0 = 0 if up else w + width
            out.append(
                pltpu.make_async_remote_copy(
                    src_ref=a.at[pl.ds(s0, width)],
                    dst_ref=b.at[pl.ds(d0, width)],
                    send_sem=hs_send.at[base + k],
                    recv_sem=hs_recv.at[base + k],
                    device_id={"gx": to},
                )
            )
        return out

    up_copies = halo_copies(True)
    dn_copies = halo_copies(False)

    def fill(lo):
        e2 = pl.ds(0 if lo else w + 2, 2)
        e1 = pl.ds(0 if lo else w + 1, 1)
        lp_e[e2] = jnp.zeros((2, ny, nz), f32)
        sat_e[e2] = jnp.full((2, ny, nz), 0.5, f32)
        por_e[e1] = jnp.full((1, ny, nz), 0.2, f32)
        bits_e[e1] = jnp.full((1, ny, nz), 255, jnp.int32)
        halo[0 if lo else 1] = jnp.zeros((176, nz), f32)

    @pl.when(jnp.logical_not(has_lo))
    def _():
        fill(True)

    @pl.when(jnp.logical_not(has_hi))
    def _():
        fill(False)

    row = lax.broadcasted_iota(jnp.int32, (ny, nz), 0)
    lane = lax.broadcasted_iota(jnp.int32, (ny, nz), 1)
    y_top = (row & (BY - 1)) == BY - 1
    y_bot = (row & (BY - 1)) == 0
    z_top = (lane & (BZ - 1)) == BZ - 1
    z_bot = (lane & (BZ - 1)) == 0
    py = (row >> 4) & 1
    pz = (lane >> 3) & 1

    def yz_bit(jy, jz):
        return jnp.left_shift(jnp.int32(1), 2 * (py ^ jy) + 4 * (pz ^ jz))

    zero = jnp.zeros((ny, nz), f32)
    lo_r, hi_r = BY - 8, BY + 8
    row_r = lax.broadcasted_iota(jnp.int32, (16, nz), 0)
    lane_r = lax.broadcasted_iota(jnp.int32, (16, nz), 1)
    y_top_r = row_r == 7
    y_bot_r = row_r == 8
    z_top_r = (lane_r & (BZ - 1)) == BZ - 1
    z_bot_r = (lane_r & (BZ - 1)) == 0
    py_r = row_r >> 3
    pz_r = (lane_r >> 3) & 1

    def yz_bit_r(jy, jz):
        return jnp.left_shift(jnp.int32(1), 2 * (py_r ^ jy) + 4 * (pz_r ^ jz))

    def near(v):
        return v[lo_r:hi_r]

    def patch(v, part):
        return jnp.concatenate([v[:lo_r], part, v[hi_r:]], axis=0)

    def fold(v):
        return jnp.concatenate([v[0:8] + v[8:16], v[16:24] + v[24:32]], axis=0)

    def keep(bits, bit_yz, kx, value):
        return jnp.where((bits & (bit_yz * (1 + kx))) != 0, value, 0.0)

    def yn(v):
        return pltpu.roll(v, v.shape[0] - 1, 0)

    def yp(v):
        return pltpu.roll(v, 1, 0)

    def zn(v):
        return pltpu.roll(v, nz - 1, 1)

    def zp(v):
        return pltpu.roll(v, 1, 1)

    def prepare(i):
        q_e[i] = jnp.exp(-lp_e[i])
        s = sat_e[i]
        r = 1.0 - s
        m = s * s + 0.25 * (r * r)
        m_e[i] = m
        f_e[i] = s * s / m

    def face(f):
        return (m_e[f] + m_e[f + 1]) / (q_e[f] + q_e[f + 1])

    def first_sweep(e, kind, kx, slot):
        q = q_e[e + 1]
        m = m_e[e + 1]
        t_y = jnp.where(row < ny - 1, (m + yn(m)) / (q + yn(q)), 0.0)
        t_z = jnp.where(lane < nz - 1, (m + zn(m)) / (q + zn(q)), 0.0)
        ty[e] = t_y
        tz[e] = t_z
        t_ym = yp(t_y)
        t_zm = zp(t_z)
        txm, txp = tx[e], tx[e + 1]
        bits = bits_e[e]
        b_y = jnp.where(y_top_r, near(t_y), jnp.where(y_bot_r, near(t_ym), 0.0))
        b_z = jnp.where(z_top, t_z, jnp.where(z_bot, t_zm, 0.0))
        all_y, all_z = t_y + t_ym, t_z + t_zm
        inner = patch(all_y, near(all_y) - b_y) + (all_z - b_z)
        diag = 0.02 * por_e[e] + txm + txp + all_y + all_z
        scale = RELAX / diag
        wd[e] = scale
        if kind is None:
            inner = inner + txm + txp
        elif kind == "lo":
            inner = inner + txp
        else:
            inner = inner + txm
        h = keep(bits, yz_bit(0, 0), kx, THIRD + scale * inner)
        by = keep(near(bits), yz_bit_r(1, 0), kx, near(scale) * b_y)
        bz = keep(bits, yz_bit(0, 1), kx, scale * b_z)
        total = h + bz
        total = patch(total, near(total) + by)
        if kind is not None:
            bx = keep(bits, yz_bit(0, 0), 1 - kx, scale * (txm if kind == "lo" else txp))
            total = total + bx
        inv = 1.0 / total
        h1[e] = h * inv
        y1[e] = by * near(inv)
        z1[e] = bz * inv
        if kind is not None:
            x1[slot] = bx * inv

    gi = lax.broadcasted_iota(jnp.int32, (nz, nz), 0)
    gc = lax.broadcasted_iota(jnp.int32, (nz, nz), 1)
    nodes_z = nz // BZ
    gk = gi >> 3
    gu = (gi & 7) >= 4
    ck = gc & (nodes_z - 1)
    same_k = gk == ck
    up_k = gu & (gk + 1 == ck)
    dn_k = jnp.logical_not(gu) & (gk - 1 == ck)
    one = lambda c: jnp.where(c, 1.0, 0.0).astype(jnp.bfloat16)
    ga[0:nz, 0:nz] = one(same_k & jnp.logical_not(gu))
    ga[0:nz, nz:] = one(same_k & gu)
    ga[nz:, 0:nz] = one(up_k)
    ga[nz:, nz:] = one(dn_k)
    gb[0:nz, :] = one(same_k)
    gb[nz:, :] = one(up_k | dn_k)
    ek = gc >> 3
    eb = jnp.where((gc & 7) >= 4, ek + 1, ek - 1)
    eb_ok = (eb >= 0) & (eb < nodes_z)
    for j in range(2):
        ge[:, 2 * j * nz : (2 * j + 1) * nz] = one(gi == j * nodes_z + ek)
        ge[:, (2 * j + 1) * nz : (2 * j + 2) * nz] = one((gi == j * nodes_z + eb) & eb_ok)
    pa[...] = jnp.zeros(pa.shape, f32)
    pb[...] = jnp.zeros(pb.shape, f32)

    def exact_dot(a, b):
        a1 = a.astype(jnp.bfloat16)
        r1 = a - a1.astype(f32)
        a2 = r1.astype(jnp.bfloat16)
        a3 = (r1 - a2.astype(f32)).astype(jnp.bfloat16)
        m = a.shape[0]
        out = jnp.dot(jnp.concatenate([a1, a2, a3], axis=0), b, preferred_element_type=f32)
        return (out[2 * m :] + out[m : 2 * m]) + out[:m]

    px = lax.rem(me, 2)

    for c in own:
        c.wait()

    def loop(lo, hi, fn):
        def body(i, _):
            fn(i)
            return 0

        lax.fori_loop(lo, hi, body, 0, unroll=4 if (hi - lo) % 4 == 0 else 2 - (hi - lo) % 2)

    loop(2, w + 2, prepare)

    def set_face(f):
        tx[f] = face(f)

    loop(2, w + 1, set_face)
    pl.semaphore_wait(barrier, n - 1)

    @pl.when(has_hi)
    def _():
        for c in up_copies:
            c.start()

    @pl.when(has_lo)
    def _():
        for c in dn_copies:
            c.start()

    loop(2, w, lambda e: first_sweep(e, None, px, 0))

    def second_sweep(e, kind):
        t_y, t_z, scale, bits = ty[e], tz[e], wd[e], bits_e[e]
        t_ym, t_zm = yp(t_y), zp(t_z)
        txm, txp = tx[e], tx[e + 1]

        t_yr, t_ymr, t_zr, t_zmr = near(t_y), near(t_ym), near(t_z), near(t_zm)
        txmr, txpr, scale_r, bits_r = near(txm), near(txp), near(scale), near(bits)

        def shift_z(v, t, tm, top, bot):
            c, d = t * zn(v), tm * zp(v)
            zb = jnp.where(top, c, jnp.where(bot, d, 0.0))
            return jnp.where(top, d, jnp.where(bot, c, c + d)), zb

        def shift_y(a, b):
            yb = jnp.where(y_top_r, a, jnp.where(y_bot_r, b, 0.0))
            return jnp.where(y_top_r, b, jnp.where(y_bot_r, a, a + b)), yb

        def shifts(v):
            a, b = t_y * yn(v), t_ym * yp(v)
            yi, yb = shift_y(near(a), near(b))
            return (patch(a + b, yi), yb) + shift_z(v, t_z, t_zm, z_top, z_bot)

        def shifts_r(v):
            yi, yb = shift_y(t_yr * yn(v), t_ymr * yp(v))
            return (yi, yb) + shift_z(v, t_zr, t_zmr, z_top_r, z_bot_r)

        h, y, z = h1[e], y1[e], z1[e]
        h_yi, h_yb, h_zi, h_zb = shifts(h)
        y_yi, y_yb, y_zi, y_zb = shifts_r(y)
        z_yi, z_yb, z_zi, z_zb = shifts(z)

        pull_h = h_yi + h_zi + z_zb
        pull_h = patch(pull_h, near(pull_h) + y_yb)
        pull_y = y_yi + y_zi + h_yb
        pull_z = z_yi + z_zi + h_zb
        if kind != 0:
            pull_h = pull_h + txm * h1[e - 1]
            pull_y = pull_y + txmr * y1[e - 1]
            pull_z = pull_z + txm * z1[e - 1]
        else:
            pull_h = pull_h + txm * x1[0]
        if kind != w - 1:
            pull_h = pull_h + txp * h1[e + 1]
            pull_y = pull_y + txpr * y1[e + 1]
            pull_z = pull_z + txp * z1[e + 1]
        else:
            pull_h = pull_h + txp * x1[3]
        nh = keep(bits, yz_bit(0, 0), px, THIRD * h + scale * pull_h)
        nyy = keep(bits_r, yz_bit_r(1, 0), px, THIRD * y + scale_r * pull_y)
        nzz = keep(bits, yz_bit(0, 1), px, THIRD * z + scale * pull_z)
        nyz = keep(bits_r, yz_bit_r(1, 1), px, scale_r * (y_zb + z_yb))
        total = nh + nzz
        part = nyy + nyz
        rest = []
        if kind is not None:
            qx = 1 - px
            if kind in (0, w - 1):
                xo = x1[1] if kind == 0 else x1[2]
                t_out = txm if kind == 0 else txp
                other = e - 1 if kind == 0 else e + 1
                x_yi, x_yb, x_zi, x_zb = shifts(xo)
                nx = THIRD * xo + scale * (x_yi + x_zi + t_out * h1[other])
                nxy = scale_r * (x_yb + near(t_out) * y1[other])
                rest = [
                    keep(bits, yz_bit(0, 0), qx, nx),
                    keep(bits_r, yz_bit_r(1, 0), qx, nxy),
                    keep(bits, yz_bit(0, 1), qx, scale * (x_zb + t_out * z1[other])),
                ]
                total = total + rest[0] + rest[2]
                part = part + rest[1]
            else:
                nx = scale * (txm * x1[1] if kind == 1 else txp * x1[2])
                rest = [keep(bits, yz_bit(0, 0), qx, nx)]
                total = total + rest[0]
        inv = 1.0 / patch(total, near(total) + part)
        inv_r = near(inv)
        fields = [nh * inv, nyy * inv_r, nzz * inv, nyz * inv_r]
        rest = [v * (inv_r if j == 1 else inv) for j, v in enumerate(rest)]
        x = e - 1
        h2[x], y2[x], z2[x], yz2[x] = fields
        b_y = jnp.where(y_top_r, t_yr, jnp.where(y_bot_r, t_ymr, 0.0))
        b_z = jnp.where(z_top, t_z, jnp.where(z_bot, t_zm, 0.0))
        share = 0.02 * por_e[e] + b_z
        share = patch(share, near(share) + b_y)
        if kind == 0:
            share = share + txm
        if kind == w - 1:
            share = share + txp
        return fields, rest, share, b_y, b_z

    def times(coef, fields):
        return [
            None if v is None else (near(coef) * v if j % 2 else fold(coef * v))
            for j, v in enumerate(fields)
        ]

    def parts(fields, share, b_y, b_z):
        y_face = [
            None if v is None else b_y * (v if j % 2 else near(v)) for j, v in enumerate(fields)
        ]
        return times(share, fields) + y_face + times(b_z, fields)

    def inner_plane(e, acc):
        fields, _, share, b_y, b_z = second_sweep(e, None)
        new = parts(fields, share, b_y, b_z) + [fold(src[e - 1])]
        return tuple(a + b for a, b in zip(acc, new))

    acc = lax.fori_loop(3, w - 1, inner_plane, (jnp.zeros((16, nz), f32),) * 13, unroll=2)

    @pl.when(has_lo)
    def _():
        for c in up_copies:
            c.wait_recv()

    @pl.when(has_hi)
    def _():
        for c in dn_copies:
            c.wait_recv()

    for i in (0, 1, w + 2, w + 3):
        prepare(i)
    for f in (0, 1, w + 1, w + 2):
        t = face(f)
        if f == 1:
            t = jnp.where(has_lo, t, 0.0)
        if f == w + 1:
            t = jnp.where(has_hi, t, 0.0)
        tx[f] = t
    first_sweep(0, "hi", 1 - px, 0)
    first_sweep(1, "lo", px, 1)
    first_sweep(w, "hi", px, 2)
    first_sweep(w + 1, "lo", 1 - px, 3)

    acc = list(acc)
    cross = {}
    sides = {}
    for kind in (0, 1, w - 2, w - 1):
        fields, rest, share, b_y, b_z = second_sweep(kind + 1, kind)
        new = parts(fields, share, b_y, b_z) + [fold(src[kind])]
        acc = [a + b for a, b in zip(acc, new)]
        if kind in (0, w - 1):
            k = 0 if kind == 0 else 1
            both = fields + rest
            for j in range(7):
                edge[k, EDGE[j] : EDGE[j] + both[j].shape[0], :] = both[j]
            t_out = tx[1] if kind == 0 else tx[w + 1]
            cross[k] = times(t_out, fields), times(t_out, rest)
        else:
            k = 0 if kind == 1 else 1
            x2[k] = rest[0]
        padded = rest + [None] * (4 - len(rest))
        more = parts(padded, share, b_y, b_z)
        if k in sides:
            sides[k] = [
                b if a is None else (a if b is None else a + b) for a, b in zip(sides[k], more)
            ]
        else:
            sides[k] = more

    def halves(v):
        return [jnp.sum(v[8 * j : 8 * j + 8], axis=0, keepdims=True) for j in range(2)]

    def put(index, slot, value, group=0):
        for j, r in enumerate(value):
            ref, col = ((pb, 0), (pa, 0), (pa, nz), (pb, nz))[index % 4]
            at = 16 * group + 8 * (index // 4) + 2 * slot + j
            ref[at : at + 1, col : col + nz] = r

    def add(a, b, sign, swap):
        if b is None:
            return a
        hb = halves(b)
        if swap:
            hb = [hb[1], hb[0]]
        if a is None:
            return [sign * v for v in hb]
        return [u + sign * v for u, v in zip(a, hb)]

    def fill_slot(slot, sums):
        o, yf, zf = sums[0:4], sums[4:8], sums[8:12]
        same0 = add(add(None, o[0], 1.0, False), yf[1], -1.0, True)
        same1 = add(add(None, o[2], 1.0, False), yf[3], -1.0, True)
        oth0 = add(add(None, o[1], 1.0, False), yf[0], -1.0, True)
        oth1 = add(add(None, o[3], 1.0, False), yf[2], -1.0, True)
        for index, v in ((0, same0), (1, same1), (4, oth0), (5, oth1)):
            if v is not None:
                put(index, slot, v)
        for index, v in ((2, zf[0]), (3, zf[2]), (6, zf[1]), (7, zf[3])):
            if v is not None:
                put(index, slot, [-u for u in halves(v)])

    fill_slot(1, acc[0:12])
    fill_slot(0, sides[0])
    fill_slot(2, sides[1])
    put(0, 3, halves(acc[12]))

    sub8 = lax.broadcasted_iota(jnp.int32, (8, nz), 0)
    lane8 = lax.broadcasted_iota(jnp.int32, (8, nz), 1)
    pick = sub8 == (lane8 >> 4)

    def fill_cross(slot, values):
        for index, v in zip((0, 4, 1, 5), values):
            put(index, slot, [-u for u in halves(v)], 1)

    fill_cross(2, cross[0][0])
    fill_cross(1, cross[0][1])
    fill_cross(0, cross[1][0])
    fill_cross(3, cross[1][1])
    out_a = exact_dot(pa[...], ga[...])
    out_b = exact_dot(pb[...], gb[...])
    for group in range(2):
        for yo in range(2):
            at = 16 * group + 8 * yo
            three = (out_a[at : at + 8, 0:nz], out_b[at : at + 8], out_a[at : at + 8, nz:])
            for z, v in enumerate(three):
                r = 6 * group + 3 * yo + z
                gsend[r : r + 1, :] = jnp.sum(jnp.where(pick, v, 0.0), axis=0, keepdims=True)

    def gather(d):
        to = wrap(me + d)
        return pltpu.make_async_remote_copy(
            src_ref=gsend.at[pl.ds(0, ROWS)],
            dst_ref=gbuf.at[pl.ds(pl.multiple_of(me * 16, 16), ROWS)],
            send_sem=g_send.at[d],
            recv_sem=g_recv.at[me],
            device_id={"gx": to},
        )

    def gather_from(d):
        frm = wrap(me + n - d)
        return pltpu.make_async_remote_copy(
            src_ref=gsend.at[pl.ds(0, ROWS)],
            dst_ref=gbuf.at[pl.ds(pl.multiple_of(frm * 16, 16), ROWS)],
            send_sem=g_send.at[d],
            recv_sem=g_recv.at[frm],
            device_id={"gx": frm},
        )

    for d in range(1, n):
        gather(d).start()
    gbuf[pl.ds(pl.multiple_of(me * 16, 16), ROWS), :] = gsend[0:ROWS, :]

    up_edge = pltpu.make_async_remote_copy(
        src_ref=edge.at[1], dst_ref=halo.at[0], send_sem=es_send.at[0], recv_sem=es_recv.at[0],
        device_id={"gx": wrap(me + 1)},
    )
    dn_edge = pltpu.make_async_remote_copy(
        src_ref=edge.at[0], dst_ref=halo.at[1], send_sem=es_send.at[1], recv_sem=es_recv.at[1],
        device_id={"gx": wrap(me + n - 1)},
    )

    @pl.when(has_hi)
    def _():
        up_edge.start()

    @pl.when(has_lo)
    def _():
        dn_edge.start()

    for d in range(1, n):
        gather_from(d).wait_recv()

    lane_n = lax.broadcasted_iota(jnp.int32, (n, nz), 1)
    sub_n = lax.broadcasted_iota(jnp.int32, (n, nz), 0)
    slot = lane_n >> 5

    def rolls(v, s, axis):
        return pltpu.roll(v, s % v.shape[axis], axis)

    def every(v):
        v = v + rolls(v, 32, 1)
        return v + rolls(v, 64, 1)

    mats = []
    rhs = None
    for r in range(6):
        o = gbuf[pl.ds(r, n, stride=16), :]
        b = gbuf[pl.ds(6 + r, n, stride=16), :]
        if r == 1:
            rhs = every(jnp.where(slot == 3, o, 0.0))
        left = rolls(b, -1, 0)
        right = rolls(b, 1, 0)
        moved = rolls(right, 64, 1)
        m = jnp.where(slot == 3, 0.0, o)
        m = m + jnp.where((slot == 1) | (slot == 2), left, 0.0)
        m = m + jnp.where(slot == 0, right, 0.0) + jnp.where(slot == 1, moved, 0.0)
        mats.append(m)
    weight = every(sum(jnp.abs(m) for m in mats))
    inv_weight = 1.0 / weight

    def apply_op(v):
        a = jnp.where(slot == 0, rolls(v, 1, 0), jnp.where(slot == 2, rolls(v, -1, 0), v))
        b = jnp.where((lane_n & 16) == 0, rolls(a, -16, 1), rolls(a, 16, 1))
        total = mats[1] * a + mats[4] * b
        total = total + mats[0] * rolls(a, 1, 1) + mats[2] * rolls(a, -1, 1)
        total = total + mats[3] * rolls(b, 1, 1) + mats[5] * rolls(b, -1, 1)
        return every(total)

    def mean_square(v):
        s = jnp.sum(jnp.sum(v * v, axis=0, keepdims=True), axis=1, keepdims=True)
        return s / (4.0 * (n * 32))

    first = apply_op(rhs) * inv_weight
    second = apply_op(first) * inv_weight
    spectral = jnp.sqrt(mean_square(second) / (mean_square(first) + 1e-6))
    upper = 1.25 * spectral
    lower = 0.1 * upper
    centre = 0.5 * (upper + lower)
    half = 0.5 * (upper - lower)
    ratio = centre / half
    damping = 1.0 / ratio
    residual = rhs
    update = residual * inv_weight / centre
    sol = jnp.zeros_like(rhs)
    for sweep in range(CHEBY):
        sol = sol + update
        if sweep + 1 < CHEBY:
            residual = residual - apply_op(update)
            following = 1.0 / (2.0 * ratio - damping)
            update = following * damping * update + 2.0 * following / half * residual * inv_weight
            damping = following

    def sol_row(x):
        return jnp.sum(jnp.where(sub_n == x, sol, 0.0), axis=0, keepdims=True)

    rows3 = jnp.where(
        sub8 == 0,
        sol_row(me - 1),
        jnp.where(sub8 == 1, sol_row(me), jnp.where(sub8 == 2, sol_row(me + 1), 0.0)),
    )
    spread_out = exact_dot(rows3, ge[...])
    maps = {
        (j, k): spread_out[:, (2 * j + k) * nz : (2 * j + k + 1) * nz]
        for j in range(2)
        for k in range(2)
    }
    for x in range(3):
        for jz in range(2):
            a, b = maps[0, jz][x : x + 1], maps[1, jz][x : x + 1]
            sbuf[x, 2 * jz] = jnp.where(row < BY, a, b)
            sbuf[x, 2 * jz + 1] = jnp.where(row < BY, b, a)

    def base_pressure(h, y, z, yz, node):
        p = h * sbuf[node, 0] + z * sbuf[node, 2]
        q = y * near(sbuf[node, 1]) + yz * near(sbuf[node, 3])
        return patch(p, near(p) + q)

    def plane_pressure(x):
        p = base_pressure(h2[x], y2[x], z2[x], yz2[x], 1)
        p_e[x + 1] = p
        pres[x] = p

    loop(2, w - 2, plane_pressure)

    @pl.when(has_lo)
    def _():
        up_edge.wait_recv()

    @pl.when(has_hi)
    def _():
        dn_edge.wait_recv()

    def edge_pressure(ref, k, home, beside):
        v = [ref[k, EDGE[j] : EDGE[j] + (16 if j in (1, 3, 5) else 32), :] for j in range(7)]
        p = base_pressure(v[0], v[1], v[2], v[3], home)
        p = p + v[4] * sbuf[beside, 0] + v[6] * sbuf[beside, 2]
        return patch(p, near(p) + v[5] * near(sbuf[beside, 1]))

    for x, k, beside in ((0, 0, 0), (w - 1, 1, 2)):
        p = edge_pressure(edge, k, 1, beside)
        p_e[x + 1] = p
        pres[x] = p
    for x, k, beside in ((1, 0, 0), (w - 2, 1, 2)):
        p = base_pressure(h2[x], y2[x], z2[x], yz2[x], 1) + x2[k] * sbuf[beside, 0]
        p_e[x + 1] = p
        pres[x] = p
    p_e[0] = edge_pressure(halo, 0, 0, 1)
    p_e[w + 1] = edge_pressure(halo, 1, 2, 1)

    def flow(t, p, pn, f, fn):
        v = t * (p - pn)
        return v, jnp.where(v > 0, f, fn) * v

    def transport(x, carry):
        vx, wx, top = carry
        e, i = x + 1, x + 2
        p, f = p_e[e], f_e[i]
        vn, wn = flow(tx[e + 1], p, p_e[e + 1], f, f_e[i + 1])
        vy, wy = flow(ty[e], p, yn(p), f, yn(f))
        vz, wz = flow(tz[e], p, zn(p), f, zn(f))
        net = (wn - wx) + (wy - yp(wy)) + (wz - zp(wz))
        s = src[x]
        leaving = jnp.maximum(vn, 0.0) + jnp.maximum(-vx, 0.0)
        leaving = leaving + jnp.maximum(vy, 0.0) + jnp.maximum(-yp(vy), 0.0)
        leaving = leaving + jnp.maximum(vz, 0.0) + jnp.maximum(-zp(vz), 0.0)
        leaving = leaving + jnp.maximum(-s, 0.0)
        gain = jnp.maximum(s, 0.0) + jnp.minimum(s, 0.0) * f - net
        inv = 1.0 / por_e[e]
        new_sat[x] = gain * inv
        return vn, wn, jnp.maximum(top, leaving * inv)

    v0, w0 = flow(tx[1], p_e[0], p_e[1], f_e[1], f_e[2])
    _, _, top = lax.fori_loop(0, w, transport, (v0, w0, zero), unroll=4)
    top = jnp.max(jnp.max(top, axis=0, keepdims=True), axis=1, keepdims=True)
    msend[...] = jnp.broadcast_to(top, (1, nz))

    def spread(d):
        return pltpu.make_async_remote_copy(
            src_ref=msend,
            dst_ref=mbuf.at[me],
            send_sem=m_send.at[d],
            recv_sem=m_recv.at[me],
            device_id={"gx": wrap(me + d)},
        )

    def spread_from(d):
        frm = wrap(me + n - d)
        return pltpu.make_async_remote_copy(
            src_ref=msend,
            dst_ref=mbuf.at[frm],
            send_sem=m_send.at[d],
            recv_sem=m_recv.at[frm],
            device_id={"gx": frm},
        )

    for d in range(1, n):
        spread(d).start()
    mbuf[me] = msend[...]
    for d in range(1, n):
        spread_from(d).wait_recv()
    best = mbuf[0]
    for k in range(1, n):
        best = jnp.maximum(best, mbuf[k])
    step = 0.5 / best

    def finish(x):
        new_sat[x] = sat_e[x + 2] + step * new_sat[x]

    loop(0, w, finish)

    @pl.when(has_hi)
    def _():
        for c in up_copies:
            c.wait_send()
        up_edge.wait_send()

    @pl.when(has_lo)
    def _():
        for c in dn_copies:
            c.wait_send()
        dn_edge.wait_send()

    for d in range(1, n):
        gather(d).wait_send()
        spread(d).wait_send()


def copy_kernel(a, b, out_a, out_b, sem):
    copies = [
        pltpu.make_async_copy(a, out_a, sem.at[0]),
        pltpu.make_async_copy(b, out_b, sem.at[1]),
    ]
    for c in copies:
        c.start()
    for c in copies:
        c.wait()


def write_out(a, b):
    shape = jax.ShapeDtypeStruct(a.shape, a.dtype)
    return pl.pallas_call(
        copy_kernel,
        name="write_out",
        out_shape=(shape, shape),
        in_specs=[pl.BlockSpec(memory_space=pltpu.VMEM)] * 2,
        out_specs=(pl.BlockSpec(memory_space=pltpu.HBM),) * 2,
        scratch_shapes=[pltpu.SemaphoreType.DMA((2,))],
        compiler_params=pltpu.CompilerParams(vmem_limit_bytes=4 * 1024 * 1024),
    )(a, b)


def solution(mesh):
    n = mesh.shape["gx"]

    def on_device(log_perm, saturation, porosity, source, support_bits):
        w, ny, nz = log_perm.shape
        plane = (ny, nz)
        f32 = jnp.float32

        def v(*lead):
            return pltpu.VMEM(lead + plane, f32)

        r = lambda k: pltpu.VMEM((k, 16, nz), f32)
        dma = lambda k: pltpu.SemaphoreType.DMA((k,))
        out = jax.ShapeDtypeStruct(log_perm.shape, f32)
        pinned = [
            pltpu.with_memory_space_constraint(a, pltpu.HBM)
            for a in (log_perm, saturation, porosity, source, support_bits)
        ]
        results = pl.pallas_call(
            lambda *refs: kernel(n, *refs),
            name="multiscale_step",
            out_shape=(out, out),
            in_specs=[pl.BlockSpec(memory_space=pltpu.HBM)] * 5,
            out_specs=(pl.BlockSpec(memory_space=pltpu.VMEM),) * 2,
            scratch_shapes=[
                v(w + 4), v(w + 4), v(w + 2), pltpu.VMEM((w + 2,) + plane, jnp.int32), v(w),
                v(w + 4), v(w + 4), v(w + 4), v(w + 3), v(w + 2), v(w + 2), v(w + 2),
                v(w + 2), r(w + 2), v(w + 2), v(4), v(w), r(w), v(w), r(w), v(2),
                pltpu.VMEM((2, 176, nz), f32), pltpu.VMEM((2, 176, nz), f32),
                pltpu.VMEM((32, 2 * nz), f32), pltpu.VMEM((32, 2 * nz), f32),
                pltpu.VMEM((2 * nz, 2 * nz), jnp.bfloat16), pltpu.VMEM((2 * nz, nz), jnp.bfloat16),
                pltpu.VMEM((nz, 4 * nz), jnp.bfloat16), pltpu.VMEM((16, nz), f32),
                pltpu.VMEM((16 * n, nz), f32), v(3, 4), v(w + 2),
                pltpu.VMEM((1, nz), f32), pltpu.VMEM((n, 1, nz), f32),
                dma(5), dma(8), dma(8), dma(2), dma(2), dma(n), dma(n), dma(n), dma(n),
            ],
            compiler_params=pltpu.CompilerParams(
                collective_id=0, has_side_effects=True, vmem_limit_bytes=33554432
            ),
        )(*pinned)
        return write_out(*results)

    spec = P(("groups", "gx"), None, None)
    return jax.shard_map(
        on_device, mesh=mesh, in_specs=(spec,) * 5, out_specs=(spec, spec), check_vma=False
    )
```
